32 devices in a mesh: dp: 8 (over z, y), mp: 4 (over x, core).
Axes of the slice: x: 2, y: 2, z: 4, core: 2. Of those that a mesh axis runs over, the one named last changes fastest.
Arguments:
- block_in: bfloat16 [4096, 768], P(('dp', 'mp')), may hold values from -6 to 6
- coords: float32 [3, 4096], P(None, 'dp'), may hold values from -10 to 10
- lengths: int32 [8, 16], P('dp'), may hold values from 1 to 256, 512 in all within a row
- cotangent: bfloat16 [4096, 768], P(('dp', 'mp')), may hold values from -6 to 6
- step_count: int32 [1], replicated, may hold values from 1 to 20
- qkv_weight: float32 [3, 768, 768], P(None, 'mp'), may hold values from -0.21875 to 0.21875
- proj_weight: float32 [768, 768], P('mp'), may hold values from -0.625 to 0.625
- pair_weight: float32 [32, 128], P('mp'), may hold values from -3.6 to 3.6
- in_weight: float32 [3072, 768], P('mp'), may hold values from -0.21875 to 0.21875
- in_bias: float32 [3072], P('mp'), may hold values from -1.8 to 1.8
- out_weight: float32 [3072, 768], P('mp'), may hold values from -0.109375 to 0.109375
- norm_params: float32 [5, 768], replicated, may hold values from -0.4 to 1.3, as said below
- qkv_first: float32 [3, 768, 768], P(None, 'mp'), may hold values from -0.00033 to 0.00033
- proj_first: float32 [768, 768], P('mp'), may hold values from -0.000165 to 0.000165
- pair_first: float32 [32, 128], P('mp'), may hold values from -0.00016 to 0.00016
- in_first: float32 [3072, 768], P('mp'), may hold values from -0.00013 to 0.00013
- bias_first: float32 [3072], P('mp'), may hold values from -0.00013 to 0.00013
- out_first: float32 [3072, 768], P('mp'), may hold values from -0.00028 to 0.00028
- norm_first: float32 [5, 768], replicated, may hold values from -0.00046 to 0.00046
- qkv_second: float32 [3, 768, 768], P(None, 'mp'), may hold values from 1.25e-10 to 2e-09
- proj_second: float32 [768, 768], P('mp'), may hold values from 3.1e-11 to 5e-10
- pair_second: float32 [32, 128], P('mp'), may hold values from 2.9e-11 to 4.7e-10
- in_second: float32 [3072, 768], P('mp'), may hold values from 2e-11 to 3.2e-10
- bias_second: float32 [3072], P('mp'), may hold values from 2e-11 to 3.2e-10
- out_second: float32 [3072, 768], P('mp'), may hold values from 8.8e-11 to 1.4e-09
- norm_second: float32 [5, 768], replicated, may hold values from 2.45e-10 to 3.9e-09
Outputs:
- block_out: float32 [4096, 768], P(('dp', 'mp'))
- grad_input: float32 [4096, 768], P(('dp', 'mp'))
- grad_norm: float32 [1], replicated
- qkv_new: float32 [3, 768, 768], P(None, 'mp')
- qkv_first_new: float32 [3, 768, 768], P(None, 'mp')
- qkv_second_new: float32 [3, 768, 768], P(None, 'mp')
- proj_new: float32 [768, 768], P('mp')
- proj_first_new: float32 [768, 768], P('mp')
- proj_second_new: float32 [768, 768], P('mp')
- pair_new: float32 [32, 128], P('mp')
- pair_first_new: float32 [32, 128], P('mp')
- pair_second_new: float32 [32, 128], P('mp')
- in_new: float32 [3072, 768], P('mp')
- in_first_new: float32 [3072, 768], P('mp')
- in_second_new: float32 [3072, 768], P('mp')
- bias_new: float32 [3072], P('mp')
- bias_first_new: float32 [3072], P('mp')
- bias_second_new: float32 [3072], P('mp')
- out_new: float32 [3072, 768], P('mp')
- out_first_new: float32 [3072, 768], P('mp')
- out_second_new: float32 [3072, 768], P('mp')
- norm_new: float32 [5, 768], replicated
- norm_first_new: float32 [5, 768], replicated
- norm_second_new: float32 [5, 768], replicated
The draws below stay inside these ranges and needn't reach their ends.
Inputs may be any that keep to these rules, and one draw needn't show every extreme that they name: `lengths`: each row lists, in order, the atom counts of 16 whole molecules that fill one block of 512 consecutive atoms; each row sums to 512 and its largest entry is 256. `norm_params`: rows 0 and 2 are gains, rows 1, 3 and 4 are shifts and the output bias.
All inputs are finite; a program needn't handle non-finite values.
Results may differ from the reference program's by a relative error of at most 0.012.
The reference program's roundings to bfloat16 on the way count: a program that leaves them out, or rounds other values in their place, can miss the bound.
Values may be sent and summed in bfloat16 or wider, within the bound.
A program may use at most 128 MiB of HBM per device.

```python
import math
import jax
import jax.numpy as jnp
import numpy as np
from jax import lax

D = 768
HEADS = 32
HD = 24
FF = 3072
KERN = 128
MOLBLK = 512
MOLS = 16
MOST = 256
TOKENS = 4096
NBLOCKS = 8


def draw_norm_params(key, part):
    gain_key = jax.random.fold_in(key, 11)
    shift_key = jax.random.fold_in(key, 23)
    gains = jax.random.uniform(gain_key, (5, D), jnp.float32, 0.7, 1.3)
    shifts = jnp.clip(0.1 * jax.random.normal(shift_key, (5, D), jnp.float32), -0.4, 0.4)
    places = lax.broadcasted_iota(jnp.int32, (5, D), 0)
    is_gain = (places == 0) | (places == 2)
    return jnp.where(is_gain, gains, shifts)


def shared_rows(key, first_tag, second_tag):
    pattern_key = jax.random.fold_in(key, first_tag)
    noise_key = jax.random.fold_in(key, second_tag)
    pattern = jax.random.normal(pattern_key, (MOLBLK, D), jnp.float32)
    noise = jax.random.normal(noise_key, (TOKENS, D), jnp.float32)
    repeated = jnp.tile(pattern, (TOKENS // MOLBLK, 1))
    return jnp.clip(0.5 * repeated + 0.8660254 * noise, -6.0, 6.0)


def draw_block_in(key, part):
    return shared_rows(key, 31, 37).astype(jnp.bfloat16)


def draw_cotangent(key, part):
    return shared_rows(key, 41, 43).astype(jnp.bfloat16)


def steps_of(rng, extent, shards, low, largest):
    level = 1.0
    for axis_at, parts in shards:
        heights = jax.random.uniform(jax.random.fold_in(jax.random.fold_in(rng, 6), axis_at), (parts,), jnp.float32, low / len(shards), largest / len(shards))
        level = level * jnp.repeat(jnp.exp(heights), extent[axis_at] // parts).reshape((-1,) + (1,) * (len(extent) - 1 - axis_at))
    return level


def split_up(amount, total, reach, slope):
    portions = [(1 << 20) // math.isqrt(grade ** slope) + 1 for grade in range(2, amount + 1)]
    spare, given = total - reach - (amount - 1), [1] * (amount - 1)
    while spare > 0:
        candidates = [i for i in range(amount - 1) if given[i] < reach]
        mass, budget = sum([portions[i] for i in candidates]), spare
        for i in candidates:
            more = min(reach - given[i], max(1, budget * portions[i] // mass), spare)
            given[i] = given[i] + more
            spare = spare - more
    return np.array([reach] + given)


def ragged(rng, count, total, limit, lean):
    if count == 2:
        one = jax.random.randint(rng, (), max(1, total - limit), min(limit, total - 1) + 1)
        return jnp.stack([one, total - one])
    sizes = jnp.asarray(split_up(count, total, limit, lean), jnp.int32)
    couples = (count - 1) // 2
    donor, receiver = sizes[1:1 + 2 * couples:2], sizes[2:2 + 2 * couples:2]
    room = jnp.minimum(donor - 1, limit - receiver)
    shifted = jax.random.randint(jax.random.fold_in(rng, 1), (couples,), 0, 1 << 20) % (room + 1)
    sizes = sizes.at[1:1 + 2 * couples:2].set(donor - shifted).at[2:2 + 2 * couples:2].set(receiver + shifted)
    return sizes[jax.random.permutation(jax.random.fold_in(rng, 2), count)]


def scatter_about(own_key, dims, deviation, limit, cuts=(), held_as=jnp.bfloat16):
    array = deviation * jax.random.normal(own_key, dims, jnp.float32)
    if cuts:
        array = array * steps_of(own_key, dims, cuts, -0.22, 0.18)
    return jnp.clip(array, -limit, limit).astype(held_as)


def setup_inputs(seed: int = 0) -> dict:
    key_list = jax.random.split(jax.random.key(seed), 27)
    block_in = draw_block_in(jax.random.fold_in(key_list[26], 71), 0)
    coords = scatter_about(key_list[1], (3, TOKENS), 2.0, 10.0, ((1, 8),), jnp.float32)
    lengths = jax.vmap(lambda own: ragged(own, MOLS, MOLBLK, MOST, 2))(jax.random.split(key_list[2], NBLOCKS)).reshape((NBLOCKS, MOLS)).astype(jnp.int32)
    cotangent = draw_cotangent(jax.random.fold_in(key_list[26], 71), 0)
    step_count = jax.random.randint(key_list[4], (1,), 1, 21).astype(jnp.int32)
    qkv_weight = scatter_about(key_list[5], (3, HEADS * HD, D), D ** -0.5, 0.21875, ((1, 4),), jnp.float32)
    proj_weight = scatter_about(key_list[6], (HEADS * HD, D), (HEADS * HD // 8) ** -0.5, 0.625, ((0, 4),), jnp.float32)
    pair_weight = scatter_about(key_list[7], (HEADS, KERN), 0.6, 3.6, ((0, 4),), jnp.float32)
    in_weight = scatter_about(key_list[8], (FF, D), D ** -0.5, 0.21875, ((0, 4),), jnp.float32)
    in_bias = scatter_about(key_list[9], (FF,), 0.3, 1.8, ((0, 4),), jnp.float32)
    out_weight = scatter_about(key_list[10], (FF, D), FF ** -0.5, 0.109375, ((0, 4),), jnp.float32)
    norm_params = draw_norm_params(jax.random.fold_in(key_list[26], 71), 0)
    qkv_first = scatter_about(key_list[12], (3, HEADS * HD, D), 0.000055, 0.00033, ((1, 4),), jnp.float32)
    proj_first = scatter_about(key_list[13], (HEADS * HD, D), 0.0000275, 0.000165, ((0, 4),), jnp.float32)
    pair_first = scatter_about(key_list[14], (HEADS, KERN), 0.000027, 0.00016, ((0, 4),), jnp.float32)
    in_first = scatter_about(key_list[15], (FF, D), 0.000022, 0.00013, ((0, 4),), jnp.float32)
    bias_first = scatter_about(key_list[16], (FF,), 0.000022, 0.00013, ((0, 4),), jnp.float32)
    out_first = scatter_about(key_list[17], (FF, D), 0.000046, 0.00028, ((0, 4),), jnp.float32)
    norm_first = scatter_about(key_list[18], (5, D), 0.000077, 0.00046, (), jnp.float32)
    qkv_second = jnp.clip(jnp.exp(math.log(1.999999943436137e-09) - 2.7725887 * jax.random.uniform(key_list[19], (3, HEADS * HD, D), jnp.float32) ** steps_of(key_list[19], (3, HEADS * HD, D), ((1, 4),), -0.2, 0.2)), 1.2499999646475857e-10, 1.999999943436137e-09)
    proj_second = jnp.clip(jnp.exp(math.log(4.999999858590343e-10) - 2.7806208 * jax.random.uniform(key_list[20], (HEADS * HD, D), jnp.float32) ** steps_of(key_list[20], (HEADS * HD, D), ((0, 4),), -0.2, 0.2)), 3.100000117717272e-11, 4.999999858590343e-10)
    pair_second = jnp.clip(jnp.exp(math.log(4.699999833768231e-10) - 2.7854368 * jax.random.uniform(key_list[21], (HEADS, KERN), jnp.float32) ** steps_of(key_list[21], (HEADS, KERN), ((0, 4),), -0.2, 0.2)), 2.9000000317802588e-11, 4.699999833768231e-10)
    in_second = jnp.clip(jnp.exp(math.log(3.199999987213431e-10) - 2.7725887 * jax.random.uniform(key_list[22], (FF, D), jnp.float32) ** steps_of(key_list[22], (FF, D), ((0, 4),), -0.2, 0.2)), 1.9999999920083944e-11, 3.199999987213431e-10)
    bias_second = jnp.clip(jnp.exp(math.log(3.199999987213431e-10) - 2.7725887 * jax.random.uniform(key_list[23], (FF,), jnp.float32) ** steps_of(key_list[23], (FF,), ((0, 4),), -0.2, 0.2)), 1.9999999920083944e-11, 3.199999987213431e-10)
    out_second = jnp.clip(jnp.exp(math.log(1.400000004814217e-09) - 2.7668907 * jax.random.uniform(key_list[24], (FF, D), jnp.float32) ** steps_of(key_list[24], (FF, D), ((0, 4),), -0.2, 0.2)), 8.80000031178163e-11, 1.400000004814217e-09)
    norm_second = jnp.clip(jnp.exp(jax.random.uniform(key_list[25], (5, D), jnp.float32, math.log(2.449999925158153e-10), math.log(3.899999878598237e-09))), 2.449999925158153e-10, 3.899999878598237e-09)
    return {"block_in": block_in, "coords": coords, "lengths": lengths, "cotangent": cotangent, "step_count": step_count, "qkv_weight": qkv_weight, "proj_weight": proj_weight, "pair_weight": pair_weight, "in_weight": in_weight, "in_bias": in_bias, "out_weight": out_weight, "norm_params": norm_params, "qkv_first": qkv_first, "proj_first": proj_first, "pair_first": pair_first, "in_first": in_first, "bias_first": bias_first, "out_first": out_first, "norm_first": norm_first, "qkv_second": qkv_second, "proj_second": proj_second, "pair_second": pair_second, "in_second": in_second, "bias_second": bias_second, "out_second": out_second, "norm_second": norm_second}


@jax.custom_vjp
def low(v):
    return lax.optimization_barrier(v.astype(jnp.bfloat16)).astype(jnp.float32)

@jax.custom_vjp
def low_back(v):
    return v

def low_keep(v):
    return (low(v), None)

def low_pass(kept, grad):
    return (grad,)

def back_keep(v):
    return (v, None)

def back_low(kept, grad):
    return (low(grad),)
low.defvjp(low_keep, low_pass)
low_back.defvjp(back_keep, back_low)
highest = lax.Precision.HIGHEST
ln_eps = 1e-05
mask_fill = -1e+30
beta_one = 0.9
beta_two = 0.999
adam_eps = 1e-08
clip_level = 1.0

def layer_norm(rows, gain, shift):
    mean = lax.optimization_barrier(jnp.mean(rows, axis=-1, keepdims=True))
    centred = rows - mean
    variance = lax.optimization_barrier(jnp.mean(centred * centred, axis=-1, keepdims=True))
    return centred * lax.rsqrt(variance + ln_eps) * gain + shift

def segment_ids(lengths, width):
    ends = jnp.cumsum(lengths, axis=-1)
    places = lax.broadcasted_iota(jnp.int32, (lengths.shape[0], width, lengths.shape[1]), 1)
    return lax.optimization_barrier(jnp.sum((places >= ends[:, None, :]).astype(jnp.int32), axis=-1))

def gaussians(points):
    delta = points[:, :, None] - points[:, None, :]
    dist = jnp.sqrt(lax.optimization_barrier(jnp.sum(delta * delta, axis=0)))
    spacing = 12.8 / KERN
    centres = lax.broadcasted_iota(jnp.float32, (KERN,), 0) * spacing
    scaled = (dist[:, :, None] - centres) / spacing
    return jnp.exp(-0.5 * scaled * scaled)

def adam_step(weight, grad, first, second, clip, fix_one, fix_two, rate, decay):
    scaled = grad * clip
    first_new = beta_one * first + (1.0 - beta_one) * scaled
    second_new = beta_two * second + (1.0 - beta_two) * scaled * scaled
    ratio = first_new / fix_one / (jnp.sqrt(second_new / fix_two) + adam_eps)
    return (weight - rate * (ratio + decay * weight), first_new, second_new)

def reference(block_in, coords, lengths, cotangent, step_count, qkv_weight, proj_weight, pair_weight, in_weight, in_bias, out_weight, norm_params, qkv_first, proj_first, pair_first, in_first, bias_first, out_first, norm_first, qkv_second, proj_second, pair_second, in_second, bias_second, out_second, norm_second):
    labels = segment_ids(lengths, MOLBLK)
    points = coords.reshape(3, NBLOCKS, MOLBLK).transpose(1, 0, 2)
    scale = 1.0 / math.sqrt(HD)

    def forward(rows, w_qkv, w_proj, w_pair, w_in, b_in, w_out, params):
        first_norm = low(layer_norm(rows, params[0], params[1]))
        qkv = jnp.einsum('rd,scd->src', first_norm, low(w_qkv), precision=highest, preferred_element_type=jnp.float32)
        qkv = low(low_back(qkv))
        split = qkv.reshape(3, NBLOCKS, MOLBLK, HEADS, HD)
        pair_low = low(w_pair)

        def attend(items):
            query, keys, values, spots, marks = items
            gauss = low(gaussians(spots))
            bias = jnp.einsum('ijk,hk->hij', gauss, pair_low, precision=highest, preferred_element_type=jnp.float32)
            score = jnp.einsum('ihd,jhd->hij', query, keys, precision=highest, preferred_element_type=jnp.float32) * scale + bias
            score = low_back(score)
            same = marks[:, None] == marks[None, :]
            score = jnp.where(same[None], score, mask_fill)
            probs = jax.nn.softmax(score, axis=-1)
            return jnp.einsum('hij,jhd->ihd', low(probs), values, precision=highest, preferred_element_type=jnp.float32)
        mixed = lax.map(jax.checkpoint(attend), (split[0], split[1], split[2], points, labels))
        mixed = low(low_back(mixed.reshape(TOKENS, HEADS * HD)))
        attn = low_back(jnp.dot(mixed, low(w_proj), precision=highest, preferred_element_type=jnp.float32))
        mid = rows + attn
        second_norm = low(layer_norm(mid, params[2], params[3]))
        pre = jnp.einsum('rd,fd->rf', second_norm, low(w_in), precision=highest, preferred_element_type=jnp.float32)
        pre = low_back(pre + low(b_in))
        act = low(jax.nn.gelu(pre, approximate=False))
        ffn = low_back(jnp.dot(act, low(w_out), precision=highest, preferred_element_type=jnp.float32))
        return mid + ffn + params[4]
    rows_in = block_in.astype(jnp.float32)
    block_out, pullback = jax.vjp(forward, rows_in, qkv_weight, proj_weight, pair_weight, in_weight, in_bias, out_weight, norm_params)
    grads = pullback(cotangent.astype(jnp.float32))
    grad_input = grads[0]
    total = jnp.float32(0.0)
    for grad in grads[1:]:
        total = total + jnp.sum(grad * grad)
    grad_norm = jnp.sqrt(total)
    clip = clip_level / jnp.maximum(grad_norm, clip_level)
    count = step_count[0].astype(jnp.float32)
    fix_one = 1.0 - jnp.power(beta_one, count)
    fix_two = 1.0 - jnp.power(beta_two, count)
    qkv_out = adam_step(qkv_weight, grads[1], qkv_first, qkv_second, clip, fix_one, fix_two, 0.9, 0.01)
    proj_out = adam_step(proj_weight, grads[2], proj_first, proj_second, clip, fix_one, fix_two, 2.5, 0.01)
    pair_out = adam_step(pair_weight, grads[3], pair_first, pair_second, clip, fix_one, fix_two, 7.5, 0.01)
    in_out = adam_step(in_weight, grads[4], in_first, in_second, clip, fix_one, fix_two, 0.9, 0.01)
    bias_out = adam_step(in_bias, grads[5], bias_first, bias_second, clip, fix_one, fix_two, 7.5, 0.0)
    out_out = adam_step(out_weight, grads[6], out_first, out_second, clip, fix_one, fix_two, 0.45, 0.01)
    norm_out = adam_step(norm_params, grads[7], norm_first, norm_second, clip, fix_one, fix_two, 3.0, 0.0)
    return (block_out, grad_input, grad_norm.reshape(1), qkv_out[0], qkv_out[1], qkv_out[2], proj_out[0], proj_out[1], proj_out[2], pair_out[0], pair_out[1], pair_out[2], in_out[0], in_out[1], in_out[2], bias_out[0], bias_out[1], bias_out[2], out_out[0], out_out[1], out_out[2], norm_out[0], norm_out[1], norm_out[2])
```

```python
import functools
import math

import jax
import jax.numpy as jnp
from jax import lax
from jax.experimental import pallas as pl
from jax.experimental.pallas import tpu as pltpu
from jax.sharding import PartitionSpec as P

ln_eps = 1e-05
beta_one = 0.9
beta_two = 0.999
adam_eps = 1e-08
clip_level = 1.0
F32, BF16 = jnp.float32, jnp.bfloat16
NT = (((1,), (1,)), ((), ()))
TN = (((0,), (0,)), ((), ()))
KERN = 128
LANE = 128
SUB = 8
CHUNK = 32
KS = math.sqrt(0.5 * math.log2(math.e))
UNIT = KS / (12.8 / KERN)

def head_mask(heads, inner):
    rows = lax.broadcasted_iota(jnp.int32, (SUB, inner), 0)
    cols = lax.broadcasted_iota(jnp.int32, (SUB, inner), 1)
    hd = inner // heads
    return ((cols >= rows * hd) & (cols < (rows + 1) * hd)).astype(F32)

def setup_pairs(len_ref, b, coords_ref, dist, labs, labr, span, mols):
    pts = coords_ref[...]
    cols = jnp.transpose(jnp.concatenate([pts, jnp.zeros((5, span), F32)], 0))
    acc = None
    for a in range(3):
        d = cols[:, a:a + 1] - pts[a:a + 1, :]
        acc = d * d if acc is None else acc + d * d
    dist[...] = jnp.sqrt(acc) * UNIT
    rows = lax.broadcasted_iota(jnp.int32, (span, LANE), 0)
    lanes = lax.broadcasted_iota(jnp.int32, (SUB, span), 1)
    lr = jnp.zeros((span, LANE), jnp.int32)
    lc = jnp.zeros((SUB, span), jnp.int32)
    end = jnp.int32(0)
    for m in range(mols):
        end = end + len_ref[b, m]
        lr = lr + (rows >= end).astype(jnp.int32)
        lc = lc + (lanes >= end).astype(jnp.int32)
    labs[...] = lr
    labr[...] = lc

def tile_range(len_ref, b, first, last, span, mols):
    lo = jnp.int32(0); hi = jnp.int32(span); end = jnp.int32(0)
    for m in range(mols):
        end = end + len_ref[b, m]
        lo = jnp.where(end <= first, end, lo)
        hi = jnp.where((end > last) & (end < hi), end, hi)
    return lo // LANE, (hi + LANE - 1) // LANE

def gauss_tile(drow):
    sub = lax.broadcasted_iota(jnp.int32, (SUB, LANE), 0).astype(F32) * KS
    base = drow - sub
    parts = []
    for c in range(KERN // SUB):
        t = base - (KS * SUB * c)
        parts.append(jnp.exp2(-(t * t)))
    return jnp.concatenate(parts, 0).astype(BF16)

def expand(rows, mask):
    n, w = rows.shape
    return (rows[:, None, :] * mask[None]).reshape(n * SUB, w).astype(BF16)

def collapse(wide, mask):
    n, w = wide.shape
    return jnp.sum(wide.reshape(n // SUB, SUB, w) * mask[None], axis=1)

def fwd_kernel(heads, mols, len_ref, coords_ref, q_ref, k_ref, v_ref, w_ref, o_ref, p_ref, dist, labs, labr, sc, qf):
    span, inner = q_ref.shape
    b = pl.program_id(0)
    scale = 1.0 / math.sqrt(inner // heads)
    setup_pairs(len_ref, b, coords_ref, dist, labs, labr, span, mols)
    mask = head_mask(heads, inner)
    qf[...] = q_ref[...].astype(F32)
    kb = k_ref[...]; vb = v_ref[...]; wb = w_ref[...]

    def chunk(ci, carry):
        sc[...] = jnp.full(sc.shape, -1e30, F32)
        def group(g, carry):
            i0 = pl.multiple_of(ci * CHUNK + g * SUB, SUB)
            lo, hi = tile_range(len_ref, b, i0, i0 + SUB - 1, span, mols)
            def tile(jt, carry):
                j0 = pl.multiple_of(jt * LANE, LANE)
                lab = labr[:, pl.ds(j0, LANE)]
                dblk = dist[pl.ds(i0, SUB), pl.ds(j0, LANE)]
                lblk = labs[pl.ds(i0, SUB), :]
                for r in range(SUB):
                    drow = jnp.broadcast_to(dblk[r:r + 1], (SUB, LANE))
                    li = jnp.broadcast_to(lblk[r:r + 1], (SUB, LANE))
                    bias = jnp.dot(wb, gauss_tile(drow), preferred_element_type=F32)
                    row0 = pl.multiple_of((g * SUB + r) * SUB, SUB)
                    sc[pl.ds(row0, SUB), pl.ds(j0, LANE)] = jnp.where(li == lab, bias, -1e30)
                return carry
            return lax.fori_loop(lo, hi, tile, carry)
        lax.fori_loop(0, CHUNK // SUB, group, 0)
        c0 = pl.multiple_of(ci * CHUNK, CHUNK)
        qt = expand(qf[pl.ds(c0, CHUNK), :], mask)
        s = lax.dot_general(qt, kb, NT, preferred_element_type=F32)
        bias = sc[...]
        s = s * scale + bias
        top = jnp.max(s, axis=-1, keepdims=True)
        e = jnp.exp(s - top)
        pr = (e / jnp.sum(e, axis=-1, keepdims=True)).astype(BF16)
        p_ref[pl.ds(pl.multiple_of(ci * CHUNK * SUB, CHUNK * SUB), CHUNK * SUB), :] = pr
        ow = jnp.dot(pr, vb, preferred_element_type=F32)
        o_ref[pl.ds(c0, CHUNK), :] = collapse(ow, mask).astype(BF16)
        return carry
    lax.fori_loop(0, span // CHUNK, chunk, 0)

def attention(qkv, coords, lengths, pair_low, heads):
    _, rows, inner = qkv.shape
    blocks, mols = lengths.shape
    span = rows // blocks
    w = jnp.pad(pair_low, ((0, SUB - heads), (0, 0)))
    part = lambda s: pl.BlockSpec((None, span, inner), lambda b, *_: (s, b, 0))
    return pl.pallas_call(
        functools.partial(fwd_kernel, heads, mols),
        out_shape=(jax.ShapeDtypeStruct((rows, inner), BF16), jax.ShapeDtypeStruct((rows * SUB, span), BF16)),
        grid_spec=pltpu.PrefetchScalarGridSpec(
            num_scalar_prefetch=1, grid=(blocks,),
            in_specs=[pl.BlockSpec((3, span), lambda b, *_: (0, b)), part(0), part(1), part(2),
                      pl.BlockSpec((SUB, KERN), lambda b, *_: (0, 0))],
            out_specs=[pl.BlockSpec((span, inner), lambda b, *_: (b, 0)),
                       pl.BlockSpec((span * SUB, span), lambda b, *_: (b, 0))],
            scratch_shapes=[pltpu.VMEM((span, span), F32), pltpu.VMEM((span, LANE), jnp.int32),
                            pltpu.VMEM((SUB, span), jnp.int32), pltpu.VMEM((CHUNK * SUB, span), F32),
                            pltpu.VMEM((span, inner), F32)]),
        name="attend",
    )(lengths, coords, qkv, qkv, qkv, w)

def bwd_kernel(heads, mols, len_ref, coords_ref, q_ref, k_ref, v_ref, do_ref, p_ref, dqkv_ref, pg_ref,
               dist, labs, labr, ds, qf, dof, dkt, dvt):
    span, inner = q_ref.shape
    b = pl.program_id(0)
    scale = 1.0 / math.sqrt(inner // heads)
    setup_pairs(len_ref, b, coords_ref, dist, labs, labr, span, mols)
    mask = head_mask(heads, inner)
    qf[...] = q_ref[...].astype(F32)
    dof[...] = do_ref[...].astype(F32)
    kb = k_ref[...]; vb = v_ref[...]
    dkt[...] = jnp.zeros_like(dkt); dvt[...] = jnp.zeros_like(dvt)
    @pl.when(b == 0)
    def _():
        pg_ref[...] = jnp.zeros_like(pg_ref)

    def chunk(ci, carry):
        c0 = pl.multiple_of(ci * CHUNK, CHUNK)
        r0 = pl.multiple_of(ci * CHUNK * SUB, CHUNK * SUB)
        qt = expand(qf[pl.ds(c0, CHUNK), :], mask)
        dot = expand(dof[pl.ds(c0, CHUNK), :], mask)
        pb = p_ref[pl.ds(r0, CHUNK * SUB), :]
        pf = pb.astype(F32)
        dp = lax.dot_general(dot, vb, NT, preferred_element_type=F32)
        rowdot = jnp.sum(pf * dp, axis=-1, keepdims=True)
        dsf = pf * (dp - rowdot)
        dsb = dsf.astype(BF16)
        ds[...] = dsf
        dqkv_ref[0, pl.ds(c0, CHUNK), :] = (collapse(jnp.dot(dsb, kb, preferred_element_type=F32), mask) * scale).astype(BF16)
        dkt[...] += lax.dot_general(qt, dsb, TN, preferred_element_type=F32)
        dvt[...] += lax.dot_general(dot, pb, TN, preferred_element_type=F32)

        def group(g, carry):
            i0 = pl.multiple_of(ci * CHUNK + g * SUB, SUB)
            lo, hi = tile_range(len_ref, b, i0, i0 + SUB - 1, span, mols)
            def tile(jt, acc):
                j0 = pl.multiple_of(jt * LANE, LANE)
                dblk = dist[pl.ds(i0, SUB), pl.ds(j0, LANE)]
                for r in range(SUB):
                    drow = jnp.broadcast_to(dblk[r:r + 1], (SUB, LANE))
                    row0 = pl.multiple_of((g * SUB + r) * SUB, SUB)
                    d = ds[pl.ds(row0, SUB), pl.ds(j0, LANE)].astype(BF16)
                    acc = acc + lax.dot_general(d, gauss_tile(drow), NT, preferred_element_type=F32)
                return acc
            return lax.fori_loop(lo, hi, tile, carry)
        return lax.fori_loop(0, CHUNK // SUB, group, carry)
    pg_ref[...] += lax.fori_loop(0, span // CHUNK, chunk, jnp.zeros((SUB, KERN), F32))
    dqkv_ref[1] = jnp.transpose(dkt[...] * scale).astype(BF16)
    dqkv_ref[2] = jnp.transpose(dvt[...]).astype(BF16)

def attention_back(qkv, grad_heads, probs, coords, lengths, heads):
    _, rows, inner = qkv.shape
    blocks, mols = lengths.shape
    span = rows // blocks
    part = lambda s: pl.BlockSpec((None, span, inner), lambda b, *_: (s, b, 0))
    return pl.pallas_call(
        functools.partial(bwd_kernel, heads, mols),
        out_shape=(jax.ShapeDtypeStruct((3, rows, inner), BF16), jax.ShapeDtypeStruct((SUB, KERN), F32)),
        grid_spec=pltpu.PrefetchScalarGridSpec(
            num_scalar_prefetch=1, grid=(blocks,),
            in_specs=[pl.BlockSpec((3, span), lambda b, *_: (0, b)), part(0), part(1), part(2),
                      pl.BlockSpec((span, inner), lambda b, *_: (b, 0)),
                      pl.BlockSpec((span * SUB, span), lambda b, *_: (b, 0))],
            out_specs=[pl.BlockSpec((3, span, inner), lambda b, *_: (0, b, 0)),
                       pl.BlockSpec((SUB, KERN), lambda b, *_: (0, 0))],
            scratch_shapes=[pltpu.VMEM((span, span), F32), pltpu.VMEM((span, LANE), jnp.int32),
                            pltpu.VMEM((SUB, span), jnp.int32), pltpu.VMEM((CHUNK * SUB, span), F32),
                            pltpu.VMEM((span, inner), F32), pltpu.VMEM((span, inner), F32),
                            pltpu.VMEM((inner, span), F32), pltpu.VMEM((inner, span), F32)]),
        name="attend_back",
    )(lengths, coords, qkv, qkv, qkv, grad_heads, probs)


MESH = pl.DeviceIdType.MESH
NN = (((1,), (0,)), ((), ()))
VM = pl.BlockSpec(memory_space=pltpu.VMEM)
HBM = pl.BlockSpec(memory_space=pl.ANY)
DMA = pltpu.SemaphoreType.DMA


def mm(a, b, dims=NN):
    return lax.dot_general(a, b, dims, preferred_element_type=F32)


def remote(src, dst, send, recv, axis, target):
    return pltpu.make_async_remote_copy(
        src_ref=src, dst_ref=dst, send_sem=send, recv_sem=recv,
        device_id={axis: target}, device_id_type=MESH)


def greet(sizes):
    barrier = pltpu.get_barrier_semaphore()
    total = 0
    for axis, size in sizes.items():
        me = lax.axis_index(axis)
        for k in range(1, size):
            pl.semaphore_signal(barrier, inc=1, device_id={axis: lax.rem(me + k, size)}, device_id_type=MESH)
        total += size - 1
    pl.semaphore_wait(barrier, total)


class Seat:
    def __init__(self, n):
        self.n, self.nx = n, n // 2
        self.me = lax.axis_index("mp")
        self.core = lax.rem(self.me, 2)
        self.x = self.me // 2
        self.sib = self.me + 1 - 2 * self.core

    def chip(self, k):
        return lax.rem(self.x + 1 + k, self.nx)

    def source(self, k):
        return lax.rem(self.x + self.nx - 1 - k, self.nx)


def scatter_scratch(n, rows, width):
    nx = n // 2
    buf = lambda m: pltpu.VMEM((m, rows, width), BF16)
    return [buf(nx), buf(nx), buf(max(nx - 1, 1)), buf(max(nx - 1, 1)), DMA((nx,)), DMA((nx,)),
            DMA((max(nx - 1, 1),)), DMA((max(nx - 1, 1),))]


class Scatter:
    def __init__(self, seat, scratch):
        self.seat = seat
        self.out1, self.in1, self.out2, self.in2, self.s1, self.r1, self.s2, self.r2 = scratch

    def first(self, k):
        return remote(self.out1.at[k], self.in1.at[k], self.s1.at[k], self.r1.at[k], "mp", self.seat.sib)

    def second(self, k):
        target = self.seat.chip(k) * 2 + self.seat.core
        return remote(self.out2.at[k], self.in2.at[k], self.s2.at[k], self.r2.at[k], "mp", target)

    def push(self, block):
        for k in range(self.seat.nx):
            self.out1[k] = block(self.seat.chip(k) * 2 + 1 - self.seat.core).astype(BF16)
            self.first(k).start()

    def pass_on(self, block):
        seat = self.seat
        parts = [block(seat.chip(k) * 2 + seat.core) for k in range(seat.nx)]
        for k in range(seat.nx):
            self.first(k).wait_recv()
            whole = parts[k] + self.in1[k].astype(F32)
            if k < seat.nx - 1:
                self.out2[k] = whole.astype(BF16)
                self.second(k).start()
        return whole

    def finish(self, whole):
        for k in range(self.seat.nx - 1):
            self.second(k).wait_recv()
            whole = whole + self.in2[k].astype(F32)
        return whole

    def drain(self):
        for k in range(self.seat.nx):
            self.first(k).wait_send()
        for k in range(self.seat.nx - 1):
            self.second(k).wait_send()


def gather_scratch(n):
    nx = n // 2
    return [DMA((max(nx - 1, 1),)), DMA((max(nx - 1, 1),)), DMA((nx,)), DMA((nx,))]


class Gather:
    def __init__(self, seat, rows, scratch):
        self.seat, self.rows = seat, rows
        self.sx, self.rx, self.sc, self.rc = scratch

    def across(self, k):
        r = self.rows.at[self.seat.me]
        return remote(r, r, self.sx.at[k], self.rx.at[k], "mp", self.seat.chip(k) * 2 + self.seat.core)

    def along(self, k):
        chip = self.seat.x if k == self.seat.nx - 1 else self.seat.source(k)
        r = self.rows.at[chip * 2 + self.seat.core]
        return remote(r, r, self.sc.at[k], self.rc.at[k], "mp", self.seat.sib)

    def start(self):
        for k in range(self.seat.nx - 1):
            self.across(k).start()
        self.along(self.seat.nx - 1).start()

    def forward(self):
        for k in range(self.seat.nx - 1):
            self.across(k).wait_recv()
            self.along(k).start()

    def finish(self):
        for k in range(self.seat.nx):
            self.along(k).wait_recv()

    def drain(self):
        for k in range(self.seat.nx - 1):
            self.across(k).wait_send()
        for k in range(self.seat.nx):
            self.along(k).wait_send()


def centre(rows):
    c = rows - jnp.mean(rows, axis=-1, keepdims=True)
    r = lax.rsqrt(jnp.mean(c * c, axis=-1, keepdims=True) + ln_eps)
    return c * r, r


def norm_back(rows, gain, e):
    vhat, r = centre(rows)
    ge = e * gain
    dv = r * (ge - jnp.mean(ge, axis=-1, keepdims=True) - vhat * jnp.mean(ge * vhat, axis=-1, keepdims=True))
    return dv, jnp.sum(e * vhat, axis=0, keepdims=True), jnp.sum(e, axis=0, keepdims=True)


def enter_kernel(n, x_ref, dy_ref, np_ref, w_hbm, h_ref, dyall_ref, qkv_ref, w32, wsem, *sems):
    seat = Seat(n)
    load = pltpu.make_async_copy(w_hbm, w32, wsem)
    load.start()
    greet({"mp": n})
    vhat, _ = centre(x_ref[...].astype(F32))
    h_ref[seat.me] = (vhat * np_ref[0:1] + np_ref[1:2]).astype(BF16)
    dyall_ref[seat.me] = dy_ref[...]
    gh = Gather(seat, h_ref, sems[:4])
    gd = Gather(seat, dyall_ref, sems[4:])
    gh.start()
    load.wait()
    gh.forward()
    gd.start()
    gh.finish()
    rows = h_ref.shape[1]
    for s in range(3):
        w = w32[s].astype(BF16)

        def block(b, carry):
            r0 = pl.multiple_of(b * rows, rows)
            qkv_ref[s, pl.ds(r0, rows), :] = mm(h_ref[b], w, NT).astype(BF16)
            return carry

        lax.fori_loop(0, n, block, 0)
    gd.forward()
    gd.finish()
    gh.drain()
    gd.drain()


def enter(n, x, dy, params, qkv_weight):
    rows, width = x.shape
    _, inner, _ = qkv_weight.shape
    return pl.pallas_call(
        functools.partial(enter_kernel, n),
        out_shape=(jax.ShapeDtypeStruct((n, rows, width), BF16), jax.ShapeDtypeStruct((n, rows, width), BF16),
                   jax.ShapeDtypeStruct((3, n * rows, inner), BF16)),
        in_specs=[VM, VM, VM, HBM], out_specs=[VM, VM, VM],
        scratch_shapes=[pltpu.VMEM(qkv_weight.shape, F32), DMA, *gather_scratch(n), *gather_scratch(n)],
        compiler_params=pltpu.CompilerParams(collective_id=0, has_side_effects=True),
        name="enter",
    )(x, dy, params, qkv_weight)


def middle_kernel(n, x_ref, dy_ref, dyall_ref, o_ref, np_ref, bias_ref, pw_hbm, iw_hbm, ow_hbm,
                  block_ref, mid_ref, do_ref, og_ref, ig_ref, pg_ref, bg_ref, small_ref,
                  pw32, iw32, ow32, pw, iw, ow, h2, da, act, dpre, dact, wsem, *rest):
    seat = Seat(n)
    rows, width = x_ref.shape
    loads = [pltpu.make_async_copy(a, b, wsem.at[i])
             for i, (a, b) in enumerate([(pw_hbm, pw32), (ow_hbm, ow32), (iw_hbm, iw32)])]
    for c in loads:
        c.start()
    scat = [Scatter(seat, rest[8 * i:8 * i + 8]) for i in range(3)]
    gath = [Gather(seat, r, rest[24 + 4 * i:28 + 4 * i]) for i, r in enumerate((h2, da))]
    greet({"mp": n})
    at = lambda b: pl.ds(pl.multiple_of(b * rows, rows), rows)

    loads[0].wait()
    pw[...] = pw32[...].astype(BF16)
    attn_block = lambda b: mm(o_ref[at(b), :], pw[...])
    scat[0].push(attn_block)
    loads[1].wait()
    ow[...] = ow32[...].astype(BF16)
    whole = scat[0].pass_on(attn_block)
    loads[2].wait()
    iw[...] = iw32[...].astype(BF16)

    def back_act(b, carry):
        dact[b] = mm(dyall_ref[b], ow[...], NT)
        return carry

    lax.fori_loop(0, n, back_act, 0)
    mid = x_ref[...].astype(F32) + scat[0].finish(whole)
    vhat, _ = centre(mid)
    h2[seat.me] = (vhat * np_ref[2:3] + np_ref[3:4]).astype(BF16)
    mid_ref[...] = mid
    gath[0].start()
    gath[0].forward()
    gath[0].finish()

    bg_ref[...] = jnp.zeros_like(bg_ref)
    bias = bias_ref[...].astype(BF16).astype(F32)

    def feed_block(b):
        pre = mm(h2[b], iw[...], NT) + bias
        phi = 0.5 + 0.5 * lax.erf(pre * math.sqrt(0.5))
        act[b] = (pre * phi).astype(BF16)
        slope = phi + pre * (jnp.exp(-0.5 * pre * pre) * (1.0 / math.sqrt(2.0 * math.pi)))
        d = (dact[b] * slope).astype(BF16)
        dpre[b] = d
        bg_ref[...] += jnp.sum(d.astype(F32), axis=0, keepdims=True)
        return mm(d, iw[...])

    scat[1].push(feed_block)
    whole = scat[1].pass_on(feed_block)
    out_block = lambda b: mm(act[b], ow[...])
    scat[2].push(out_block)
    dh2 = scat[1].finish(whole)
    dv, gain, shift = norm_back(mid_ref[...], np_ref[2:3], dh2)
    dy = dy_ref[...].astype(F32)
    dx1 = dy + dv
    da[seat.me] = dx1.astype(BF16)
    gath[1].start()
    small_ref[...] = jnp.concatenate(
        [gain, shift, jnp.sum(dy, axis=0, keepdims=True), jnp.zeros((5, width), F32)], 0)
    whole = scat[2].pass_on(out_block)
    gath[1].forward()

    hidden = iw.shape[0]
    step = LANE if hidden % LANE == 0 else hidden

    def grads(i, carry):
        c0 = pl.multiple_of(i * step, step)
        acc_o = jnp.zeros((step, width), F32)
        acc_i = jnp.zeros((step, width), F32)
        for b in range(n):
            acc_o += mm(act[b, :, pl.ds(c0, step)], dyall_ref[b], TN)
            acc_i += mm(dpre[b, :, pl.ds(c0, step)], h2[b], TN)
        og_ref[pl.ds(c0, step), :] = acc_o
        ig_ref[pl.ds(c0, step), :] = acc_i
        return carry

    lax.fori_loop(0, hidden // step, grads, 0)
    block_ref[...] = mid_ref[...] + scat[2].finish(whole) + np_ref[4:5]
    mid_ref[...] = dx1
    gath[1].finish()

    def heads_block(b, carry):
        do_ref[at(b), :] = mm(da[b], pw[...], NT).astype(BF16)
        pg_ref[...] += mm(o_ref[at(b), :], da[b], TN)
        return carry

    pg_ref[...] = jnp.zeros_like(pg_ref)
    lax.fori_loop(0, n, heads_block, 0)
    for c in scat + gath:
        c.drain()


def middle(n, x, dy, dy_all, o, params, bias, proj_weight, in_weight, out_weight):
    rows, width = x.shape
    hidden = in_weight.shape[0]
    inner = proj_weight.shape[0]
    f = lambda *s: jax.ShapeDtypeStruct(s, F32)
    return pl.pallas_call(
        functools.partial(middle_kernel, n),
        out_shape=(f(rows, width), f(rows, width), jax.ShapeDtypeStruct((n * rows, inner), BF16),
                   f(hidden, width), f(hidden, width), f(inner, width), f(1, hidden), f(8, width)),
        in_specs=[VM] * 6 + [HBM] * 3, out_specs=[VM] * 8,
        scratch_shapes=[pltpu.VMEM((inner, width), F32), pltpu.VMEM((hidden, width), F32),
                        pltpu.VMEM((hidden, width), F32), pltpu.VMEM((inner, width), BF16),
                        pltpu.VMEM((hidden, width), BF16), pltpu.VMEM((hidden, width), BF16),
                        pltpu.VMEM((n, rows, width), BF16), pltpu.VMEM((n, rows, width), BF16),
                        pltpu.VMEM((n, rows, hidden), BF16), pltpu.VMEM((n, rows, hidden), BF16),
                        pltpu.VMEM((n, rows, hidden), F32), DMA((3,)),
                        *[s for _ in range(3) for s in scatter_scratch(n, rows, width)],
                        *gather_scratch(n), *gather_scratch(n)],
        compiler_params=pltpu.CompilerParams(collective_id=1, has_side_effects=True, vmem_limit_bytes=60 << 20),
        name="middle",
    )(x, dy, dy_all, o, params, bias, proj_weight, in_weight, out_weight)


class Grid:
    def __init__(self, ny, nz):
        self.ny, self.nz = ny, nz
        self.me = lax.axis_index("dp")
        self.z, self.y = self.me // ny, lax.rem(self.me, ny)

    def yto(self, k):
        return lax.rem(self.y + 1 + k, self.ny)

    def yfrom(self, k):
        return lax.rem(self.y + self.ny - 1 - k, self.ny)

    def zto(self, k):
        return lax.rem(self.z + 1 + k, self.nz)

    def zfrom(self, k):
        return lax.rem(self.z + self.nz - 1 - k, self.nz)


def sum_scratch(ny, nz, chunk, width):
    y, z = max(ny - 1, 1), max(nz - 1, 1)
    return [pltpu.VMEM((y, nz, chunk, width), BF16), pltpu.VMEM((y, nz, chunk, width), BF16),
            pltpu.VMEM((z, chunk, width), BF16), pltpu.VMEM((z, chunk, width), BF16),
            DMA((y,)), DMA((y,)), DMA((z,)), DMA((z,)), DMA((z,)), DMA((z,)), DMA((nz, y)), DMA((nz, y))]


class Sum:
    def __init__(self, grid, grad, result, scratch):
        self.grid, self.grad, self.result = grid, grad, result
        (self.oa, self.ia, self.ob, self.ib, self.sa, self.ra, self.sb, self.rb,
         self.sz, self.rz, self.sy, self.ry) = scratch
        self.chunk = result.shape[1]

    def piece(self, z, y):
        start = pl.multiple_of((z * self.grid.ny + y) * self.chunk, 8)
        return self.grad[pl.ds(start, self.chunk), :]

    def copy_y(self, k):
        g = self.grid
        return remote(self.oa.at[k], self.ia.at[k], self.sa.at[k], self.ra.at[k], "dp", g.z * g.ny + g.yto(k))

    def copy_z(self, k):
        g = self.grid
        return remote(self.ob.at[k], self.ib.at[k], self.sb.at[k], self.rb.at[k], "dp", g.zto(k) * g.ny + g.y)

    def push(self):
        g = self.grid
        for k in range(g.ny - 1):
            for z in range(g.nz):
                self.oa[k, z] = self.piece(z, g.yto(k)).astype(BF16)
            self.copy_y(k).start()

    def pass_on(self):
        g = self.grid
        for k in range(g.ny - 1):
            self.copy_y(k).wait_recv()
        for k in range(g.nz):
            z = g.zto(k)
            whole = self.piece(z, g.y)
            for j in range(g.ny - 1):
                whole = whole + self.ia[j, z].astype(F32)
            if k < g.nz - 1:
                self.ob[k] = whole.astype(BF16)
                self.copy_z(k).start()
        self.own = whole

    def finish(self):
        for k in range(self.grid.nz - 1):
            self.copy_z(k).wait_recv()
            self.own = self.own + self.ib[k].astype(F32)
        self.result[self.grid.me] = self.own.astype(BF16)
        for k in range(self.grid.nz - 1):
            self.back_z(k).start()
        for k in range(self.grid.ny - 1):
            self.back_y(self.grid.nz - 1, k).start()
        return self.own

    def back_z(self, k):
        g = self.grid
        r = self.result.at[g.me]
        return remote(r, r, self.sz.at[k], self.rz.at[k], "dp", g.zto(k) * g.ny + g.y)

    def back_y(self, k, j):
        g = self.grid
        z = g.z if k == g.nz - 1 else g.zfrom(k)
        r = self.result.at[z * g.ny + g.y]
        return remote(r, r, self.sy.at[k, j], self.ry.at[k, j], "dp", g.z * g.ny + g.yto(j))

    def forward(self):
        g = self.grid
        for k in range(g.nz - 1):
            self.back_z(k).wait_recv()
            for j in range(g.ny - 1):
                self.back_y(k, j).start()

    def close(self):
        g = self.grid
        for k in range(g.nz):
            for j in range(g.ny - 1):
                self.back_y(k, j).wait_recv()
        for k in range(g.ny - 1):
            self.copy_y(k).wait_send()
        for k in range(g.nz - 1):
            self.copy_z(k).wait_send()
            self.back_z(k).wait_send()
        for k in range(g.nz):
            for j in range(g.ny - 1):
                self.back_y(k, j).wait_send()


class Share:
    def __init__(self, axis, slots, send, recv):
        self.axis, self.slots, self.send, self.recv = axis, slots, send, recv
        self.size = slots.shape[0]
        self.me = lax.axis_index(axis)

    def copy(self, k):
        r = self.slots.at[self.me]
        return remote(r, r, self.send.at[k], self.recv.at[k], self.axis, lax.rem(self.me + 1 + k, self.size))

    def start(self, value):
        self.slots[self.me] = value
        for k in range(self.size - 1):
            self.copy(k).start()

    def total(self):
        for k in range(self.size - 1):
            self.copy(k).wait_recv()
        out = self.slots[0]
        for i in range(1, self.size):
            out = out + self.slots[i]
        return out

    def drain(self):
        for k in range(self.size - 1):
            self.copy(k).wait_send()


def share_scratch(size, rows, width):
    return [pltpu.VMEM((size, rows, width), F32), DMA((max(size - 1, 1),)), DMA((max(size - 1, 1),))]


def square(v):
    return jnp.sum(jnp.sum(v * v, axis=1, keepdims=True), axis=0, keepdims=True)


def leave_kernel(n, ny, nz, x_ref, dx_ref, np_ref, dqkv_ref, h_ref, og_ref, ig_ref, pg_ref, bg_ref, pair_ref,
                 mid_small_ref, w_hbm, gi_ref, so_ref, si_ref, sp_ref, sq_ref, small_ref, bias_ref, pairs_ref, norm_ref,
                 w32, w, qg, wsem, *rest):
    seat, grid = Seat(n), Grid(ny, nz)
    rows, width = x_ref.shape
    inner = w.shape[1]
    load = pltpu.make_async_copy(w_hbm, w32, wsem)
    load.start()
    scat = Scatter(seat, rest[:8])
    sums = [Sum(grid, g, r, rest[8 + 12 * i:20 + 12 * i])
            for i, (g, r) in enumerate([(og_ref, so_ref), (ig_ref, si_ref), (pg_ref, sp_ref), (qg, sq_ref)])]
    shares = [Share(a, *rest[56 + 3 * i:59 + 3 * i]) for i, a in enumerate(("mp", "dp", "dp", "dp", "mp", "dp"))]
    small_mp, small_dp, bias_dp, pair_dp, sq_mp, sq_dp = shares
    greet({"mp": n, "dp": ny * nz})
    at = lambda b: pl.ds(pl.multiple_of(b * rows, rows), rows)

    load.wait()
    w[...] = w32[...].astype(BF16)

    def first_block(b):
        return sum(mm(dqkv_ref[s, at(b), :], w[s]) for s in range(3))

    scat.push(first_block)
    whole = scat.pass_on(first_block)
    for s in sums[:3]:
        s.push()
    bias_dp.start(jnp.broadcast_to(bg_ref[...], bias_dp.slots.shape[1:]))
    pair_dp.start(pair_ref[...])
    for s in range(3):
        acc = jnp.zeros((inner, width), F32)
        for b in range(n):
            acc = acc + mm(dqkv_ref[s, at(b), :], h_ref[b], TN)
        qg[pl.ds(s * inner, inner), :] = acc
    sums[3].push()
    dh1 = scat.finish(whole)
    dv, gain, shift = norm_back(x_ref[...].astype(F32), np_ref[0:1], dh1)
    gi_ref[...] = dx_ref[...] + dv
    small_mp.start(jnp.concatenate([gain, shift, mid_small_ref[0:6]], 0))
    sums[0].pass_on()
    small_dp.start(small_mp.total())
    sums[1].pass_on()
    squares = square(sums[0].finish())
    sums[2].pass_on()
    sums[3].pass_on()
    squares = squares + square(sums[1].finish())
    squares = squares + square(sums[2].finish())
    squares = squares + square(sums[3].finish())
    small = small_dp.total()
    small_ref[...] = small
    bias = bias_dp.total()
    bias_ref[...] = bias
    pairs = pair_dp.total()
    pairs_ref[...] = pairs
    row = lax.broadcasted_iota(jnp.int32, (8, LANE), 0)
    local = square(bias[0:1]) + square(pairs)
    sq_mp.start(jnp.where(row == 0, squares, jnp.where(row == 1, local, 0.0)))
    sums[0].forward()
    sq_dp.start(sq_mp.total())
    for s in sums[1:]:
        s.forward()
    norm_ref[...] = sq_dp.total()[0:1] + sq_dp.slots[0, 1:2] + square(small)
    for s in sums:
        s.close()
    scat.drain()
    for s in shares:
        s.drain()


def leave(n, ny, nz, x, dx, params, dqkv, h, grads, bias_grad, pair_grad, small, qkv_weight):
    rows, width = x.shape
    inner = qkv_weight.shape[1]
    ndp = ny * nz
    tall = [g.shape[0] for g in grads] + [3 * inner]
    hidden = bias_grad.shape[1]
    f = lambda *s: jax.ShapeDtypeStruct(s, F32)
    return pl.pallas_call(
        functools.partial(leave_kernel, n, ny, nz),
        out_shape=(f(rows, width), *[jax.ShapeDtypeStruct((ndp, t // ndp, width), BF16) for t in tall],
                   f(8, width), f(8, hidden), f(8, LANE), f(1, LANE)),
        in_specs=[VM] * 11 + [HBM], out_specs=[VM] * 9,
        scratch_shapes=[pltpu.VMEM(qkv_weight.shape, F32), pltpu.VMEM(qkv_weight.shape, BF16),
                        pltpu.VMEM((3 * inner, width), F32), DMA, *scatter_scratch(n, rows, width),
                        *[s for t in tall for s in sum_scratch(ny, nz, t // ndp, width)],
                        *share_scratch(n, 8, width), *share_scratch(ndp, 8, width), *share_scratch(ndp, 8, hidden),
                        *share_scratch(ndp, 8, LANE), *share_scratch(n, 8, LANE), *share_scratch(ndp, 8, LANE)],
        compiler_params=pltpu.CompilerParams(collective_id=2, has_side_effects=True, vmem_limit_bytes=60 << 20),
        name="leave",
    )(x, dx, params, dqkv, h, *grads, bias_grad, pair_grad, small, qkv_weight)


def leave_plain(n, x, dx, params, dqkv, h, grads, bias_grad, pair_grad, small, qkv_weight):
    part = sum(mm(dqkv[s], qkv_weight[s].astype(BF16)) for s in range(3))
    dh1 = lax.psum_scatter(part, "mp", scatter_dimension=0, tiled=True)
    dv, gain, shift = norm_back(x.astype(F32), params[0:1], dh1)
    hh = h.reshape(-1, h.shape[-1])
    qg = jnp.concatenate([mm(dqkv[s], hh, TN) for s in range(3)], 0)
    og, ig, pg, qg, bias, pair = lax.psum((*grads, qg, bias_grad, pair_grad), "dp")
    small = lax.psum(jnp.concatenate([gain, shift, small[0:6]], 0), ("dp", "mp"))
    local = sum(square(v) for v in (og, ig, pg, qg, bias, pair))
    total = lax.psum(local, "mp") + square(small)
    return dx + dv, og, ig, pg, qg, small, bias, pair, total


def adam_step(weight, grad, first, second, clip, fix_one, fix_two, rate, decay):
    scaled = grad * clip
    first_new = beta_one * first + (1.0 - beta_one) * scaled
    second_new = beta_two * second + (1.0 - beta_two) * scaled * scaled
    ratio = first_new / fix_one / (jnp.sqrt(second_new / fix_two) + adam_eps)
    return (weight - rate * (ratio + decay * weight), first_new, second_new)


def per_device(n, ndp, block_in, coords, lengths, cotangent, step_count, *state):
    weights, firsts, seconds = state[:7], state[7:14], state[14:]
    qkv_weight, proj_weight, pair_weight, in_weight, in_bias, out_weight, params = weights
    heads = pair_weight.shape[0]
    pair_low = pair_weight.astype(BF16)
    h, dy_all, qkv = enter(n, block_in, cotangent, params, qkv_weight)
    o, probs = attention(qkv, coords, lengths, pair_low, heads)
    block_out, dx, do, og, ig, pg, bg, small = middle(
        n, block_in, cotangent, dy_all, o, params, in_bias.reshape(1, -1), proj_weight, in_weight, out_weight)
    dqkv, pair_grad = attention_back(qkv, do, probs, coords, lengths, heads)
    ny = n // 2 if ndp % (n // 2) == 0 else 1
    rest = (block_in, dx, params, dqkv, h, (og, ig, pg), bg, pair_grad, small, qkv_weight)
    if all(t % (8 * ndp) == 0 for t in (og.shape[0], pg.shape[0], 3 * qkv_weight.shape[1])):
        done = leave(n, ny, ndp // ny, *rest)
    else:
        done = leave_plain(n, *rest)
    grad_input, og, ig, pg, qg, small, bias, pair, total = done
    grad_norm = jnp.sqrt(total[0, 0])
    clip = clip_level / jnp.maximum(grad_norm, clip_level)
    count = step_count[0].astype(F32)
    fix_one = 1.0 - jnp.power(beta_one, count)
    fix_two = 1.0 - jnp.power(beta_two, count)
    grads = (qg.reshape(qkv_weight.shape), pg.reshape(proj_weight.shape), pair[:heads], ig.reshape(in_weight.shape),
             bias[0], og.reshape(out_weight.shape), small[:5])
    rates = (0.9, 2.5, 7.5, 0.9, 7.5, 0.45, 3.0)
    decays = (0.01, 0.01, 0.01, 0.01, 0.0, 0.01, 0.0)
    outs = [block_out, grad_input, grad_norm.reshape(1)]
    for w, g, m, u, rate, decay in zip(weights, grads, firsts, seconds, rates, decays):
        outs.extend(adam_step(w, g.astype(F32), m, u, clip, fix_one, fix_two, rate, decay))
    return tuple(outs)


def solution(mesh):
    rows, mp = P(("dp", "mp"), None), P("mp", None)
    stacked = P(None, "mp", None)
    params = (stacked, mp, mp, mp, P("mp"), mp, P())
    in_specs = (rows, P(None, "dp"), P("dp", None), rows, P(), *params, *params, *params)
    out_specs = (rows, rows, P(), *[s for s in params for _ in range(3)])
    return jax.shard_map(
        functools.partial(per_device, mesh.shape["mp"], mesh.shape["dp"]),
        mesh=mesh, in_specs=in_specs, out_specs=out_specs, check_vma=False)
```

```python
import functools
import math

import jax
import jax.numpy as jnp
from jax import lax
from jax.experimental import pallas as pl
from jax.experimental.pallas import tpu as pltpu
from jax.sharding import PartitionSpec as P

ln_eps = 1e-05
beta_one = 0.9
beta_two = 0.999
adam_eps = 1e-08
clip_level = 1.0
F32, BF16 = jnp.float32, jnp.bfloat16
NT = (((1,), (1,)), ((), ()))
TN = (((0,), (0,)), ((), ()))
KERN = 128
LANE = 128
SUB = 8
CHUNK = 32
KS = math.sqrt(0.5 * math.log2(math.e))
UNIT = KS / (12.8 / KERN)

def head_mask(heads, inner):
    rows = lax.broadcasted_iota(jnp.int32, (SUB, inner), 0)
    cols = lax.broadcasted_iota(jnp.int32, (SUB, inner), 1)
    hd = inner // heads
    return ((cols >= rows * hd) & (cols < (rows + 1) * hd)).astype(F32)

def setup_pairs(len_ref, b, coords_ref, dist, labs, labr, span, mols):
    pts = coords_ref[...]
    cols = jnp.transpose(jnp.concatenate([pts, jnp.zeros((5, span), F32)], 0))
    acc = None
    for a in range(3):
        d = cols[:, a:a + 1] - pts[a:a + 1, :]
        acc = d * d if acc is None else acc + d * d
    dist[...] = jnp.sqrt(acc) * UNIT
    rows = lax.broadcasted_iota(jnp.int32, (span, LANE), 0)
    lanes = lax.broadcasted_iota(jnp.int32, (SUB, span), 1)
    lr = jnp.zeros((span, LANE), jnp.int32)
    lc = jnp.zeros((SUB, span), jnp.int32)
    end = jnp.int32(0)
    for m in range(mols):
        end = end + len_ref[b, m]
        lr = lr + (rows >= end).astype(jnp.int32)
        lc = lc + (lanes >= end).astype(jnp.int32)
    labs[...] = lr
    labr[...] = lc

def tile_range(len_ref, b, first, last, span, mols):
    lo = jnp.int32(0); hi = jnp.int32(span); end = jnp.int32(0)
    for m in range(mols):
        end = end + len_ref[b, m]
        lo = jnp.where(end <= first, end, lo)
        hi = jnp.where((end > last) & (end < hi), end, hi)
    return lo // LANE, (hi + LANE - 1) // LANE

def gauss_tile(drow):
    sub = lax.broadcasted_iota(jnp.int32, (SUB, LANE), 0).astype(F32) * KS
    base = drow - sub
    parts = []
    for c in range(KERN // SUB):
        t = base - (KS * SUB * c)
        parts.append(jnp.exp2(-(t * t)))
    return jnp.concatenate(parts, 0).astype(BF16)

def expand(rows, mask):
    n, w = rows.shape
    return (rows[:, None, :] * mask[None]).reshape(n * SUB, w).astype(BF16)

def collapse(wide, mask):
    n, w = wide.shape
    return jnp.sum(wide.reshape(n // SUB, SUB, w) * mask[None], axis=1)

def fwd_kernel(heads, mols, len_ref, coords_ref, q_ref, k_ref, v_ref, w_ref, o_ref, p_ref, dist, labs, labr, sc, qf):
    span, inner = q_ref.shape
    b = pl.program_id(0)
    scale = 1.0 / math.sqrt(inner // heads)
    setup_pairs(len_ref, b, coords_ref, dist, labs, labr, span, mols)
    mask = head_mask(heads, inner)
    qf[...] = q_ref[...].astype(F32)
    kb = k_ref[...]; vb = v_ref[...]; wb = w_ref[...]

    def chunk(ci, carry):
        sc[...] = jnp.full(sc.shape, -1e30, F32)
        def group(g, carry):
            i0 = pl.multiple_of(ci * CHUNK + g * SUB, SUB)
            lo, hi = tile_range(len_ref, b, i0, i0 + SUB - 1, span, mols)
            def tile(jt, carry):
                j0 = pl.multiple_of(jt * LANE, LANE)
                lab = labr[:, pl.ds(j0, LANE)]
                dblk = dist[pl.ds(i0, SUB), pl.ds(j0, LANE)]
                lblk = labs[pl.ds(i0, SUB), :]
                for r in range(SUB):
                    drow = jnp.broadcast_to(dblk[r:r + 1], (SUB, LANE))
                    li = jnp.broadcast_to(lblk[r:r + 1], (SUB, LANE))
                    bias = jnp.dot(wb, gauss_tile(drow), preferred_element_type=F32)
                    row0 = pl.multiple_of((g * SUB + r) * SUB, SUB)
                    sc[pl.ds(row0, SUB), pl.ds(j0, LANE)] = jnp.where(li == lab, bias, -1e30)
                return carry
            return lax.fori_loop(lo, hi, tile, carry)
        lax.fori_loop(0, CHUNK // SUB, group, 0)
        c0 = pl.multiple_of(ci * CHUNK, CHUNK)
        qt = expand(qf[pl.ds(c0, CHUNK), :], mask)
        s = lax.dot_general(qt, kb, NT, preferred_element_type=F32)
        bias = sc[...]
        s = s * scale + bias
        top = jnp.max(s, axis=-1, keepdims=True)
        e = jnp.exp(s - top)
        pr = (e / jnp.sum(e, axis=-1, keepdims=True)).astype(BF16)
        p_ref[pl.ds(pl.multiple_of(ci * CHUNK * SUB, CHUNK * SUB), CHUNK * SUB), :] = pr
        ow = jnp.dot(pr, vb, preferred_element_type=F32)
        o_ref[pl.ds(c0, CHUNK), :] = collapse(ow, mask).astype(BF16)
        return carry
    lax.fori_loop(0, span // CHUNK, chunk, 0)

def attention(qkv, coords, lengths, pair_low, heads):
    _, rows, inner = qkv.shape
    blocks, mols = lengths.shape
    span = rows // blocks
    w = jnp.pad(pair_low, ((0, SUB - heads), (0, 0)))
    part = lambda s: pl.BlockSpec((None, span, inner), lambda b, *_: (s, b, 0))
    return pl.pallas_call(
        functools.partial(fwd_kernel, heads, mols),
        out_shape=(jax.ShapeDtypeStruct((rows, inner), BF16), jax.ShapeDtypeStruct((rows * SUB, span), BF16)),
        grid_spec=pltpu.PrefetchScalarGridSpec(
            num_scalar_prefetch=1, grid=(blocks,),
            in_specs=[pl.BlockSpec((3, span), lambda b, *_: (0, b)), part(0), part(1), part(2),
                      pl.BlockSpec((SUB, KERN), lambda b, *_: (0, 0))],
            out_specs=[pl.BlockSpec((span, inner), lambda b, *_: (b, 0)),
                       pl.BlockSpec((span * SUB, span), lambda b, *_: (b, 0))],
            scratch_shapes=[pltpu.VMEM((span, span), F32), pltpu.VMEM((span, LANE), jnp.int32),
                            pltpu.VMEM((SUB, span), jnp.int32), pltpu.VMEM((CHUNK * SUB, span), F32),
                            pltpu.VMEM((span, inner), F32)]),
        name="attend",
    )(lengths, coords, qkv, qkv, qkv, w)

def bwd_kernel(heads, mols, len_ref, coords_ref, q_ref, k_ref, v_ref, do_ref, p_ref, dqkv_ref, pg_ref,
               dist, labs, labr, ds, qf, dof, dkt, dvt):
    span, inner = q_ref.shape
    b = pl.program_id(0)
    scale = 1.0 / math.sqrt(inner // heads)
    setup_pairs(len_ref, b, coords_ref, dist, labs, labr, span, mols)
    mask = head_mask(heads, inner)
    qf[...] = q_ref[...].astype(F32)
    dof[...] = do_ref[...].astype(F32)
    kb = k_ref[...]; vb = v_ref[...]
    dkt[...] = jnp.zeros_like(dkt); dvt[...] = jnp.zeros_like(dvt)
    @pl.when(b == 0)
    def _():
        pg_ref[...] = jnp.zeros_like(pg_ref)

    def chunk(ci, carry):
        c0 = pl.multiple_of(ci * CHUNK, CHUNK)
        r0 = pl.multiple_of(ci * CHUNK * SUB, CHUNK * SUB)
        qt = expand(qf[pl.ds(c0, CHUNK), :], mask)
        dot = expand(dof[pl.ds(c0, CHUNK), :], mask)
        pb = p_ref[pl.ds(r0, CHUNK * SUB), :]
        pf = pb.astype(F32)
        dp = lax.dot_general(dot, vb, NT, preferred_element_type=F32)
        rowdot = jnp.sum(pf * dp, axis=-1, keepdims=True)
        dsf = pf * (dp - rowdot)
        dsb = dsf.astype(BF16)
        ds[...] = dsf
        dqkv_ref[0, pl.ds(c0, CHUNK), :] = (collapse(jnp.dot(dsb, kb, preferred_element_type=F32), mask) * scale).astype(BF16)
        dkt[...] += lax.dot_general(qt, dsb, TN, preferred_element_type=F32)
        dvt[...] += lax.dot_general(dot, pb, TN, preferred_element_type=F32)

        def group(g, carry):
            i0 = pl.multiple_of(ci * CHUNK + g * SUB, SUB)
            lo, hi = tile_range(len_ref, b, i0, i0 + SUB - 1, span, mols)
            def tile(jt, acc):
                j0 = pl.multiple_of(jt * LANE, LANE)
                dblk = dist[pl.ds(i0, SUB), pl.ds(j0, LANE)]
                for r in range(SUB):
                    drow = jnp.broadcast_to(dblk[r:r + 1], (SUB, LANE))
                    row0 = pl.multiple_of((g * SUB + r) * SUB, SUB)
                    d = ds[pl.ds(row0, SUB), pl.ds(j0, LANE)].astype(BF16)
                    acc = acc + lax.dot_general(d, gauss_tile(drow), NT, preferred_element_type=F32)
                return acc
            return lax.fori_loop(lo, hi, tile, carry)
        return lax.fori_loop(0, CHUNK // SUB, group, carry)
    pg_ref[...] += lax.fori_loop(0, span // CHUNK, chunk, jnp.zeros((SUB, KERN), F32))
    dqkv_ref[1] = jnp.transpose(dkt[...] * scale).astype(BF16)
    dqkv_ref[2] = jnp.transpose(dvt[...]).astype(BF16)

def attention_back(qkv, grad_heads, probs, coords, lengths, heads):
    _, rows, inner = qkv.shape
    blocks, mols = lengths.shape
    span = rows // blocks
    part = lambda s: pl.BlockSpec((None, span, inner), lambda b, *_: (s, b, 0))
    return pl.pallas_call(
        functools.partial(bwd_kernel, heads, mols),
        out_shape=(jax.ShapeDtypeStruct((3, rows, inner), BF16), jax.ShapeDtypeStruct((SUB, KERN), F32)),
        grid_spec=pltpu.PrefetchScalarGridSpec(
            num_scalar_prefetch=1, grid=(blocks,),
            in_specs=[pl.BlockSpec((3, span), lambda b, *_: (0, b)), part(0), part(1), part(2),
                      pl.BlockSpec((span, inner), lambda b, *_: (b, 0)),
                      pl.BlockSpec((span * SUB, span), lambda b, *_: (b, 0))],
            out_specs=[pl.BlockSpec((3, span, inner), lambda b, *_: (0, b, 0)),
                       pl.BlockSpec((SUB, KERN), lambda b, *_: (0, 0))],
            scratch_shapes=[pltpu.VMEM((span, span), F32), pltpu.VMEM((span, LANE), jnp.int32),
                            pltpu.VMEM((SUB, span), jnp.int32), pltpu.VMEM((CHUNK * SUB, span), F32),
                            pltpu.VMEM((span, inner), F32), pltpu.VMEM((span, inner), F32),
                            pltpu.VMEM((inner, span), F32), pltpu.VMEM((inner, span), F32)]),
        name="attend_back",
    )(lengths, coords, qkv, qkv, qkv, grad_heads, probs)


MESH = pl.DeviceIdType.MESH
NN = (((1,), (0,)), ((), ()))
VM = pl.BlockSpec(memory_space=pltpu.VMEM)
HBM = pl.BlockSpec(memory_space=pl.ANY)
DMA = pltpu.SemaphoreType.DMA


def mm(a, b, dims=NN):
    return lax.dot_general(a, b, dims, preferred_element_type=F32)


def remote(src, dst, send, recv, axis, target):
    return pltpu.make_async_remote_copy(
        src_ref=src, dst_ref=dst, send_sem=send, recv_sem=recv,
        device_id={axis: target}, device_id_type=MESH)


def greet(sizes):
    barrier = pltpu.get_barrier_semaphore()
    total = 0
    for axis, size in sizes.items():
        me = lax.axis_index(axis)
        for k in range(1, size):
            pl.semaphore_signal(barrier, inc=1, device_id={axis: lax.rem(me + k, size)}, device_id_type=MESH)
        total += size - 1
    pl.semaphore_wait(barrier, total)


class Seat:
    def __init__(self, n):
        self.n, self.nx = n, n // 2
        self.me = lax.axis_index("mp")
        self.core = lax.rem(self.me, 2)
        self.x = self.me // 2
        self.sib = self.me + 1 - 2 * self.core

    def chip(self, k):
        return lax.rem(self.x + 1 + k, self.nx)

    def source(self, k):
        return lax.rem(self.x + self.nx - 1 - k, self.nx)


def scatter_scratch(n, rows, width):
    nx = n // 2
    buf = lambda m: pltpu.VMEM((m, rows, width), BF16)
    return [buf(nx), buf(nx), buf(max(nx - 1, 1)), buf(max(nx - 1, 1)), DMA((nx,)), DMA((nx,)),
            DMA((max(nx - 1, 1),)), DMA((max(nx - 1, 1),))]


class Scatter:
    def __init__(self, seat, scratch):
        self.seat = seat
        self.out1, self.in1, self.out2, self.in2, self.s1, self.r1, self.s2, self.r2 = scratch

    def first(self, k):
        return remote(self.out1.at[k], self.in1.at[k], self.s1.at[k], self.r1.at[k], "mp", self.seat.sib)

    def second(self, k):
        target = self.seat.chip(k) * 2 + self.seat.core
        return remote(self.out2.at[k], self.in2.at[k], self.s2.at[k], self.r2.at[k], "mp", target)

    def push(self, block):
        for k in range(self.seat.nx):
            self.out1[k] = block(self.seat.chip(k) * 2 + 1 - self.seat.core).astype(BF16)
            self.first(k).start()

    def pass_on(self, block):
        seat = self.seat
        parts = [block(seat.chip(k) * 2 + seat.core) for k in range(seat.nx)]
        for k in range(seat.nx):
            self.first(k).wait_recv()
            whole = parts[k] + self.in1[k].astype(F32)
            if k < seat.nx - 1:
                self.out2[k] = whole.astype(BF16)
                self.second(k).start()
        return whole

    def finish(self, whole):
        for k in range(self.seat.nx - 1):
            self.second(k).wait_recv()
            whole = whole + self.in2[k].astype(F32)
        return whole

    def drain(self):
        for k in range(self.seat.nx):
            self.first(k).wait_send()
        for k in range(self.seat.nx - 1):
            self.second(k).wait_send()


def gather_scratch(n):
    nx = n // 2
    return [DMA((max(nx - 1, 1),)), DMA((max(nx - 1, 1),)), DMA((nx,)), DMA((nx,))]


class Gather:
    def __init__(self, seat, rows, scratch):
        self.seat, self.rows = seat, rows
        self.sx, self.rx, self.sc, self.rc = scratch

    def across(self, k):
        r = self.rows.at[self.seat.me]
        return remote(r, r, self.sx.at[k], self.rx.at[k], "mp", self.seat.chip(k) * 2 + self.seat.core)

    def along(self, k):
        chip = self.seat.x if k == self.seat.nx - 1 else self.seat.source(k)
        r = self.rows.at[chip * 2 + self.seat.core]
        return remote(r, r, self.sc.at[k], self.rc.at[k], "mp", self.seat.sib)

    def start(self):
        for k in range(self.seat.nx - 1):
            self.across(k).start()
        self.along(self.seat.nx - 1).start()

    def forward(self):
        for k in range(self.seat.nx - 1):
            self.across(k).wait_recv()
            self.along(k).start()

    def finish(self):
        for k in range(self.seat.nx):
            self.along(k).wait_recv()

    def drain(self):
        for k in range(self.seat.nx - 1):
            self.across(k).wait_send()
        for k in range(self.seat.nx):
            self.along(k).wait_send()


def centre(rows):
    c = rows - jnp.mean(rows, axis=-1, keepdims=True)
    r = lax.rsqrt(jnp.mean(c * c, axis=-1, keepdims=True) + ln_eps)
    return c * r, r


def norm_back(rows, gain, e):
    vhat, r = centre(rows)
    ge = e * gain
    dv = r * (ge - jnp.mean(ge, axis=-1, keepdims=True) - vhat * jnp.mean(ge * vhat, axis=-1, keepdims=True))
    return dv, jnp.sum(e * vhat, axis=0, keepdims=True), jnp.sum(e, axis=0, keepdims=True)


def enter_kernel(n, x_ref, dy_ref, np_ref, w_hbm, h_ref, dyall_ref, qkv_ref, w32, wsem, *sems):
    seat = Seat(n)
    load = pltpu.make_async_copy(w_hbm, w32, wsem)
    load.start()
    greet({"mp": n})
    vhat, _ = centre(x_ref[...].astype(F32))
    h_ref[seat.me] = (vhat * np_ref[0:1] + np_ref[1:2]).astype(BF16)
    dyall_ref[seat.me] = dy_ref[...]
    gh = Gather(seat, h_ref, sems[:4])
    gd = Gather(seat, dyall_ref, sems[4:])
    gh.start()
    load.wait()
    gh.forward()
    gd.start()
    gh.finish()
    rows = h_ref.shape[1]
    for s in range(3):
        w = w32[s].astype(BF16)

        def block(b, carry):
            r0 = pl.multiple_of(b * rows, rows)
            qkv_ref[s, pl.ds(r0, rows), :] = mm(h_ref[b], w, NT).astype(BF16)
            return carry

        lax.fori_loop(0, n, block, 0)
    gd.forward()
    gd.finish()
    gh.drain()
    gd.drain()


def enter(n, x, dy, params, qkv_weight):
    rows, width = x.shape
    _, inner, _ = qkv_weight.shape
    return pl.pallas_call(
        functools.partial(enter_kernel, n),
        out_shape=(jax.ShapeDtypeStruct((n, rows, width), BF16), jax.ShapeDtypeStruct((n, rows, width), BF16),
                   jax.ShapeDtypeStruct((3, n * rows, inner), BF16)),
        in_specs=[VM, VM, VM, HBM], out_specs=[VM, VM, VM],
        scratch_shapes=[pltpu.VMEM(qkv_weight.shape, F32), DMA, *gather_scratch(n), *gather_scratch(n)],
        compiler_params=pltpu.CompilerParams(collective_id=0, has_side_effects=True),
        name="enter",
    )(x, dy, params, qkv_weight)


def middle_kernel(n, x_ref, dy_ref, dyall_ref, o_ref, np_ref, bias_ref, pw_hbm, iw_hbm, ow_hbm,
                  block_ref, mid_ref, do_ref, og_ref, ig_ref, pg_ref, bg_ref, small_ref,
                  pw32, iw32, ow32, pw, iw, ow, h2, da, act, dpre, dact, wsem, *rest):
    seat = Seat(n)
    rows, width = x_ref.shape
    loads = [pltpu.make_async_copy(a, b, wsem.at[i])
             for i, (a, b) in enumerate([(pw_hbm, pw32), (ow_hbm, ow32), (iw_hbm, iw32)])]
    for c in loads:
        c.start()
    scat = [Scatter(seat, rest[8 * i:8 * i + 8]) for i in range(3)]
    gath = [Gather(seat, r, rest[24 + 4 * i:28 + 4 * i]) for i, r in enumerate((h2, da))]
    greet({"mp": n})
    at = lambda b: pl.ds(pl.multiple_of(b * rows, rows), rows)

    loads[0].wait()
    pw[...] = pw32[...].astype(BF16)
    attn_block = lambda b: mm(o_ref[at(b), :], pw[...])
    scat[0].push(attn_block)
    loads[1].wait()
    ow[...] = ow32[...].astype(BF16)
    whole = scat[0].pass_on(attn_block)
    loads[2].wait()
    iw[...] = iw32[...].astype(BF16)

    def back_act(b, carry):
        dact[b] = mm(dyall_ref[b], ow[...], NT)
        return carry

    lax.fori_loop(0, n, back_act, 0)
    mid = x_ref[...].astype(F32) + scat[0].finish(whole)
    vhat, _ = centre(mid)
    h2[seat.me] = (vhat * np_ref[2:3] + np_ref[3:4]).astype(BF16)
    mid_ref[...] = mid
    gath[0].start()
    gath[0].forward()
    gath[0].finish()

    bg_ref[...] = jnp.zeros_like(bg_ref)
    bias = bias_ref[...].astype(BF16).astype(F32)

    def feed_block(b):
        pre = mm(h2[b], iw[...], NT) + bias
        phi = 0.5 + 0.5 * lax.erf(pre * math.sqrt(0.5))
        act[b] = (pre * phi).astype(BF16)
        slope = phi + pre * (jnp.exp(-0.5 * pre * pre) * (1.0 / math.sqrt(2.0 * math.pi)))
        d = (dact[b] * slope).astype(BF16)
        dpre[b] = d
        bg_ref[...] += jnp.sum(d.astype(F32), axis=0, keepdims=True)
        return mm(d, iw[...])

    scat[1].push(feed_block)
    whole = scat[1].pass_on(feed_block)
    out_block = lambda b: mm(act[b], ow[...])
    scat[2].push(out_block)
    dh2 = scat[1].finish(whole)
    dv, gain, shift = norm_back(mid_ref[...], np_ref[2:3], dh2)
    dy = dy_ref[...].astype(F32)
    dx1 = dy + dv
    da[seat.me] = dx1.astype(BF16)
    gath[1].start()
    small_ref[...] = jnp.concatenate(
        [gain, shift, jnp.sum(dy, axis=0, keepdims=True), jnp.zeros((5, width), F32)], 0)
    whole = scat[2].pass_on(out_block)
    gath[1].forward()

    hidden = iw.shape[0]
    step = LANE if hidden % LANE == 0 else hidden

    def grads(i, carry):
        c0 = pl.multiple_of(i * step, step)
        acc_o = jnp.zeros((step, width), F32)
        acc_i = jnp.zeros((step, width), F32)
        for b in range(n):
            acc_o += mm(act[b, :, pl.ds(c0, step)], dyall_ref[b], TN)
            acc_i += mm(dpre[b, :, pl.ds(c0, step)], h2[b], TN)
        og_ref[pl.ds(c0, step), :] = acc_o.astype(BF16)
        ig_ref[pl.ds(c0, step), :] = acc_i.astype(BF16)
        return carry

    lax.fori_loop(0, hidden // step, grads, 0)
    block_ref[...] = mid_ref[...] + scat[2].finish(whole) + np_ref[4:5]
    mid_ref[...] = dx1
    gath[1].finish()

    def heads_block(b, acc):
        do_ref[at(b), :] = mm(da[b], pw[...], NT).astype(BF16)
        return acc + mm(o_ref[at(b), :], da[b], TN)

    pg_ref[...] = lax.fori_loop(0, n, heads_block, jnp.zeros(pg_ref.shape, F32)).astype(BF16)
    for c in scat + gath:
        c.drain()


def middle(n, x, dy, dy_all, o, params, bias, proj_weight, in_weight, out_weight):
    rows, width = x.shape
    hidden = in_weight.shape[0]
    inner = proj_weight.shape[0]
    f = lambda *s: jax.ShapeDtypeStruct(s, F32)
    return pl.pallas_call(
        functools.partial(middle_kernel, n),
        out_shape=(f(rows, width), f(rows, width), jax.ShapeDtypeStruct((n * rows, inner), BF16),
                   *[jax.ShapeDtypeStruct((t, width), BF16) for t in (hidden, hidden, inner)], f(1, hidden), f(8, width)),
        in_specs=[VM] * 6 + [HBM] * 3, out_specs=[VM] * 8,
        scratch_shapes=[pltpu.VMEM((inner, width), F32), pltpu.VMEM((hidden, width), F32),
                        pltpu.VMEM((hidden, width), F32), pltpu.VMEM((inner, width), BF16),
                        pltpu.VMEM((hidden, width), BF16), pltpu.VMEM((hidden, width), BF16),
                        pltpu.VMEM((n, rows, width), BF16), pltpu.VMEM((n, rows, width), BF16),
                        pltpu.VMEM((n, rows, hidden), BF16), pltpu.VMEM((n, rows, hidden), BF16),
                        pltpu.VMEM((n, rows, hidden), F32), DMA((3,)),
                        *[s for _ in range(3) for s in scatter_scratch(n, rows, width)],
                        *gather_scratch(n), *gather_scratch(n)],
        compiler_params=pltpu.CompilerParams(collective_id=1, has_side_effects=True, vmem_limit_bytes=60 << 20),
        name="middle",
    )(x, dy, dy_all, o, params, bias, proj_weight, in_weight, out_weight)


class Grid:
    def __init__(self, ny, nz):
        self.ny, self.nz = ny, nz
        self.me = lax.axis_index("dp")
        self.z, self.y = self.me // ny, lax.rem(self.me, ny)

    def yto(self, k):
        return lax.rem(self.y + 1 + k, self.ny)

    def yfrom(self, k):
        return lax.rem(self.y + self.ny - 1 - k, self.ny)

    def zto(self, k):
        return lax.rem(self.z + 1 + k, self.nz)

    def zfrom(self, k):
        return lax.rem(self.z + self.nz - 1 - k, self.nz)


def sum_scratch(ny, nz, chunk, width):
    y, z = max(ny - 1, 1), max(nz - 1, 1)
    return [pltpu.VMEM((y, nz, chunk, width), BF16), pltpu.VMEM((z, chunk, width), BF16),
            pltpu.VMEM((z, chunk, width), BF16), pltpu.VMEM((chunk, width), F32),
            DMA((y,)), DMA((y,)), DMA((z,)), DMA((z,)), DMA((z,)), DMA((z,)), DMA((nz, y)), DMA((nz, y))]


SUMS = 12


class Sum:
    def __init__(self, grid, grad, result, scratch):
        self.grid, self.grad, self.result = grid, grad, result
        (self.ia, self.ob, self.ib, self.own, self.sa, self.ra, self.sb, self.rb,
         self.sz, self.rz, self.sy, self.ry) = scratch

    def copy_y(self, k):
        g = self.grid
        return remote(self.grad.at[g.yto(k)], self.ia.at[k], self.sa.at[k], self.ra.at[k], "dp",
                      g.z * g.ny + g.yto(k))

    def copy_z(self, k):
        g = self.grid
        return remote(self.ob.at[k], self.ib.at[k], self.sb.at[k], self.rb.at[k], "dp", g.zto(k) * g.ny + g.y)

    def back_z(self, k):
        g = self.grid
        r = self.result.at[g.y, g.z]
        return remote(r, r, self.sz.at[k], self.rz.at[k], "dp", g.zto(k) * g.ny + g.y)

    def back_y(self, k, j):
        g = self.grid
        r = self.result.at[g.y, g.z if k == g.nz - 1 else g.zfrom(k)]
        return remote(r, r, self.sy.at[k, j], self.ry.at[k, j], "dp", g.z * g.ny + g.yto(j))

    def push(self):
        for k in range(self.grid.ny - 1):
            self.copy_y(k).start()

    def pass_on(self):
        g = self.grid
        for k in range(g.ny - 1):
            self.copy_y(k).wait_recv()
        for k in range(g.nz):
            z = g.zto(k)
            whole = self.grad[g.y, z].astype(F32)
            for j in range(g.ny - 1):
                whole = whole + self.ia[j, z].astype(F32)
            if k < g.nz - 1:
                self.ob[k] = whole.astype(BF16)
                self.copy_z(k).start()
            else:
                self.own[...] = whole

    def finish(self):
        g = self.grid
        whole = self.own[...]
        for k in range(g.nz - 1):
            self.copy_z(k).wait_recv()
            whole = whole + self.ib[k].astype(F32)
        self.result[g.y, g.z] = whole.astype(BF16)
        for k in range(g.nz - 1):
            self.back_z(k).start()
        for k in range(g.ny - 1):
            self.back_y(g.nz - 1, k).start()
        return square(whole)

    def forward(self):
        g = self.grid
        for k in range(g.nz - 1):
            self.back_z(k).wait_recv()
            for j in range(g.ny - 1):
                self.back_y(k, j).start()

    def close(self):
        g = self.grid
        for k in range(g.nz):
            for j in range(g.ny - 1):
                self.back_y(k, j).wait_recv()
        for k in range(g.ny - 1):
            self.copy_y(k).wait_send()
        for k in range(g.nz - 1):
            self.copy_z(k).wait_send()
            self.back_z(k).wait_send()
        for k in range(g.nz):
            for j in range(g.ny - 1):
                self.back_y(k, j).wait_send()


class Share:
    def __init__(self, axis, slots, send, recv):
        self.axis, self.slots, self.send, self.recv = axis, slots, send, recv
        self.size = slots.shape[0]
        self.me = lax.axis_index(axis)

    def copy(self, k):
        r = self.slots.at[self.me]
        return remote(r, r, self.send.at[k], self.recv.at[k], self.axis, lax.rem(self.me + 1 + k, self.size))

    def start(self, value):
        self.slots[self.me] = value
        for k in range(self.size - 1):
            self.copy(k).start()

    def total(self):
        for k in range(self.size - 1):
            self.copy(k).wait_recv()
        out = self.slots[0]
        for i in range(1, self.size):
            out = out + self.slots[i]
        return out

    def drain(self):
        for k in range(self.size - 1):
            self.copy(k).wait_send()


def share_scratch(size, rows, width):
    return [pltpu.VMEM((size, rows, width), F32), DMA((max(size - 1, 1),)), DMA((max(size - 1, 1),))]


def square(v):
    return jnp.sum(jnp.sum(v * v, axis=1, keepdims=True), axis=0, keepdims=True)


def leave_kernel(n, ny, nz, x_ref, dx_ref, np_ref, dqkv_ref, h_ref, bg_ref, pair_ref, squares_ref,
                 mid_small_ref, w_hbm, gi_ref, sq_ref, small_ref, bias_ref, pairs_ref, norm_ref,
                 w32, w, qg, wsem, *rest):
    seat, grid = Seat(n), Grid(ny, nz)
    rows, width = x_ref.shape
    inner = w.shape[1]
    load = pltpu.make_async_copy(w_hbm, w32, wsem)
    load.start()
    scat = Scatter(seat, rest[:8])
    sums = [Sum(grid, qg.at[s], sq_ref.at[s], rest[8 + SUMS * s:8 + SUMS * (s + 1)]) for s in range(3)]
    rest = rest[8 + 3 * SUMS:]
    shares = [Share(a, *rest[3 * i:3 * i + 3]) for i, a in enumerate(("mp", "dp", "dp", "dp", "mp", "dp"))]
    small_mp, small_dp, bias_dp, pair_dp, sq_mp, sq_dp = shares
    greet({"mp": n, "dp": ny * nz})
    at = lambda b: pl.ds(pl.multiple_of(b * rows, rows), rows)

    load.wait()
    w[...] = w32[...].astype(BF16)

    def first_block(b):
        return sum(mm(dqkv_ref[s, at(b), :], w[s]) for s in range(3))

    scat.push(first_block)
    for s in range(3):
        acc = jnp.zeros((inner, width), F32)
        for b in range(n):
            acc = acc + mm(dqkv_ref[s, at(b), :], h_ref[b], TN)
        qg[s] = acc.reshape(qg.shape[1:]).astype(BF16)
        sums[s].push()
        if s == 0:
            whole = scat.pass_on(first_block)
            bias_dp.start(jnp.broadcast_to(bg_ref[...], bias_dp.slots.shape[1:]))
            pair_dp.start(pair_ref[...])
    dh1 = scat.finish(whole)
    dv, gain, shift = norm_back(x_ref[...].astype(F32), np_ref[0:1], dh1)
    gi_ref[...] = dx_ref[...] + dv
    small_mp.start(jnp.concatenate([gain, shift, mid_small_ref[0:6]], 0))
    sums[0].pass_on()
    small_dp.start(small_mp.total())
    sums[1].pass_on()
    squares = squares_ref[0:1] + sums[0].finish()
    sums[2].pass_on()
    squares = squares + sums[1].finish()
    squares = squares + sums[2].finish()
    sums[0].forward()
    bias = bias_dp.total()
    bias_ref[...] = bias
    pairs = pair_dp.total()
    pairs_ref[...] = pairs
    row = lax.broadcasted_iota(jnp.int32, (8, LANE), 0)
    local = square(bias[0:1]) + square(pairs)
    sq_mp.start(jnp.where(row == 0, squares, jnp.where(row == 1, local, 0.0)))
    small = small_dp.total()
    small_ref[...] = small
    sums[1].forward()
    sq_dp.start(sq_mp.total())
    sums[2].forward()
    norm_ref[...] = sq_dp.total()[0:1] + sq_dp.slots[0, 1:2] + square(small)
    for s in sums:
        s.close()
    scat.drain()
    for s in shares:
        s.drain()


def leave(n, ny, nz, x, dx, params, dqkv, h, bias_grad, pair_grad, squares, small, qkv_weight):
    rows, width = x.shape
    inner = qkv_weight.shape[1]
    ndp = ny * nz
    hidden = bias_grad.shape[1]
    chunks = (3, ny, nz, inner // ndp, width)
    f = lambda *s: jax.ShapeDtypeStruct(s, F32)
    return pl.pallas_call(
        functools.partial(leave_kernel, n, ny, nz),
        out_shape=(f(rows, width), jax.ShapeDtypeStruct(chunks, BF16), f(8, width), f(8, hidden), f(8, LANE), f(1, LANE)),
        in_specs=[VM] * 9 + [HBM], out_specs=[VM] * 6,
        scratch_shapes=[pltpu.VMEM(qkv_weight.shape, F32), pltpu.VMEM(qkv_weight.shape, BF16),
                        pltpu.VMEM(chunks, BF16), DMA, *scatter_scratch(n, rows, width),
                        *[s for _ in range(3) for s in sum_scratch(ny, nz, inner // ndp, width)],
                        *share_scratch(n, 8, width), *share_scratch(ndp, 8, width), *share_scratch(ndp, 8, hidden),
                        *share_scratch(ndp, 8, LANE), *share_scratch(n, 8, LANE), *share_scratch(ndp, 8, LANE)],
        compiler_params=pltpu.CompilerParams(collective_id=2, has_side_effects=True, vmem_limit_bytes=60 << 20),
        name="leave",
    )(x, dx, params, dqkv, h, bias_grad, pair_grad, squares, small, qkv_weight)


def back_kernel(heads, ny, nz, coords_ref, qkv_ref, do_ref, p_ref, og_ref, ig_ref, pg_ref,
                dqkv_ref, pair_ref, so_ref, si_ref, sp_ref, squares_ref,
                dist, ds, qf, dof, dkt, dvt, *rest):
    span, inner = do_ref.shape
    scale = 1.0 / math.sqrt(inner // heads)
    grid = Grid(ny, nz)
    parts = og_ref.shape[0]
    pieces = [(g.at[i], r.at[i]) for g, r in ((og_ref, so_ref), (ig_ref, si_ref)) for i in range(parts)]
    pieces.append((pg_ref, sp_ref))
    sums = [Sum(grid, g, r, rest[SUMS * i:SUMS * (i + 1)]) for i, (g, r) in enumerate(pieces)]
    greet({"dp": ny * nz})
    for s in sums:
        s.push()
    squares_ref[...] = jnp.zeros_like(squares_ref)

    def finish(s):
        squares_ref[...] += s.finish()

    jobs = {}
    for i, s in enumerate(sums):
        jobs.setdefault(PASS_AT[i], []).append(s.pass_on)
        jobs.setdefault(FINISH_AT[i], []).append(functools.partial(finish, s))
        jobs.setdefault(FORWARD_AT[i], []).append(s.forward)
    last = span // CHUNK

    pair_distances(coords_ref, dist, span)
    mask = head_mask(heads, inner)
    qf[...] = qkv_ref[0].astype(F32)
    dof[...] = do_ref[...].astype(F32)
    dkt[...] = jnp.zeros_like(dkt)
    dvt[...] = jnp.zeros_like(dvt)

    def chunk(ci, acc):
        for when in sorted(jobs):
            if when < last:
                @pl.when(ci == when)
                def _():
                    for job in jobs[when]:
                        job()
        c0 = pl.multiple_of(ci * CHUNK, CHUNK)
        r0 = pl.multiple_of(ci * CHUNK * SUB, CHUNK * SUB)
        qt = expand(qf[pl.ds(c0, CHUNK), :], mask)
        dot = expand(dof[pl.ds(c0, CHUNK), :], mask)
        pb = p_ref[pl.ds(r0, CHUNK * SUB), :]
        pf = pb.astype(F32)
        dp = mm(dot, qkv_ref[2], NT)
        rowdot = jnp.sum(pf * dp, axis=-1, keepdims=True)
        dsf = pf * (dp - rowdot)
        dsb = dsf.astype(BF16)
        ds[...] = dsf
        dqkv_ref[0, pl.ds(c0, CHUNK), :] = (collapse(mm(dsb, qkv_ref[1]), mask) * scale).astype(BF16)
        dkt[...] += mm(qt, dsb, TN)
        dvt[...] += mm(dot, pb, TN)

        def group(g, acc):
            i0 = pl.multiple_of(ci * CHUNK + g * SUB, SUB)

            def tile(jt, acc):
                j0 = pl.multiple_of(jt * LANE, LANE)
                dblk = dist[pl.ds(i0, SUB), pl.ds(j0, LANE)]
                left, right = [], []
                for r in range(SUB):
                    row0 = pl.multiple_of((g * SUB + r) * SUB, SUB)
                    left.append(ds[pl.ds(row0, SUB), pl.ds(j0, LANE)].astype(BF16))
                    right.append(gauss_tile(jnp.broadcast_to(dblk[r:r + 1], (SUB, LANE))))
                return acc + mm(jnp.concatenate(left, 1), jnp.concatenate(right, 1), NT)

            return lax.fori_loop(0, span // LANE, tile, acc)

        return lax.fori_loop(0, CHUNK // SUB, group, acc)

    pair_ref[...] = lax.fori_loop(0, last, chunk, jnp.zeros((SUB, KERN), F32))
    dqkv_ref[1] = jnp.transpose(dkt[...] * scale).astype(BF16)
    dqkv_ref[2] = jnp.transpose(dvt[...]).astype(BF16)
    for when in sorted(jobs):
        if when >= last:
            for job in jobs[when]:
                job()
    for s in sums:
        s.close()


PASS_AT = (2, 4, 6, 8, 9)
FINISH_AT = (5, 7, 10, 12, 14)
FORWARD_AT = (8, 10, 13, 16, 16)


def pair_distances(coords_ref, dist, span):
    pts = coords_ref[...]
    cols = jnp.transpose(jnp.concatenate([pts, jnp.zeros((5, span), F32)], 0))
    acc = None
    for a in range(3):
        d = cols[:, a:a + 1] - pts[a:a + 1, :]
        acc = d * d if acc is None else acc + d * d
    dist[...] = jnp.sqrt(acc) * UNIT


def attention_back_sums(qkv, do, probs, coords, heads, ny, nz, og, ig, pg):
    _, span, inner = qkv.shape
    width = og.shape[1]
    ndp, parts = ny * nz, 2
    cut = lambda g, p: g.reshape(p, ny, nz, g.shape[0] // (p * ndp), width)
    og, ig, pg = cut(og, parts), cut(ig, parts), cut(pg, 1)[0]
    shapes = [og.shape[1:]] * parts + [ig.shape[1:]] * parts + [pg.shape]
    out = lambda a: jax.ShapeDtypeStruct(a.shape, BF16)
    return pl.pallas_call(
        functools.partial(back_kernel, heads, ny, nz),
        out_shape=(jax.ShapeDtypeStruct((3, span, inner), BF16), jax.ShapeDtypeStruct((SUB, KERN), F32),
                   out(og), out(ig), out(pg), jax.ShapeDtypeStruct((SUB, LANE), F32)),
        in_specs=[VM] * 7, out_specs=[VM] * 6,
        scratch_shapes=[pltpu.VMEM((span, span), F32), pltpu.VMEM((CHUNK * SUB, span), F32),
                        pltpu.VMEM((span, inner), F32), pltpu.VMEM((span, inner), F32),
                        pltpu.VMEM((inner, span), F32), pltpu.VMEM((inner, span), F32),
                        *[s for shape in shapes for s in sum_scratch(ny, nz, shape[2], width)]],
        compiler_params=pltpu.CompilerParams(collective_id=3, has_side_effects=True, vmem_limit_bytes=60 << 20),
        name="attend_back_sums",
    )(coords, qkv, do, probs, og, ig, pg)


def leave_plain(n, x, dx, params, dqkv, h, grads, bias_grad, pair_grad, small, qkv_weight):
    part = sum(mm(dqkv[s], qkv_weight[s].astype(BF16)) for s in range(3))
    dh1 = lax.psum_scatter(part, "mp", scatter_dimension=0, tiled=True)
    dv, gain, shift = norm_back(x.astype(F32), params[0:1], dh1)
    hh = h.reshape(-1, h.shape[-1])
    qg = jnp.concatenate([mm(dqkv[s], hh, TN) for s in range(3)], 0)
    og, ig, pg, qg, bias, pair = lax.psum((*[g.astype(F32) for g in grads], qg, bias_grad, pair_grad), "dp")
    small = lax.psum(jnp.concatenate([gain, shift, small[0:6]], 0), ("dp", "mp"))
    local = sum(square(v) for v in (og, ig, pg, qg, bias, pair))
    total = lax.psum(local, "mp") + square(small)
    return dx + dv, og, ig, pg, qg, small, bias, pair, total


def adam_step(weight, grad, first, second, clip, fix_one, fix_two, rate, decay):
    scaled = grad * clip
    first_new = beta_one * first + (1.0 - beta_one) * scaled
    second_new = beta_two * second + (1.0 - beta_two) * scaled * scaled
    ratio = first_new / fix_one / (jnp.sqrt(second_new / fix_two) + adam_eps)
    return (weight - rate * (ratio + decay * weight), first_new, second_new)


def per_device(n, ndp, block_in, coords, lengths, cotangent, step_count, *state):
    weights, firsts, seconds = state[:7], state[7:14], state[14:]
    qkv_weight, proj_weight, pair_weight, in_weight, in_bias, out_weight, params = weights
    heads = pair_weight.shape[0]
    pair_low = pair_weight.astype(BF16)
    h, dy_all, qkv = enter(n, block_in, cotangent, params, qkv_weight)
    o, probs = attention(qkv, coords, lengths, pair_low, heads)
    block_out, dx, do, og, ig, pg, bg, small = middle(
        n, block_in, cotangent, dy_all, o, params, in_bias.reshape(1, -1), proj_weight, in_weight, out_weight)
    ny = n // 2 if ndp % (n // 2) == 0 else 1
    nz = ndp // ny
    inner = proj_weight.shape[0]
    if lengths.shape[0] == 1 and inner % (8 * ndp) == 0 and og.shape[0] % (32 * ndp) == 0:
        dqkv, pair_grad, og, ig, pg, squares = attention_back_sums(qkv, do, probs, coords, heads, ny, nz, og, ig, pg)
        grad_input, qg, small, bias, pair, total = leave(
            n, ny, nz, block_in, dx, params, dqkv, h, bg, pair_grad, squares, small, qkv_weight)
    else:
        dqkv, pair_grad = attention_back(qkv, do, probs, coords, lengths, heads)
        grad_input, og, ig, pg, qg, small, bias, pair, total = leave_plain(
            n, block_in, dx, params, dqkv, h, (og, ig, pg), bg, pair_grad, small, qkv_weight)
    grad_norm = jnp.sqrt(total[0, 0])
    clip = clip_level / jnp.maximum(grad_norm, clip_level)
    count = step_count[0].astype(F32)
    fix_one = 1.0 - jnp.power(beta_one, count)
    fix_two = 1.0 - jnp.power(beta_two, count)
    grads = (qg.reshape(qkv_weight.shape), pg.reshape(proj_weight.shape), pair[:heads], ig.reshape(in_weight.shape),
             bias[0], og.reshape(out_weight.shape), small[:5])
    rates = (0.9, 2.5, 7.5, 0.9, 7.5, 0.45, 3.0)
    decays = (0.01, 0.01, 0.01, 0.01, 0.0, 0.01, 0.0)
    outs = [block_out, grad_input, grad_norm.reshape(1)]
    for w, g, m, u, rate, decay in zip(weights, grads, firsts, seconds, rates, decays):
        outs.extend(adam_step(w, g.astype(F32), m, u, clip, fix_one, fix_two, rate, decay))
    return tuple(outs)


def solution(mesh):
    rows, mp = P(("dp", "mp"), None), P("mp", None)
    stacked = P(None, "mp", None)
    params = (stacked, mp, mp, mp, P("mp"), mp, P())
    in_specs = (rows, P(None, "dp"), P("dp", None), rows, P(), *params, *params, *params)
    out_specs = (rows, rows, P(), *[s for s in params for _ in range(3)])
    return jax.shard_map(
        functools.partial(per_device, mesh.shape["mp"], mesh.shape["dp"]),
        mesh=mesh, in_specs=in_specs, out_specs=out_specs, check_vma=False)
```

```python
import functools
import math

import jax
import jax.numpy as jnp
from jax import lax
from jax.experimental import pallas as pl
from jax.experimental.pallas import tpu as pltpu
from jax.sharding import PartitionSpec as P

ln_eps = 1e-05
beta_one = 0.9
beta_two = 0.999
adam_eps = 1e-08
clip_level = 1.0

F32, BF16 = jnp.float32, jnp.bfloat16
MESH = pl.DeviceIdType.MESH
NN = (((1,), (0,)), ((), ()))
NT = (((1,), (1,)), ((), ()))
TN = (((0,), (0,)), ((), ()))
VM = pl.BlockSpec(memory_space=pltpu.VMEM)
HBM = pl.BlockSpec(memory_space=pl.ANY)
DMA = pltpu.SemaphoreType.DMA
KERN = 128
LANE = 128
SUB = 8
TALL = 32
KS = math.sqrt(0.5 * math.log2(math.e))
UNIT = KS / (12.8 / KERN)


def pair_distances(coords_ref, dist, span):
    pts = coords_ref[...]
    cols = jnp.transpose(jnp.concatenate([pts, jnp.zeros((5, span), F32)], 0))
    acc = None
    for a in range(3):
        d = cols[:, a:a + 1] - pts[a:a + 1, :]
        acc = d * d if acc is None else acc + d * d
    dist[...] = jnp.sqrt(acc) * UNIT


def pair_labels(len_ref, b, labs, labr, span, mols):
    lanes = lax.broadcasted_iota(jnp.int32, (SUB, span), 1)
    lc = jnp.zeros((SUB, span), F32)
    end = jnp.int32(0)
    for m in range(mols):
        end = end + len_ref[b, m]
        lc = lc + (lanes >= end).astype(F32)
    labr[...] = lc
    labs[...] = jnp.broadcast_to(jnp.transpose(lc)[:, 0:1], (span, LANE))


def tile_range(len_ref, b, first, last, span, mols):
    lo = jnp.int32(0)
    hi = jnp.int32(span)
    end = jnp.int32(0)
    for m in range(mols):
        end = end + len_ref[b, m]
        lo = jnp.where(end <= first, end, lo)
        hi = jnp.where((end > last) & (end < hi), end, hi)
    return lo // LANE, (hi + LANE - 1) // LANE


def row_of(block, r):
    return jnp.broadcast_to(block[r:r + 1], (SUB, LANE))


def gauss_tile(drow):
    sub = lax.broadcasted_iota(jnp.int32, (SUB, LANE), 0).astype(F32) * KS
    base = drow - sub
    parts = []
    for c in range(KERN // SUB):
        t = base - (KS * SUB * c)
        parts.append(jnp.exp2(-(t * t)))
    return jnp.concatenate(parts, 0).astype(BF16)


def wide(ref, rows):
    return jnp.concatenate([ref[t, rows, :] for t in range(ref.shape[0])], 1)


def fwd_kernel(heads, mols, len_ref, coords_ref, qkv_ref, w_ref, o_ref, p_ref, dist, labs, labr, sc):
    hd, span = qkv_ref.shape[2:]
    b = pl.program_id(0)
    scale = 1.0 / math.sqrt(hd)
    pair_distances(coords_ref, dist, span)
    pair_labels(len_ref, b, labs, labr, span, mols)
    wb = w_ref[...]
    step = LANE

    def fill(i, carry):
        r0 = pl.multiple_of(i * step, step)
        sc[:, pl.ds(r0, step), :] = jnp.full((span // LANE, step, LANE), -1e30, F32)
        return carry

    lax.fori_loop(0, SUB * span // step, fill, 0)

    def group(g, carry):
        i0 = pl.multiple_of(g * TALL, TALL)
        lo, hi = tile_range(len_ref, b, i0, i0 + TALL - 1, span, mols)

        def tile(jt, carry):
            j0 = pl.multiple_of(jt * LANE, LANE)
            lab = labr[:, pl.ds(j0, LANE)]
            dblk = dist[pl.ds(i0, TALL), pl.ds(j0, LANE)]
            lblk = labs[pl.ds(i0, TALL), :]
            for r in range(0, TALL, 2):
                bias = mm(wb, jnp.concatenate([gauss_tile(row_of(dblk, r)), gauss_tile(row_of(dblk, r + 1))], 1))
                for k in range(2):
                    sc[jt, pl.ds(i0 + r + k, SUB, span), :] = jnp.where(
                        row_of(lblk, r + k) == lab, bias[:, k * LANE:(k + 1) * LANE], -1e30)
            return carry

        return lax.fori_loop(lo, hi, tile, carry)

    lax.fori_loop(0, span // TALL, group, 0)

    def head(h, carry):
        for c in range(span // step):
            cols = pl.ds(c * step, step)
            rows = pl.ds(pl.multiple_of(h * span + c * step, step), step)
            s = mm(qkv_ref[0, h, :, cols], qkv_ref[1, h], TN) * scale + wide(sc, rows)
            e = jnp.exp(s - jnp.max(s, axis=-1, keepdims=True))
            p = (e * (1.0 / jnp.sum(e, axis=-1, keepdims=True))).astype(BF16)
            p_ref[rows, :] = p
            o_ref[h, :, cols] = mm(qkv_ref[2, h], p, NT).astype(BF16)
        return carry

    lax.fori_loop(0, heads, head, 0)


def attention(qkv, coords, lengths, pair_low):
    _, heads, hd, rows = qkv.shape
    blocks, mols = lengths.shape
    span = rows // blocks
    w = jnp.pad(pair_low, ((0, SUB - heads), (0, 0)))
    return pl.pallas_call(
        functools.partial(fwd_kernel, heads, mols),
        out_shape=(jax.ShapeDtypeStruct((heads, hd, rows), BF16),
                   jax.ShapeDtypeStruct((blocks * heads * span, span), BF16)),
        grid_spec=pltpu.PrefetchScalarGridSpec(
            num_scalar_prefetch=1, grid=(blocks,),
            in_specs=[pl.BlockSpec((3, span), lambda b, *_: (0, b)),
                      pl.BlockSpec((3, heads, hd, span), lambda b, *_: (0, 0, 0, b)),
                      pl.BlockSpec((SUB, KERN), lambda b, *_: (0, 0))],
            out_specs=[pl.BlockSpec((heads, hd, span), lambda b, *_: (0, 0, b)),
                       pl.BlockSpec((heads * span, span), lambda b, *_: (b, 0))],
            scratch_shapes=[pltpu.VMEM((span, span), F32), pltpu.VMEM((span, LANE), F32),
                            pltpu.VMEM((SUB, span), F32), pltpu.VMEM((span // LANE, SUB * span, LANE), F32)]),
        compiler_params=pltpu.CompilerParams(vmem_limit_bytes=60 << 20),
        name="attend",
    )(lengths, coords, qkv, w)


def back_pairs(heads, coords_ref, qkv_ref, do_ref, p_ref, dqkv_ref, dist, ds, beside):
    hd, span = do_ref.shape[1:]
    scale = 1.0 / math.sqrt(hd)
    step = LANE
    pair_distances(coords_ref, dist, span)
    if heads < SUB:
        ds[...] = jnp.zeros_like(ds)

    def head(h, carry):
        beside(h, 0, heads)
        dk = jnp.zeros((hd, span), F32)
        dv = jnp.zeros((hd, span), F32)
        for c in range(span // step):
            cols = pl.ds(c * step, step)
            rows = pl.ds(pl.multiple_of(h * span + c * step, step), step)
            pb = p_ref[rows, :]
            p = pb.astype(F32)
            dp = mm(do_ref[h, :, cols], qkv_ref[2, h], TN)
            d = p * (dp - jnp.sum(p * dp, axis=-1, keepdims=True))
            for t in range(span // LANE):
                ds[t, rows, :] = d[:, t * LANE:(t + 1) * LANE]
            low = d.astype(BF16)
            dqkv_ref[0, h, :, cols] = (mm(qkv_ref[1, h], low, NT) * scale).astype(BF16)
            dk = dk + mm(qkv_ref[0, h, :, cols], low)
            dv = dv + mm(do_ref[h, :, cols], pb)
        dqkv_ref[1, h] = (dk * scale).astype(BF16)
        dqkv_ref[2, h] = dv.astype(BF16)
        return carry

    lax.fori_loop(0, heads, head, 0)

    def group(g, acc):
        beside(heads + g, heads, heads + span // SUB)
        i0 = pl.multiple_of(g * SUB, SUB)

        left, right = [], []
        for jt in range(span // LANE):
            dblk = dist[pl.ds(i0, SUB), jt * LANE:(jt + 1) * LANE]
            for r in range(SUB // 2):
                pair = (r, r + SUB // 2)
                left.append(jnp.concatenate([ds[jt, pl.ds(i0 + k, SUB, span), :] for k in pair], 0).astype(BF16))
                right.append(jnp.concatenate([gauss_tile(row_of(dblk, k)) for k in pair], 0))
        return acc + mm(jnp.concatenate(left, 1), jnp.concatenate(right, 1), NT)

    acc = lax.fori_loop(0, span // SUB, group, jnp.zeros((2 * SUB, 2 * KERN), F32))
    return acc[:SUB, :KERN] + acc[SUB:, KERN:]


def bwd_kernel(heads, coords_ref, qkv_ref, do_ref, p_ref, dqkv_ref, pair_ref, dist, ds):
    @pl.when(pl.program_id(0) == 0)
    def _():
        pair_ref[...] = jnp.zeros_like(pair_ref)

    pair_ref[...] += back_pairs(heads, coords_ref, qkv_ref, do_ref, p_ref, dqkv_ref, dist, ds, lambda *_: None)


def attention_back(qkv, do, probs, coords):
    _, heads, hd, rows = qkv.shape
    span = probs.shape[1]
    wide = pl.BlockSpec((3, heads, hd, span), lambda b: (0, 0, 0, b))
    return pl.pallas_call(
        functools.partial(bwd_kernel, heads),
        out_shape=(jax.ShapeDtypeStruct(qkv.shape, BF16), jax.ShapeDtypeStruct((SUB, KERN), F32)),
        grid=(rows // span,),
        in_specs=[pl.BlockSpec((3, span), lambda b: (0, b)), wide,
                  pl.BlockSpec((heads, hd, span), lambda b: (0, 0, b)),
                  pl.BlockSpec((heads * span, span), lambda b: (b, 0))],
        out_specs=[wide, pl.BlockSpec((SUB, KERN), lambda b: (0, 0))],
        scratch_shapes=[pltpu.VMEM((span, span), F32), pltpu.VMEM((span // LANE, SUB * span, LANE), F32)],
        compiler_params=pltpu.CompilerParams(vmem_limit_bytes=60 << 20),
        name="attend_back",
    )(coords, qkv, do, probs)


def mm(a, b, dims=NN):
    return lax.dot_general(a, b, dims, preferred_element_type=F32)


def remote(src, dst, send, recv, axis, target):
    return pltpu.make_async_remote_copy(
        src_ref=src, dst_ref=dst, send_sem=send, recv_sem=recv,
        device_id={axis: target}, device_id_type=MESH)


def greet(sizes):
    barrier = pltpu.get_barrier_semaphore()
    total = 0
    for axis, size in sizes.items():
        me = lax.axis_index(axis)
        for k in range(1, size):
            pl.semaphore_signal(barrier, inc=1, device_id={axis: lax.rem(me + k, size)}, device_id_type=MESH)
        total += size - 1
    pl.semaphore_wait(barrier, total)


class Seat:
    def __init__(self, n):
        self.n, self.nx = n, n // 2
        self.me = lax.axis_index("mp")
        self.core = lax.rem(self.me, 2)
        self.x = self.me // 2
        self.sib = self.me + 1 - 2 * self.core

    def chip(self, k):
        return lax.rem(self.x + 1 + k, self.nx)

    def source(self, k):
        return lax.rem(self.x + self.nx - 1 - k, self.nx)


def scatter_scratch(n, rows, width):
    nx = n // 2
    buf = lambda m: pltpu.VMEM((m, rows, width), BF16)
    return [buf(nx), buf(nx), buf(max(nx - 1, 1)), buf(max(nx - 1, 1)), DMA((nx,)), DMA((nx,)),
            DMA((max(nx - 1, 1),)), DMA((max(nx - 1, 1),))]


class Scatter:
    def __init__(self, seat, scratch):
        self.seat = seat
        self.out1, self.in1, self.out2, self.in2, self.s1, self.r1, self.s2, self.r2 = scratch

    def first(self, k):
        return remote(self.out1.at[k], self.in1.at[k], self.s1.at[k], self.r1.at[k], "mp", self.seat.sib)

    def second(self, k):
        target = self.seat.chip(k) * 2 + self.seat.core
        return remote(self.out2.at[k], self.in2.at[k], self.s2.at[k], self.r2.at[k], "mp", target)

    def push(self, block):
        for k in range(self.seat.nx):
            self.out1[k] = block(self.seat.chip(k) * 2 + 1 - self.seat.core).astype(BF16)
            self.first(k).start()

    def pass_on(self, block):
        seat = self.seat
        parts = [block(seat.chip(k) * 2 + seat.core) for k in range(seat.nx)]
        for k in range(seat.nx):
            self.first(k).wait_recv()
            whole = parts[k] + self.in1[k].astype(F32)
            if k < seat.nx - 1:
                self.out2[k] = whole.astype(BF16)
                self.second(k).start()
        return whole

    def finish(self, whole):
        for k in range(self.seat.nx - 1):
            self.second(k).wait_recv()
            whole = whole + self.in2[k].astype(F32)
        return whole

    def drain(self):
        for k in range(self.seat.nx):
            self.first(k).wait_send()
        for k in range(self.seat.nx - 1):
            self.second(k).wait_send()


def gather_scratch(n):
    nx = n // 2
    return [DMA((max(nx - 1, 1),)), DMA((max(nx - 1, 1),)), DMA((nx,)), DMA((nx,))]


class Gather:
    def __init__(self, seat, rows, scratch):
        self.seat, self.rows = seat, rows
        self.sx, self.rx, self.sc, self.rc = scratch

    def across(self, k):
        r = self.rows.at[self.seat.me]
        return remote(r, r, self.sx.at[k], self.rx.at[k], "mp", self.seat.chip(k) * 2 + self.seat.core)

    def along(self, k):
        chip = self.seat.x if k == self.seat.nx - 1 else self.seat.source(k)
        r = self.rows.at[chip * 2 + self.seat.core]
        return remote(r, r, self.sc.at[k], self.rc.at[k], "mp", self.seat.sib)

    def start(self):
        for k in range(self.seat.nx - 1):
            self.across(k).start()
        self.along(self.seat.nx - 1).start()

    def forward(self):
        for k in range(self.seat.nx - 1):
            self.across(k).wait_recv()
            self.along(k).start()

    def finish(self):
        for k in range(self.seat.nx):
            self.along(k).wait_recv()

    def drain(self):
        for k in range(self.seat.nx - 1):
            self.across(k).wait_send()
        for k in range(self.seat.nx):
            self.along(k).wait_send()


def centre(rows):
    c = rows - jnp.mean(rows, axis=-1, keepdims=True)
    r = lax.rsqrt(jnp.mean(c * c, axis=-1, keepdims=True) + ln_eps)
    return c * r, r


def norm_back(rows, gain, e):
    vhat, r = centre(rows)
    ge = e * gain
    dv = r * (ge - jnp.mean(ge, axis=-1, keepdims=True) - vhat * jnp.mean(ge * vhat, axis=-1, keepdims=True))
    return dv, jnp.sum(e * vhat, axis=0, keepdims=True), jnp.sum(e, axis=0, keepdims=True)


def enter_kernel(n, x_ref, dy_ref, np_ref, w_hbm, h_ref, dyall_ref, qkv_ref, w32, wsem, *sems):
    seat = Seat(n)
    load = pltpu.make_async_copy(w_hbm, w32, wsem)
    load.start()
    greet({"mp": n})
    vhat, _ = centre(x_ref[...].astype(F32))
    h_ref[seat.me] = (vhat * np_ref[0:1] + np_ref[1:2]).astype(BF16)
    dyall_ref[seat.me] = dy_ref[...]
    gh = Gather(seat, h_ref, sems[:4])
    gd = Gather(seat, dyall_ref, sems[4:])
    gh.start()
    load.wait()
    gh.forward()
    gd.start()
    gh.finish()
    rows = h_ref.shape[1]
    for s in range(3):
        w = w32[s].astype(BF16)

        def block(b, carry):
            out = mm(w, h_ref[b], NT)
            qkv_ref[s, :, :, pl.ds(pl.multiple_of(b * rows, rows), rows)] = out.reshape(
                *qkv_ref.shape[1:3], rows).astype(BF16)
            return carry

        lax.fori_loop(0, n, block, 0)
    gd.forward()
    gd.finish()
    gh.drain()
    gd.drain()


def enter(n, heads, x, dy, params, qkv_weight):
    rows, width = x.shape
    _, inner, _ = qkv_weight.shape
    return pl.pallas_call(
        functools.partial(enter_kernel, n),
        out_shape=(jax.ShapeDtypeStruct((n, rows, width), BF16), jax.ShapeDtypeStruct((n, rows, width), BF16),
                   jax.ShapeDtypeStruct((3, heads, inner // heads, n * rows), BF16)),
        in_specs=[VM, VM, VM, HBM], out_specs=[VM, VM, VM],
        scratch_shapes=[pltpu.VMEM(qkv_weight.shape, F32), DMA, *gather_scratch(n), *gather_scratch(n)],
        compiler_params=pltpu.CompilerParams(collective_id=0, has_side_effects=True),
        name="enter",
    )(x, dy, params, qkv_weight)


def middle_kernel(n, x_ref, dy_ref, dyall_ref, o_ref, np_ref, bias_ref, pw_hbm, iw_hbm, ow_hbm,
                  block_ref, mid_ref, do_ref, og_ref, ig_ref, pg_ref, bg_ref, small_ref,
                  pw32, iw32, ow32, pw, iw, ow, h2, da, act, dpre, dact, wsem, *rest):
    seat = Seat(n)
    rows, width = x_ref.shape
    loads = [pltpu.make_async_copy(a, b, wsem.at[i])
             for i, (a, b) in enumerate([(pw_hbm, pw32), (ow_hbm, ow32), (iw_hbm, iw32)])]
    for c in loads:
        c.start()
    scat = [Scatter(seat, rest[8 * i:8 * i + 8]) for i in range(3)]
    gath = [Gather(seat, r, rest[24 + 4 * i:28 + 4 * i]) for i, r in enumerate((h2, da))]
    greet({"mp": n})
    at = lambda b: pl.ds(pl.multiple_of(b * rows, rows), rows)

    loads[0].wait()
    pw[...] = pw32[...].astype(BF16)
    attn_block = lambda b: mm(o_ref[:, at(b)], pw[...], TN)
    scat[0].push(attn_block)
    loads[1].wait()
    ow[...] = ow32[...].astype(BF16)
    whole = scat[0].pass_on(attn_block)
    loads[2].wait()
    iw[...] = iw32[...].astype(BF16)

    def back_act(b, carry):
        dact[b] = mm(dyall_ref[b], ow[...], NT)
        return carry

    lax.fori_loop(0, n, back_act, 0)
    mid = x_ref[...].astype(F32) + scat[0].finish(whole)
    vhat, _ = centre(mid)
    h2[seat.me] = (vhat * np_ref[2:3] + np_ref[3:4]).astype(BF16)
    mid_ref[...] = mid
    gath[0].start()
    gath[0].forward()
    gath[0].finish()

    bg_ref[...] = jnp.zeros_like(bg_ref)
    bias = bias_ref[...].astype(BF16).astype(F32)

    def feed_block(b):
        pre = mm(h2[b], iw[...], NT) + bias
        phi = 0.5 + 0.5 * lax.erf(pre * math.sqrt(0.5))
        act[b] = (pre * phi).astype(BF16)
        slope = phi + pre * (jnp.exp(-0.5 * pre * pre) * (1.0 / math.sqrt(2.0 * math.pi)))
        d = (dact[b] * slope).astype(BF16)
        dpre[b] = d
        bg_ref[...] += jnp.sum(d.astype(F32), axis=0, keepdims=True)
        return mm(d, iw[...])

    scat[1].push(feed_block)
    whole = scat[1].pass_on(feed_block)
    out_block = lambda b: mm(act[b], ow[...])
    scat[2].push(out_block)
    dh2 = scat[1].finish(whole)
    dv, gain, shift = norm_back(mid_ref[...], np_ref[2:3], dh2)
    dy = dy_ref[...].astype(F32)
    dx1 = dy + dv
    da[seat.me] = dx1.astype(BF16)
    gath[1].start()
    small_ref[...] = jnp.concatenate(
        [gain, shift, jnp.sum(dy, axis=0, keepdims=True), jnp.zeros((5, width), F32)], 0)
    whole = scat[2].pass_on(out_block)
    gath[1].forward()

    hidden = iw.shape[0]
    step = LANE if hidden % LANE == 0 else hidden

    def grads(i, carry):
        c0 = pl.multiple_of(i * step, step)
        acc_o = jnp.zeros((step, width), F32)
        acc_i = jnp.zeros((step, width), F32)
        for b in range(n):
            acc_o += mm(act[b, :, pl.ds(c0, step)], dyall_ref[b], TN)
            acc_i += mm(dpre[b, :, pl.ds(c0, step)], h2[b], TN)
        og_ref[pl.ds(c0, step), :] = acc_o.astype(BF16)
        ig_ref[pl.ds(c0, step), :] = acc_i.astype(BF16)
        return carry

    lax.fori_loop(0, hidden // step, grads, 0)
    block_ref[...] = mid_ref[...] + scat[2].finish(whole) + np_ref[4:5]
    mid_ref[...] = dx1
    gath[1].finish()

    def heads_block(b, acc):
        out = mm(pw[...], da[b], NT)
        do_ref[:, :, at(b)] = out.reshape(*do_ref.shape[:2], rows).astype(BF16)
        return acc + mm(o_ref[:, at(b)], da[b])

    pg_ref[...] = lax.fori_loop(0, n, heads_block, jnp.zeros(pg_ref.shape, F32)).astype(BF16)
    for c in scat + gath:
        c.drain()


def middle(n, x, dy, dy_all, o, params, bias, proj_weight, in_weight, out_weight):
    rows, width = x.shape
    hidden = in_weight.shape[0]
    inner = proj_weight.shape[0]
    heads, hd, _ = o.shape
    f = lambda *s: jax.ShapeDtypeStruct(s, F32)
    return pl.pallas_call(
        functools.partial(middle_kernel, n),
        out_shape=(f(rows, width), f(rows, width), jax.ShapeDtypeStruct(o.shape, BF16),
                   *[jax.ShapeDtypeStruct((t, width), BF16) for t in (hidden, hidden, inner)], f(1, hidden), f(8, width)),
        in_specs=[VM] * 6 + [HBM] * 3, out_specs=[VM] * 8,
        scratch_shapes=[pltpu.VMEM((inner, width), F32), pltpu.VMEM((hidden, width), F32),
                        pltpu.VMEM((hidden, width), F32), pltpu.VMEM((inner, width), BF16),
                        pltpu.VMEM((hidden, width), BF16), pltpu.VMEM((hidden, width), BF16),
                        pltpu.VMEM((n, rows, width), BF16), pltpu.VMEM((n, rows, width), BF16),
                        pltpu.VMEM((n, rows, hidden), BF16), pltpu.VMEM((n, rows, hidden), BF16),
                        pltpu.VMEM((n, rows, hidden), F32), DMA((3,)),
                        *[s for _ in range(3) for s in scatter_scratch(n, rows, width)],
                        *gather_scratch(n), *gather_scratch(n)],
        compiler_params=pltpu.CompilerParams(collective_id=1, has_side_effects=True, vmem_limit_bytes=60 << 20),
        name="middle",
    )(x, dy, dy_all, o.reshape(inner, -1), params, bias, proj_weight, in_weight, out_weight)


class Grid:
    def __init__(self, ny, nz):
        self.ny, self.nz = ny, nz
        self.me = lax.axis_index("dp")
        self.z, self.y = self.me // ny, lax.rem(self.me, ny)

    def yto(self, k):
        return lax.rem(self.y + 1 + k, self.ny)

    def yfrom(self, k):
        return lax.rem(self.y + self.ny - 1 - k, self.ny)

    def zto(self, k):
        return lax.rem(self.z + 1 + k, self.nz)

    def zfrom(self, k):
        return lax.rem(self.z + self.nz - 1 - k, self.nz)


def sum_scratch(ny, nz, chunk, width):
    y, z = max(ny - 1, 1), max(nz - 1, 1)
    return [pltpu.VMEM((y, nz, chunk, width), BF16), pltpu.VMEM((z, chunk, width), BF16),
            pltpu.VMEM((z, chunk, width), BF16), DMA((y,)), DMA((y,)), DMA((z,)), DMA((z,))]


class Sum:
    count = 7

    def __init__(self, grid, grad, own, scratch):
        self.grid, self.grad, self.own = grid, grad, own
        self.ia, self.ob, self.ib, self.sa, self.ra, self.sb, self.rb = scratch

    def copy_y(self, k):
        g = self.grid
        return remote(self.grad.at[g.yto(k)], self.ia.at[k], self.sa.at[k], self.ra.at[k], "dp",
                      g.z * g.ny + g.yto(k))

    def copy_z(self, k):
        g = self.grid
        return remote(self.ob.at[k], self.ib.at[k], self.sb.at[k], self.rb.at[k], "dp", g.zto(k) * g.ny + g.y)

    def push(self):
        for k in range(self.grid.ny - 1):
            self.copy_y(k).start()

    def pass_on(self):
        g = self.grid
        for k in range(g.ny - 1):
            self.copy_y(k).wait_recv()
        for k in range(g.nz):
            z = g.zto(k)
            whole = self.grad[g.y, z].astype(F32)
            for j in range(g.ny - 1):
                whole = whole + self.ia[j, z].astype(F32)
            if k < g.nz - 1:
                self.ob[k] = whole.astype(BF16)
                self.copy_z(k).start()
            else:
                self.own[...] = whole

    def collect(self):
        whole = self.own[...]
        for k in range(self.grid.nz - 1):
            self.copy_z(k).wait_recv()
            whole = whole + self.ib[k].astype(F32)
        self.own[...] = whole

    def drain(self):
        g = self.grid
        for k in range(g.ny - 1):
            self.copy_y(k).wait_send()
        for k in range(g.nz - 1):
            self.copy_z(k).wait_send()


def spread_scratch(ny, nz):
    y, z = max(ny - 1, 1), max(nz - 1, 1)
    return [DMA((z,)), DMA((z,)), DMA((nz, y)), DMA((nz, y))]


class Spread:
    count = 4

    def __init__(self, grid, own, result, scratch):
        self.grid, self.own, self.result = grid, own, result
        self.sz, self.rz, self.sy, self.ry = scratch

    def back_z(self, k):
        g = self.grid
        r = self.result.at[g.y, g.z]
        return remote(r, r, self.sz.at[k], self.rz.at[k], "dp", g.zto(k) * g.ny + g.y)

    def back_y(self, k, j):
        g = self.grid
        r = self.result.at[g.y, g.z if k == g.nz - 1 else g.zfrom(k)]
        return remote(r, r, self.sy.at[k, j], self.ry.at[k, j], "dp", g.z * g.ny + g.yto(j))

    def start(self):
        g = self.grid
        whole = self.own[...]
        self.result[g.y, g.z] = whole.astype(BF16)
        for k in range(g.nz - 1):
            self.back_z(k).start()
        for k in range(g.ny - 1):
            self.back_y(g.nz - 1, k).start()
        return square(whole)

    def forward(self):
        g = self.grid
        for k in range(g.nz - 1):
            self.back_z(k).wait_recv()
            for j in range(g.ny - 1):
                self.back_y(k, j).start()

    def close(self):
        g = self.grid
        for k in range(g.nz):
            for j in range(g.ny - 1):
                self.back_y(k, j).wait_recv()
        for k in range(g.nz - 1):
            self.back_z(k).wait_send()
        for k in range(g.nz):
            for j in range(g.ny - 1):
                self.back_y(k, j).wait_send()


def take(rest, cls, count):
    size = cls.count
    return [rest[size * i:size * (i + 1)] for i in range(count)], rest[size * count:]


class Share:
    def __init__(self, axis, slots, send, recv):
        self.axis, self.slots, self.send, self.recv = axis, slots, send, recv
        self.size = slots.shape[0]
        self.me = lax.axis_index(axis)

    def copy(self, k):
        r = self.slots.at[self.me]
        return remote(r, r, self.send.at[k], self.recv.at[k], self.axis, lax.rem(self.me + 1 + k, self.size))

    def start(self, value):
        self.slots[self.me] = value
        for k in range(self.size - 1):
            self.copy(k).start()

    def total(self):
        for k in range(self.size - 1):
            self.copy(k).wait_recv()
        out = self.slots[0]
        for i in range(1, self.size):
            out = out + self.slots[i]
        return out

    def drain(self):
        for k in range(self.size - 1):
            self.copy(k).wait_send()


def share_scratch(size, rows, width):
    return [pltpu.VMEM((size, rows, width), F32), DMA((max(size - 1, 1),)), DMA((max(size - 1, 1),))]


def square(v):
    return jnp.sum(jnp.sum(v * v, axis=1, keepdims=True), axis=0, keepdims=True)


def leave_kernel(n, ny, nz, late, x_ref, dx_ref, np_ref, dqkv_ref, h_ref, bg_ref, pair_ref, squares_ref,
                 mid_small_ref, *rest):
    owns, (w_hbm, gi_ref), rest = rest[:late], rest[late:late + 2], rest[late + 2:]
    results, rest = rest[:late], rest[late:]
    (sq_ref, small_ref, bias_ref, pairs_ref, norm_ref, w32, w, qg, qown, wsem), rest = rest[:10], rest[10:]
    seat, grid = Seat(n), Grid(ny, nz)
    rows, width = x_ref.shape
    inner = w.shape[1]
    load = pltpu.make_async_copy(w_hbm, w32, wsem)
    load.start()
    scat, rest = Scatter(seat, rest[:8]), rest[8:]
    parts, rest = take(rest, Sum, 3)
    sums = [Sum(grid, qg.at[s], qown.at[s], p) for s, p in enumerate(parts)]
    parts, rest = take(rest, Spread, 3 + late)
    spreads = [Spread(grid, s.own, sq_ref.at[i], p) for i, (s, p) in enumerate(zip(sums, parts))]
    olds = [Spread(grid, o, r, p) for o, r, p in zip(owns, results, parts[3:])]
    shares = [Share(a, *rest[3 * i:3 * i + 3]) for i, a in enumerate(("mp", "dp", "dp", "dp", "mp", "dp"))]
    small_mp, small_dp, bias_dp, pair_dp, sq_mp, sq_dp = shares
    greet({"mp": n, "dp": ny * nz})
    at = lambda b: pl.ds(pl.multiple_of(b * rows, rows), rows)

    squares = squares_ref[0:1]
    for s in olds:
        squares = squares + s.start()
    load.wait()
    w[...] = w32[...].astype(BF16)

    def first_block(b):
        return sum(mm(dqkv_ref[s, :, at(b)], w[s], TN) for s in range(3))

    scat.push(first_block)
    for s in range(3):
        acc = jnp.zeros((inner, width), F32)
        for b in range(n):
            acc = acc + mm(dqkv_ref[s, :, at(b)], h_ref[b])
        qg[s] = acc.reshape(qg.shape[1:]).astype(BF16)
        sums[s].push()
        if s == 0:
            whole = scat.pass_on(first_block)
            bias_dp.start(jnp.broadcast_to(bg_ref[...], bias_dp.slots.shape[1:]))
            pair_dp.start(pair_ref[...])
    for s in olds:
        s.forward()
    dh1 = scat.finish(whole)
    dv, gain, shift = norm_back(x_ref[...].astype(F32), np_ref[0:1], dh1)
    gi_ref[...] = dx_ref[...] + dv
    small_mp.start(jnp.concatenate([gain, shift, mid_small_ref[0:6]], 0))
    sums[0].pass_on()
    small_dp.start(small_mp.total())
    sums[1].pass_on()
    sums[0].collect()
    squares = squares + spreads[0].start()
    sums[2].pass_on()
    for s in (1, 2):
        sums[s].collect()
        squares = squares + spreads[s].start()
    spreads[0].forward()
    bias = bias_dp.total()
    bias_ref[...] = bias
    pairs = pair_dp.total()
    pairs_ref[...] = pairs
    row = lax.broadcasted_iota(jnp.int32, (8, LANE), 0)
    local = square(bias[0:1]) + square(pairs)
    sq_mp.start(jnp.where(row == 0, squares, jnp.where(row == 1, local, 0.0)))
    small = small_dp.total()
    small_ref[...] = small
    spreads[1].forward()
    sq_dp.start(sq_mp.total())
    spreads[2].forward()
    norm_ref[...] = sq_dp.total()[0:1] + sq_dp.slots[0, 1:2] + square(small)
    for s in olds + spreads:
        s.close()
    for s in [scat] + sums + shares:
        s.drain()


def leave(n, ny, nz, x, dx, params, dqkv, h, bias_grad, pair_grad, squares, small, owns, qkv_weight):
    rows, width = x.shape
    inner = qkv_weight.shape[1]
    ndp = ny * nz
    hidden = bias_grad.shape[1]
    chunks = (3, ny, nz, inner // ndp, width)
    f = lambda *s: jax.ShapeDtypeStruct(s, F32)
    late = len(owns)
    return pl.pallas_call(
        functools.partial(leave_kernel, n, ny, nz, late),
        out_shape=(f(rows, width), *[jax.ShapeDtypeStruct((ny, nz, *o.shape), BF16) for o in owns],
                   jax.ShapeDtypeStruct(chunks, BF16), f(8, width), f(8, hidden), f(8, LANE), f(1, LANE)),
        in_specs=[VM] * (9 + late) + [HBM], out_specs=[VM] * (6 + late),
        scratch_shapes=[pltpu.VMEM(qkv_weight.shape, F32), pltpu.VMEM(qkv_weight.shape, BF16),
                        pltpu.VMEM(chunks, BF16), pltpu.VMEM((3, inner // ndp, width), F32), DMA,
                        *scatter_scratch(n, rows, width),
                        *[s for _ in range(3) for s in sum_scratch(ny, nz, inner // ndp, width)],
                        *[s for _ in range(3 + late) for s in spread_scratch(ny, nz)],
                        *share_scratch(n, 8, width), *share_scratch(ndp, 8, width), *share_scratch(ndp, 8, hidden),
                        *share_scratch(ndp, 8, LANE), *share_scratch(n, 8, LANE), *share_scratch(ndp, 8, LANE)],
        compiler_params=pltpu.CompilerParams(collective_id=2, has_side_effects=True, vmem_limit_bytes=60 << 20),
        name="leave",
    )(x, dx, params, dqkv, h, bias_grad, pair_grad, squares, small, *owns, qkv_weight)


def leave_plain(n, x, dx, params, dqkv, h, grads, bias_grad, pair_grad, small, qkv_weight):
    part = sum(mm(dqkv[s], qkv_weight[s].astype(BF16), TN) for s in range(3))
    dh1 = lax.psum_scatter(part, "mp", scatter_dimension=0, tiled=True)
    dv, gain, shift = norm_back(x.astype(F32), params[0:1], dh1)
    hh = h.reshape(-1, h.shape[-1])
    qg = jnp.concatenate([mm(dqkv[s], hh) for s in range(3)], 0)
    og, ig, pg, qg, bias, pair = lax.psum((*[g.astype(F32) for g in grads], qg, bias_grad, pair_grad), "dp")
    small = lax.psum(jnp.concatenate([gain, shift, small[0:6]], 0), ("dp", "mp"))
    local = sum(square(v) for v in (og, ig, pg, qg, bias, pair))
    total = lax.psum(local, "mp") + square(small)
    return dx + dv, og, ig, pg, qg, small, bias, pair, total


PASS_AT = (4, 10, 24, 38, 45)
COLLECT_AT = (15, 30, 44, 58, 72)
FORWARD_AT = (40, 55)
EARLY = 2


def back_kernel(heads, ny, nz, parts, coords_ref, qkv_ref, do_ref, p_ref, og_ref, ig_ref, pg_ref,
                dqkv_ref, pair_ref, squares_ref, *rest):
    owns, rest = rest[:2 * parts + 1 - EARLY], rest[2 * parts + 1 - EARLY:]
    results, (dist, ds, early), rest = rest[:EARLY], rest[EARLY:EARLY + 3], rest[EARLY + 3:]
    hd, span = do_ref.shape[1:]
    grid = Grid(ny, nz)
    pieces = [g.at[i] for g in (og_ref, ig_ref) for i in range(parts)] + [pg_ref]
    places = [early.at[i] for i in range(EARLY)] + list(owns)
    scratch, rest = take(rest, Sum, len(pieces))
    sums = [Sum(grid, *a) for a in zip(pieces, places, scratch)]
    scratch, rest = take(rest, Spread, EARLY)
    spreads = [Spread(grid, *a) for a in zip(places, results, scratch)]
    greet({"dp": ny * nz})
    for s in sums:
        s.push()
    squares_ref[...] = jnp.zeros_like(squares_ref)

    def collect(i):
        sums[i].collect()
        if i < EARLY:
            squares_ref[...] += spreads[i].start()

    jobs = {}
    for i, s in enumerate(sums):
        jobs.setdefault(PASS_AT[i], []).append(s.pass_on)
        jobs.setdefault(COLLECT_AT[i], []).append(functools.partial(collect, i))
    for i, s in enumerate(spreads):
        jobs.setdefault(FORWARD_AT[i], []).append(s.forward)
    last = heads + span // SUB

    def beside(step, first, end):
        for when in sorted(jobs):
            if first <= when < end:
                @pl.when(step == when)
                def _():
                    for job in jobs[when]:
                        job()

    pair_ref[...] = back_pairs(heads, coords_ref, qkv_ref, do_ref, p_ref, dqkv_ref, dist, ds, beside)
    for when in sorted(jobs):
        if when >= last:
            for job in jobs[when]:
                job()
    for s in spreads:
        s.close()
    for s in sums:
        s.drain()


def attention_back_sums(qkv, do, probs, coords, ny, nz, og, ig, pg):
    _, heads, hd, span = qkv.shape
    width = og.shape[1]
    ndp, parts = ny * nz, 2
    cut = lambda g, p: g.reshape(p, ny, nz, g.shape[0] // (p * ndp), width)
    og, ig, pg = cut(og, parts), cut(ig, parts), cut(pg, 1)[0]
    shapes = [og.shape[1:]] * parts + [ig.shape[1:]] * parts + [pg.shape]
    f = lambda *s: jax.ShapeDtypeStruct(s, F32)
    return pl.pallas_call(
        functools.partial(back_kernel, heads, ny, nz, parts),
        out_shape=(jax.ShapeDtypeStruct(qkv.shape, BF16), f(SUB, KERN), f(SUB, LANE),
                   *[f(*s[2:]) for s in shapes[EARLY:]], *[jax.ShapeDtypeStruct(s, BF16) for s in shapes[:EARLY]]),
        in_specs=[VM] * 7, out_specs=[VM] * (3 + len(shapes)),
        scratch_shapes=[pltpu.VMEM((span, span), F32), pltpu.VMEM((span // LANE, SUB * span, LANE), F32),
                        pltpu.VMEM((EARLY, *shapes[0][2:]), F32),
                        *[s for shape in shapes for s in sum_scratch(ny, nz, shape[2], width)],
                        *[s for _ in range(EARLY) for s in spread_scratch(ny, nz)]],
        compiler_params=pltpu.CompilerParams(collective_id=3, has_side_effects=True, vmem_limit_bytes=60 << 20),
        name="attend_back_sums",
    )(coords, qkv, do, probs, og, ig, pg)


def adam_step(weight, grad, first, second, clip, fix_one, fix_two, rate, decay):
    scaled = grad * clip
    first_new = beta_one * first + (1.0 - beta_one) * scaled
    second_new = beta_two * second + (1.0 - beta_two) * scaled * scaled
    ratio = first_new / fix_one / (jnp.sqrt(second_new / fix_two) + adam_eps)
    return (weight - rate * (ratio + decay * weight), first_new, second_new)


def per_device(n, ndp, block_in, coords, lengths, cotangent, step_count, *state):
    weights, firsts, seconds = state[:7], state[7:14], state[14:]
    qkv_weight, proj_weight, pair_weight, in_weight, in_bias, out_weight, params = weights
    heads = pair_weight.shape[0]
    pair_low = pair_weight.astype(BF16)
    h, dy_all, qkv = enter(n, heads, block_in, cotangent, params, qkv_weight)
    o, probs = attention(qkv, coords, lengths, pair_low)
    block_out, dx, do, og, ig, pg, bg, small = middle(
        n, block_in, cotangent, dy_all, o, params, in_bias.reshape(1, -1), proj_weight, in_weight, out_weight)
    ny = n // 2 if ndp % (n // 2) == 0 else 1
    nz = ndp // ny
    inner = proj_weight.shape[0]
    if lengths.shape[0] == 1 and inner % (8 * ndp) == 0 and og.shape[0] % (32 * ndp) == 0:
        dqkv, pair_grad, squares, *parts = attention_back_sums(qkv, do, probs, coords, ny, nz, og, ig, pg)
        owns, done = parts[:-EARLY], parts[-EARLY:]
        grad_input, *sums, qg, small, bias, pair, total = leave(
            n, ny, nz, block_in, dx, params, dqkv.reshape(3, inner, -1), h, bg, pair_grad, squares, small, owns, qkv_weight)
        *pieces, pg = *done, *sums
        og, ig = pieces[:len(pieces) // 2], pieces[len(pieces) // 2:]
        og, ig = [jnp.concatenate([v.reshape(-1, v.shape[-1]) for v in g], 0) for g in (og, ig)]
    else:
        dqkv, pair_grad = attention_back(qkv, do, probs, coords)
        grad_input, og, ig, pg, qg, small, bias, pair, total = leave_plain(
            n, block_in, dx, params, dqkv.reshape(3, inner, -1), h, (og, ig, pg), bg, pair_grad, small, qkv_weight)
    grad_norm = jnp.sqrt(total[0, 0])
    clip = clip_level / jnp.maximum(grad_norm, clip_level)
    count = step_count[0].astype(F32)
    fix_one = 1.0 - jnp.power(beta_one, count)
    fix_two = 1.0 - jnp.power(beta_two, count)
    grads = (qg.reshape(qkv_weight.shape), pg.reshape(proj_weight.shape), pair[:heads], ig.reshape(in_weight.shape),
             bias[0], og.reshape(out_weight.shape), small[:5])
    rates = (0.9, 2.5, 7.5, 0.9, 7.5, 0.45, 3.0)
    decays = (0.01, 0.01, 0.01, 0.01, 0.0, 0.01, 0.0)
    outs = [block_out, grad_input, grad_norm.reshape(1)]
    for w, g, m, u, rate, decay in zip(weights, grads, firsts, seconds, rates, decays):
        outs.extend(adam_step(w, g.astype(F32), m, u, clip, fix_one, fix_two, rate, decay))
    return tuple(outs)


def solution(mesh):
    rows, mp = P(("dp", "mp"), None), P("mp", None)
    stacked = P(None, "mp", None)
    params = (stacked, mp, mp, mp, P("mp"), mp, P())
    in_specs = (rows, P(None, "dp"), P("dp", None), rows, P(), *params, *params, *params)
    out_specs = (rows, rows, P(), *[s for s in params for _ in range(3)])
    return jax.shard_map(
        functools.partial(per_device, mesh.shape["mp"], mesh.shape["dp"]),
        mesh=mesh, in_specs=in_specs, out_specs=out_specs, check_vma=False)
```

```python
import functools
import math

import jax
import jax.numpy as jnp
from jax import lax
from jax.experimental import pallas as pl
from jax.experimental.pallas import tpu as pltpu
from jax.sharding import PartitionSpec as P

ln_eps = 1e-05
beta_one = 0.9
beta_two = 0.999
adam_eps = 1e-08
clip_level = 1.0

F32, BF16 = jnp.float32, jnp.bfloat16
MESH = pl.DeviceIdType.MESH
NN = (((1,), (0,)), ((), ()))
NT = (((1,), (1,)), ((), ()))
TN = (((0,), (0,)), ((), ()))
VM = pl.BlockSpec(memory_space=pltpu.VMEM)
HBM = pl.BlockSpec(memory_space=pl.ANY)
DMA = pltpu.SemaphoreType.DMA
KERN = 128
LANE = 128
SUB = 8
TALL = 32
ATTEND_MIB = 20
KS = math.sqrt(0.5 * math.log2(math.e))
UNIT = KS / (12.8 / KERN)


def pair_distances(coords_ref, dist, span):
    pts = coords_ref[...]
    cols = jnp.transpose(jnp.concatenate([pts, jnp.zeros((5, span), F32)], 0))
    acc = None
    for a in range(3):
        d = cols[:, a:a + 1] - pts[a:a + 1, :]
        acc = d * d if acc is None else acc + d * d
    dist[...] = jnp.sqrt(acc) * UNIT


def pair_labels(len_ref, b, labs, labr, span, mols):
    lanes = lax.broadcasted_iota(jnp.int32, (SUB, span), 1)
    lc = jnp.zeros((SUB, span), F32)
    end = jnp.int32(0)
    for m in range(mols):
        end = end + len_ref[b, m]
        lc = lc + (lanes >= end).astype(F32)
    labr[...] = lc
    labs[...] = jnp.broadcast_to(jnp.transpose(lc)[:, 0:1], (span, LANE))


def tile_range(len_ref, b, first, last, span, mols):
    lo = jnp.int32(0)
    hi = jnp.int32(span)
    end = jnp.int32(0)
    for m in range(mols):
        end = end + len_ref[b, m]
        lo = jnp.where(end <= first, end, lo)
        hi = jnp.where((end > last) & (end < hi), end, hi)
    return lo // LANE, (hi + LANE - 1) // LANE


def row_of(block, r):
    return jnp.broadcast_to(block[r:r + 1], (SUB, LANE))


def gauss_tile(drow):
    sub = lax.broadcasted_iota(jnp.int32, (SUB, LANE), 0).astype(F32) * KS
    base = drow - sub
    parts = []
    for c in range(KERN // SUB):
        t = base - (KS * SUB * c)
        parts.append(jnp.exp2(-(t * t)))
    return jnp.concatenate(parts, 0).astype(BF16)


def wide(ref, rows):
    return jnp.concatenate([ref[t, rows, :] for t in range(ref.shape[0])], 1)


def fwd_kernel(heads, mols, len_ref, coords_ref, qkv_ref, w_ref, o_ref, p_ref, dist, labs, labr, sc):
    hd, span = qkv_ref.shape[2:]
    b = pl.program_id(0)
    scale = 1.0 / math.sqrt(hd)
    pair_distances(coords_ref, dist, span)
    pair_labels(len_ref, b, labs, labr, span, mols)
    wb = w_ref[...]
    step = LANE

    def fill(i, carry):
        r0 = pl.multiple_of(i * step, step)
        sc[:, pl.ds(r0, step), :] = jnp.full((span // LANE, step, LANE), -1e30, F32)
        return carry

    lax.fori_loop(0, SUB * span // step, fill, 0)

    def group(g, carry):
        i0 = pl.multiple_of(g * TALL, TALL)
        lo, hi = tile_range(len_ref, b, i0, i0 + TALL - 1, span, mols)

        def tile(jt, carry):
            j0 = pl.multiple_of(jt * LANE, LANE)
            lab = labr[:, pl.ds(j0, LANE)]
            dblk = dist[pl.ds(i0, TALL), pl.ds(j0, LANE)]
            lblk = labs[pl.ds(i0, TALL), :]
            for r in range(0, TALL, 2):
                bias = mm(wb, jnp.concatenate([gauss_tile(row_of(dblk, r)), gauss_tile(row_of(dblk, r + 1))], 1))
                for k in range(2):
                    sc[jt, pl.ds(i0 + r + k, SUB, span), :] = jnp.where(
                        row_of(lblk, r + k) == lab, bias[:, k * LANE:(k + 1) * LANE], -1e30)
            return carry

        return lax.fori_loop(lo, hi, tile, carry)

    lax.fori_loop(0, span // TALL, group, 0)

    def head(h, carry):
        for c in range(span // step):
            cols = pl.ds(c * step, step)
            rows = pl.ds(pl.multiple_of(h * span + c * step, step), step)
            s = mm(qkv_ref[0, h, :, cols], qkv_ref[1, h], TN) * scale + wide(sc, rows)
            e = jnp.exp(s - jnp.max(s, axis=-1, keepdims=True))
            p = (e * (1.0 / jnp.sum(e, axis=-1, keepdims=True))).astype(BF16)
            p_ref[rows, :] = p
            o_ref[h, :, cols] = mm(qkv_ref[2, h], p, NT).astype(BF16)
        return carry

    lax.fori_loop(0, heads, head, 0)


def attention(qkv, coords, lengths, pair_low):
    _, heads, hd, rows = qkv.shape
    blocks, mols = lengths.shape
    span = rows // blocks
    w = jnp.pad(pair_low, ((0, SUB - heads), (0, 0)))
    return pl.pallas_call(
        functools.partial(fwd_kernel, heads, mols),
        out_shape=(jax.ShapeDtypeStruct((heads, hd, rows), BF16),
                   jax.ShapeDtypeStruct((blocks * heads * span, span), BF16)),
        grid_spec=pltpu.PrefetchScalarGridSpec(
            num_scalar_prefetch=1, grid=(blocks,),
            in_specs=[pl.BlockSpec((3, span), lambda b, *_: (0, b)),
                      pl.BlockSpec((3, heads, hd, span), lambda b, *_: (0, 0, 0, b)),
                      pl.BlockSpec((SUB, KERN), lambda b, *_: (0, 0))],
            out_specs=[pl.BlockSpec((heads, hd, span), lambda b, *_: (0, 0, b)),
                       pl.BlockSpec((heads * span, span), lambda b, *_: (b, 0))],
            scratch_shapes=[pltpu.VMEM((span, span), F32), pltpu.VMEM((span, LANE), F32),
                            pltpu.VMEM((SUB, span), F32), pltpu.VMEM((span // LANE, SUB * span, LANE), F32)]),
        cost_estimate=pl.CostEstimate(flops=20 * heads * hd * rows * span, bytes_accessed=8 * rows * span,
                                      transcendentals=KERN * rows * span),
        compiler_params=pltpu.CompilerParams(vmem_limit_bytes=ATTEND_MIB << 20),
        name="attend",
    )(lengths, coords, qkv, w)


def back_pairs(heads, coords_ref, qkv_ref, do_ref, p_ref, dqkv_ref, dist, ds, beside):
    hd, span = do_ref.shape[1:]
    scale = 1.0 / math.sqrt(hd)
    step = LANE
    pair_distances(coords_ref, dist, span)
    if heads < SUB:
        ds[...] = jnp.zeros_like(ds)

    def head(h, carry):
        beside(h, 0, heads)
        dk = jnp.zeros((hd, span), F32)
        dv = jnp.zeros((hd, span), F32)
        for c in range(span // step):
            cols = pl.ds(c * step, step)
            rows = pl.ds(pl.multiple_of(h * span + c * step, step), step)
            pb = p_ref[rows, :]
            p = pb.astype(F32)
            dp = mm(do_ref[h, :, cols], qkv_ref[2, h], TN)
            d = p * (dp - jnp.sum(p * dp, axis=-1, keepdims=True))
            for t in range(span // LANE):
                ds[t, rows, :] = d[:, t * LANE:(t + 1) * LANE]
            low = d.astype(BF16)
            dqkv_ref[0, h, :, cols] = (mm(qkv_ref[1, h], low, NT) * scale).astype(BF16)
            dk = dk + mm(qkv_ref[0, h, :, cols], low)
            dv = dv + mm(do_ref[h, :, cols], pb)
        dqkv_ref[1, h] = (dk * scale).astype(BF16)
        dqkv_ref[2, h] = dv.astype(BF16)
        return carry

    lax.fori_loop(0, heads, head, 0)

    def group(g, acc):
        beside(heads + g, heads, heads + span // SUB)
        i0 = pl.multiple_of(g * SUB, SUB)

        left, right = [], []
        for jt in range(span // LANE):
            dblk = dist[pl.ds(i0, SUB), jt * LANE:(jt + 1) * LANE]
            for r in range(SUB // 2):
                pair = (r, r + SUB // 2)
                left.append(jnp.concatenate([ds[jt, pl.ds(i0 + k, SUB, span), :] for k in pair], 0).astype(BF16))
                right.append(jnp.concatenate([gauss_tile(row_of(dblk, k)) for k in pair], 0))
        return acc + mm(jnp.concatenate(left, 1), jnp.concatenate(right, 1), NT)

    acc = lax.fori_loop(0, span // SUB, group, jnp.zeros((2 * SUB, 2 * KERN), F32))
    return acc[:SUB, :KERN] + acc[SUB:, KERN:]


def bwd_kernel(heads, coords_ref, qkv_ref, do_ref, p_ref, dqkv_ref, pair_ref, dist, ds):
    @pl.when(pl.program_id(0) == 0)
    def _():
        pair_ref[...] = jnp.zeros_like(pair_ref)

    pair_ref[...] += back_pairs(heads, coords_ref, qkv_ref, do_ref, p_ref, dqkv_ref, dist, ds, lambda *_: None)


def attention_back(qkv, do, probs, coords):
    _, heads, hd, rows = qkv.shape
    span = probs.shape[1]
    wide = pl.BlockSpec((3, heads, hd, span), lambda b: (0, 0, 0, b))
    return pl.pallas_call(
        functools.partial(bwd_kernel, heads),
        out_shape=(jax.ShapeDtypeStruct(qkv.shape, BF16), jax.ShapeDtypeStruct((SUB, KERN), F32)),
        grid=(rows // span,),
        in_specs=[pl.BlockSpec((3, span), lambda b: (0, b)), wide,
                  pl.BlockSpec((heads, hd, span), lambda b: (0, 0, b)),
                  pl.BlockSpec((heads * span, span), lambda b: (b, 0))],
        out_specs=[wide, pl.BlockSpec((SUB, KERN), lambda b: (0, 0))],
        scratch_shapes=[pltpu.VMEM((span, span), F32), pltpu.VMEM((span // LANE, SUB * span, LANE), F32)],
        compiler_params=pltpu.CompilerParams(vmem_limit_bytes=60 << 20),
        name="attend_back",
    )(coords, qkv, do, probs)


def mm(a, b, dims=NN):
    return lax.dot_general(a, b, dims, preferred_element_type=F32)


def remote(src, dst, send, recv, axis, target):
    return pltpu.make_async_remote_copy(
        src_ref=src, dst_ref=dst, send_sem=send, recv_sem=recv,
        device_id={axis: target}, device_id_type=MESH)


def greet(sizes, others=()):
    barrier = pltpu.get_barrier_semaphore()
    total = len(others)
    for place in others:
        pl.semaphore_signal(barrier, inc=1, device_id={"dp": place}, device_id_type=MESH)
    for axis, size in sizes.items():
        me = lax.axis_index(axis)
        for k in range(1, size):
            pl.semaphore_signal(barrier, inc=1, device_id={axis: lax.rem(me + k, size)}, device_id_type=MESH)
        total += size - 1
    pl.semaphore_wait(barrier, total)


class Seat:
    def __init__(self, n):
        self.n, self.nx = n, n // 2
        self.me = lax.axis_index("mp")
        self.core = lax.rem(self.me, 2)
        self.x = self.me // 2
        self.sib = self.me + 1 - 2 * self.core

    def chip(self, k):
        return lax.rem(self.x + 1 + k, self.nx)

    def source(self, k):
        return lax.rem(self.x + self.nx - 1 - k, self.nx)


class Grid:
    def __init__(self, ny, nz):
        self.ny, self.nz = ny, nz
        self.me = lax.axis_index("dp")
        self.z, self.y = self.me // ny, lax.rem(self.me, ny)
        self.nh, self.a, self.p = nz // 2, self.z // 2, lax.rem(self.z, 2)
        self.near = self.z + 1 - 2 * self.p

    def at(self, z, y):
        return z * self.ny + y

    def other(self, k):
        return lax.rem(self.a + 1 + k, self.nh)

    def far(self, k):
        return 2 * self.other(k) + self.p

    def yto(self, k):
        return lax.rem(self.y + 1 + k, self.ny)


def scatter_scratch(n, rows, width):
    nx = n // 2
    buf = lambda m: pltpu.VMEM((m, rows, width), BF16)
    return [buf(nx), buf(nx), buf(max(nx - 1, 1)), buf(max(nx - 1, 1)), DMA((nx,)), DMA((nx,)),
            DMA((max(nx - 1, 1),)), DMA((max(nx - 1, 1),))]


class Scatter:
    def __init__(self, seat, scratch):
        self.seat = seat
        self.out1, self.in1, self.out2, self.in2, self.s1, self.r1, self.s2, self.r2 = scratch

    def first(self, k):
        return remote(self.out1.at[k], self.in1.at[k], self.s1.at[k], self.r1.at[k], "mp", self.seat.sib)

    def second(self, k):
        target = self.seat.chip(k) * 2 + self.seat.core
        return remote(self.out2.at[k], self.in2.at[k], self.s2.at[k], self.r2.at[k], "mp", target)

    def push(self, block):
        for k in range(self.seat.nx):
            self.out1[k] = block(self.seat.chip(k) * 2 + 1 - self.seat.core).astype(BF16)
            self.first(k).start()

    def pass_on(self, block):
        seat = self.seat
        parts = [block(seat.chip(k) * 2 + seat.core) for k in range(seat.nx)]
        for k in range(seat.nx):
            self.first(k).wait_recv()
            whole = parts[k] + self.in1[k].astype(F32)
            if k < seat.nx - 1:
                self.out2[k] = whole.astype(BF16)
                self.second(k).start()
        return whole

    def finish(self, whole):
        for k in range(self.seat.nx - 1):
            self.second(k).wait_recv()
            whole = whole + self.in2[k].astype(F32)
        return whole

    def drain(self):
        for k in range(self.seat.nx):
            self.first(k).wait_send()
        for k in range(self.seat.nx - 1):
            self.second(k).wait_send()


def gather_scratch(n):
    nx = n // 2
    return [DMA((max(nx - 1, 1),)), DMA((max(nx - 1, 1),)), DMA((nx,)), DMA((nx,))]


class Gather:
    def __init__(self, seat, rows, scratch):
        self.seat, self.rows = seat, rows
        self.sx, self.rx, self.sc, self.rc = scratch

    def across(self, k):
        r = self.rows.at[self.seat.me]
        return remote(r, r, self.sx.at[k], self.rx.at[k], "mp", self.seat.chip(k) * 2 + self.seat.core)

    def along(self, k):
        chip = self.seat.x if k == self.seat.nx - 1 else self.seat.source(k)
        r = self.rows.at[chip * 2 + self.seat.core]
        return remote(r, r, self.sc.at[k], self.rc.at[k], "mp", self.seat.sib)

    def start(self):
        for k in range(self.seat.nx - 1):
            self.across(k).start()
        self.along(self.seat.nx - 1).start()

    def forward(self):
        for k in range(self.seat.nx - 1):
            self.across(k).wait_recv()
            self.along(k).start()

    def finish(self):
        for k in range(self.seat.nx):
            self.along(k).wait_recv()

    def drain(self):
        for k in range(self.seat.nx - 1):
            self.across(k).wait_send()
        for k in range(self.seat.nx):
            self.along(k).wait_send()


def centre(rows):
    c = rows - jnp.mean(rows, axis=-1, keepdims=True)
    r = lax.rsqrt(jnp.mean(c * c, axis=-1, keepdims=True) + ln_eps)
    return c * r, r


def norm_back(rows, gain, e):
    vhat, r = centre(rows)
    ge = e * gain
    dv = r * (ge - jnp.mean(ge, axis=-1, keepdims=True) - vhat * jnp.mean(ge * vhat, axis=-1, keepdims=True))
    return dv, jnp.sum(e * vhat, axis=0, keepdims=True), jnp.sum(e, axis=0, keepdims=True)


def enter_kernel(n, x_ref, np_ref, w_hbm, h_ref, qkv_ref, w32, wsem, *sems):
    seat = Seat(n)
    load = pltpu.make_async_copy(w_hbm, w32, wsem)
    load.start()
    greet({"mp": n})
    vhat, _ = centre(x_ref[...].astype(F32))
    h_ref[seat.me] = (vhat * np_ref[0:1] + np_ref[1:2]).astype(BF16)
    gh = Gather(seat, h_ref, sems)
    gh.start()
    load.wait()
    gh.forward()
    gh.finish()
    rows = h_ref.shape[1]
    for s in range(3):
        w = w32[s].astype(BF16)

        def block(b, carry):
            out = mm(w, h_ref[b], NT)
            qkv_ref[s, :, :, pl.ds(pl.multiple_of(b * rows, rows), rows)] = out.reshape(
                *qkv_ref.shape[1:3], rows).astype(BF16)
            return carry

        lax.fori_loop(0, n, block, 0)
    gh.drain()


def enter(n, heads, x, params, qkv_weight):
    rows, width = x.shape
    _, inner, _ = qkv_weight.shape
    return pl.pallas_call(
        functools.partial(enter_kernel, n),
        out_shape=(jax.ShapeDtypeStruct((n, rows, width), BF16),
                   jax.ShapeDtypeStruct((3, heads, inner // heads, n * rows), BF16)),
        in_specs=[VM, VM, HBM], out_specs=[VM, VM],
        scratch_shapes=[pltpu.VMEM(qkv_weight.shape, F32), DMA, *gather_scratch(n)],
        compiler_params=pltpu.CompilerParams(collective_id=0, has_side_effects=True, vmem_limit_bytes=60 << 20),
        name="enter",
    )(x, params, qkv_weight)


def middle_kernel(n, ny, nz, pushes, x_ref, o_ref, np_ref, bias_ref, pw_hbm, iw_hbm, ow_hbm, *rest):
    dys, rest = rest[:n], rest[n:]
    (block_ref, mid_ref, do_ref, og_ref, ig_ref, pg_ref, bg_ref, small_ref), rest = rest[:8], rest[8:]
    lands, rest = rest[:pushes], rest[pushes:]
    (pw32, iw32, ow32, pw, iw, ow, h2, da, act, dpre, dact, dyall_ref, wsem), rest = rest[:13], rest[13:]
    seat, grid = Seat(n), Grid(ny, nz)
    dy_ref = dys[0]
    rows, width = x_ref.shape
    loads = [pltpu.make_async_copy(a, b, wsem.at[i])
             for i, (a, b) in enumerate([(pw_hbm, pw32), (ow_hbm, ow32), (iw_hbm, iw32)])]
    for c in loads:
        c.start()
    scat = [Scatter(seat, rest[8 * i:8 * i + 8]) for i in range(3)]
    gath = [Gather(seat, r, rest[24 + 4 * i:28 + 4 * i]) for i, r in enumerate((h2, da))]
    places = [grid.z * ny + grid.yto(k) for k in range(ny - 1)]
    greet({"mp": n}, places if pushes else ())

    def ahead(i, k):
        part = (og_ref, ig_ref)[i // PARTS]
        tall = part.shape[0] // (PARTS * ny)
        start = pl.multiple_of(((i % PARTS) * ny + grid.yto(k)) * tall, 16)
        return remote(part.at[pl.ds(start, tall), :], lands[i].at[k], rest[32].at[i, k], rest[33].at[i, k],
                      "dp", places[k])

    copies = [[ahead(i, k) for k in range(ny - 1)] for i in range(pushes)]
    for k in range(n):
        dyall_ref[lax.rem(seat.me + k, n)] = dys[k][...]
    at = lambda b: pl.ds(pl.multiple_of(b * rows, rows), rows)

    loads[0].wait()
    pw[...] = pw32[...].astype(BF16)
    attn_block = lambda b: mm(o_ref[:, at(b)], pw[...], TN)
    scat[0].push(attn_block)
    loads[1].wait()
    ow[...] = ow32[...].astype(BF16)
    whole = scat[0].pass_on(attn_block)
    loads[2].wait()
    iw[...] = iw32[...].astype(BF16)

    def back_act(b, carry):
        dact[b] = mm(dyall_ref[b], ow[...], NT)
        return carry

    lax.fori_loop(0, n, back_act, 0)
    mid = x_ref[...].astype(F32) + scat[0].finish(whole)
    vhat, _ = centre(mid)
    h2[seat.me] = (vhat * np_ref[2:3] + np_ref[3:4]).astype(BF16)
    mid_ref[...] = mid
    gath[0].start()
    gath[0].forward()
    gath[0].finish()

    bg_ref[...] = jnp.zeros_like(bg_ref)
    bias = bias_ref[...].astype(BF16).astype(F32)

    def feed_block(b):
        pre = mm(h2[b], iw[...], NT) + bias
        phi = 0.5 + 0.5 * lax.erf(pre * math.sqrt(0.5))
        act[b] = (pre * phi).astype(BF16)
        slope = phi + pre * (jnp.exp(-0.5 * pre * pre) * (1.0 / math.sqrt(2.0 * math.pi)))
        d = (dact[b] * slope).astype(BF16)
        dpre[b] = d
        bg_ref[...] += jnp.sum(d.astype(F32), axis=0, keepdims=True)
        return mm(d, iw[...])

    scat[1].push(feed_block)
    whole = scat[1].pass_on(feed_block)
    hidden = iw.shape[0]
    step = LANE if hidden % LANE == 0 else hidden

    def grads(left, right, out, first):
        def columns(i, carry):
            c0 = pl.multiple_of(i * step, step)
            acc = jnp.zeros((step, width), F32)
            for b in range(n):
                acc += mm(left[b, :, pl.ds(c0, step)], right[b], TN)
            out[pl.ds(c0, step), :] = acc.astype(BF16)
            return carry

        lax.fori_loop(0, hidden // step, columns, 0)
        for piece in copies[first:first + PARTS]:
            for copy in piece:
                copy.start()

    grads(act, dyall_ref, og_ref, 0)
    out_block = lambda b: mm(act[b], ow[...])
    scat[2].push(out_block)
    dh2 = scat[1].finish(whole)
    dv, gain, shift = norm_back(mid_ref[...], np_ref[2:3], dh2)
    dy = dy_ref[...].astype(F32)
    dx1 = dy + dv
    da[seat.me] = dx1.astype(BF16)
    gath[1].start()
    small_ref[...] = jnp.concatenate(
        [gain, shift, jnp.sum(dy, axis=0, keepdims=True), jnp.zeros((5, width), F32)], 0)
    whole = scat[2].pass_on(out_block)
    gath[1].forward()
    grads(dpre, h2, ig_ref, PARTS)
    block_ref[...] = mid_ref[...] + scat[2].finish(whole) + np_ref[4:5]
    mid_ref[...] = dx1
    gath[1].finish()

    def heads_block(b, acc):
        out = mm(pw[...], da[b], NT)
        do_ref[:, :, at(b)] = out.reshape(*do_ref.shape[:2], rows).astype(BF16)
        return acc + mm(o_ref[:, at(b)], da[b])

    pg_ref[...] = lax.fori_loop(0, n, heads_block, jnp.zeros(pg_ref.shape, F32)).astype(BF16)
    for c in scat + gath:
        c.drain()
    for piece in copies:
        for copy in piece:
            copy.wait()


PARTS = 2
MIDDLE_MIB = 24


def middle(n, ny, nz, pushes, x, dys, o, params, bias, proj_weight, in_weight, out_weight):
    rows, width = x.shape
    hidden = in_weight.shape[0]
    inner = proj_weight.shape[0]
    heads, hd, _ = o.shape
    f = lambda *s: jax.ShapeDtypeStruct(s, F32)
    return pl.pallas_call(
        functools.partial(middle_kernel, n, ny, nz, pushes),
        out_shape=(f(rows, width), f(rows, width), jax.ShapeDtypeStruct(o.shape, BF16),
                   *[jax.ShapeDtypeStruct((t, width), BF16) for t in (hidden, hidden, inner)], f(1, hidden), f(8, width),
                   *[jax.ShapeDtypeStruct((ny - 1, hidden // (PARTS * ny), width), BF16)] * pushes),
        in_specs=[VM] * 4 + [HBM] * 3 + [VM] * n, out_specs=[VM] * (8 + pushes),
        scratch_shapes=[pltpu.VMEM((inner, width), F32), pltpu.VMEM((hidden, width), F32),
                        pltpu.VMEM((hidden, width), F32), pltpu.VMEM((inner, width), BF16),
                        pltpu.VMEM((hidden, width), BF16), pltpu.VMEM((hidden, width), BF16),
                        pltpu.VMEM((n, rows, width), BF16), pltpu.VMEM((n, rows, width), BF16),
                        pltpu.VMEM((n, rows, hidden), BF16), pltpu.VMEM((n, rows, hidden), BF16),
                        pltpu.VMEM((n, rows, hidden), F32), pltpu.VMEM((n, rows, width), BF16), DMA((3,)),
                        *[s for _ in range(3) for s in scatter_scratch(n, rows, width)],
                        *gather_scratch(n), *gather_scratch(n),
                        *[DMA((max(pushes, 1), max(ny - 1, 1)))] * 2],
        compiler_params=pltpu.CompilerParams(collective_id=1, has_side_effects=True, vmem_limit_bytes=MIDDLE_MIB << 20),
        name="middle",
    )(x, o.reshape(inner, -1), params, bias, proj_weight, in_weight, out_weight, *dys)


def sum_scratch(shape):
    ny, _, nh, chunk, width = shape
    y, f = max(ny - 1, 1), max(nh - 1, 1)
    return [pltpu.VMEM((y, 2, nh, chunk, width), BF16), pltpu.VMEM((nh, chunk, width), F32),
            pltpu.VMEM((nh, chunk, width), BF16), pltpu.VMEM((nh, chunk, width), BF16),
            pltpu.VMEM((f, chunk, width), BF16), pltpu.VMEM((f, chunk, width), BF16),
            DMA((y,)), DMA((y,)), DMA((1,)), DMA((1,)), DMA((f,)), DMA((f,))]


class Sum:
    count = 12

    def __init__(self, grid, grad, own, scratch):
        self.grid, self.grad, self.own, self.pushed = grid, grad, own, True
        (self.ia, self.keep, self.ob, self.ib, self.oc, self.ic,
         self.sa, self.ra, self.sb, self.rb, self.sc, self.rc) = scratch

    def copy_y(self, k):
        g = self.grid
        return remote(self.grad.at[g.yto(k)], self.ia.at[k], self.sa.at[k], self.ra.at[k], "dp", g.at(g.z, g.yto(k)))

    def copy_near(self):
        g = self.grid
        return remote(self.ob, self.ib, self.sb.at[0], self.rb.at[0], "dp", g.at(g.near, g.y))

    def copy_far(self, k):
        g = self.grid
        return remote(self.oc.at[k], self.ic.at[k], self.sc.at[k], self.rc.at[k], "dp", g.at(g.far(k), g.y))

    def push(self):
        for k in range(self.grid.ny - 1):
            self.copy_y(k).start()

    def half(self, p):
        g = self.grid
        whole = self.grad[g.y, p].astype(F32)
        for k in range(g.ny - 1):
            whole = whole + self.ia[k, p].astype(F32)
        return whole

    def near(self):
        g = self.grid
        for k in range(g.ny - 1 if self.pushed else 0):
            self.copy_y(k).wait_recv()
        self.ob[...] = self.half(1 - g.p).astype(BF16)
        self.copy_near().start()
        self.keep[...] = self.half(g.p)

    def far(self):
        g = self.grid
        self.copy_near().wait_recv()
        for k in range(g.nh - 1):
            a = g.other(k)
            self.oc[k] = (self.keep[a] + self.ib[a].astype(F32)).astype(BF16)
            self.copy_far(k).start()
        self.own[...] = self.keep[g.a] + self.ib[g.a].astype(F32)

    def collect(self):
        whole = self.own[...]
        for k in range(self.grid.nh - 1):
            self.copy_far(k).wait_recv()
            whole = whole + self.ic[k].astype(F32)
        self.own[...] = whole

    def drain(self):
        g = self.grid
        for k in range(g.ny - 1 if self.pushed else 0):
            self.copy_y(k).wait_send()
        self.copy_near().wait_send()
        for k in range(g.nh - 1):
            self.copy_far(k).wait_send()


def spread_scratch(ny, nz):
    y, f = max(ny - 1, 1), max(nz // 2 - 1, 1)
    return [DMA((f,)), DMA((f,)), DMA((1,)), DMA((1,)), DMA((2, y)), DMA((2, y))]


class Spread:
    count = 6

    def __init__(self, grid, own, result, scratch):
        self.grid, self.own, self.result = grid, own, result
        self.sf, self.rf, self.sn, self.rn, self.sy, self.ry = scratch

    def to_far(self, k):
        g = self.grid
        r = self.result.at[g.y, g.p, g.a]
        return remote(r, r, self.sf.at[k], self.rf.at[k], "dp", g.at(g.far(k), g.y))

    def to_near(self):
        g = self.grid
        r = self.result.at[g.y, g.p]
        return remote(r, r, self.sn.at[0], self.rn.at[0], "dp", g.at(g.near, g.y))

    def to_y(self, i, k):
        g = self.grid
        r = self.result.at[g.y, g.p if i == 0 else 1 - g.p]
        return remote(r, r, self.sy.at[i, k], self.ry.at[i, k], "dp", g.at(g.z, g.yto(k)))

    def start(self):
        g = self.grid
        whole = self.own[...]
        self.result[g.y, g.p, g.a] = whole.astype(BF16)
        for k in range(g.nh - 1):
            self.to_far(k).start()
        return square(whole)

    def second(self):
        g = self.grid
        for k in range(g.nh - 1):
            self.to_far(k).wait_recv()
        self.to_near().start()
        for k in range(g.ny - 1):
            self.to_y(0, k).start()

    def third(self):
        self.to_near().wait_recv()
        for k in range(self.grid.ny - 1):
            self.to_y(1, k).start()

    def close(self):
        g = self.grid
        for i in range(2):
            for k in range(g.ny - 1):
                self.to_y(i, k).wait()
        for k in range(g.nh - 1):
            self.to_far(k).wait_send()
        self.to_near().wait_send()


def take(rest, cls, count):
    size = cls.count
    return [rest[size * i:size * (i + 1)] for i in range(count)], rest[size * count:]


class Share:
    def __init__(self, axis, slots, send, recv):
        self.axis, self.slots, self.send, self.recv = axis, slots, send, recv
        self.size = slots.shape[0]
        self.me = lax.axis_index(axis)

    def copy(self, k):
        r = self.slots.at[self.me]
        return remote(r, r, self.send.at[k], self.recv.at[k], self.axis, lax.rem(self.me + 1 + k, self.size))

    def start(self, value):
        self.slots[self.me] = value
        for k in range(self.size - 1):
            self.copy(k).start()

    def total(self):
        for k in range(self.size - 1):
            self.copy(k).wait_recv()
        out = self.slots[0]
        for i in range(1, self.size):
            out = out + self.slots[i]
        return out

    def drain(self):
        for k in range(self.size - 1):
            self.copy(k).wait_send()


def share_scratch(size, rows, width):
    return [pltpu.VMEM((size, rows, width), F32), DMA((max(size - 1, 1),)), DMA((max(size - 1, 1),))]


def square(v):
    return jnp.sum(jnp.sum(v * v, axis=1, keepdims=True), axis=0, keepdims=True)


def leave_kernel(n, ny, nz, late, x_ref, dx_ref, np_ref, dqkv_ref, h_ref, bg_ref, pair_ref, squares_ref,
                 mid_small_ref, *rest):
    owns, (w_hbm, gi_ref), rest = rest[:late], rest[late:late + 2], rest[late + 2:]
    results, rest = rest[:late], rest[late:]
    (sq_ref, small_ref, bias_ref, pairs_ref, norm_ref, w32, w, qg, qown, wsem), rest = rest[:10], rest[10:]
    seat, grid = Seat(n), Grid(ny, nz)
    rows, width = x_ref.shape
    inner = w.shape[1]
    load = pltpu.make_async_copy(w_hbm, w32, wsem)
    load.start()
    scat, rest = Scatter(seat, rest[:8]), rest[8:]
    parts, rest = take(rest, Sum, 3)
    sums = [Sum(grid, qg.at[s], qown.at[s], p) for s, p in enumerate(parts)]
    parts, rest = take(rest, Spread, 3 + late)
    spreads = [Spread(grid, s.own, sq_ref.at[i], p) for i, (s, p) in enumerate(zip(sums, parts))]
    olds = [Spread(grid, o, r, p) for o, r, p in zip(owns, results, parts[3:])]
    shares = [Share(a, *rest[3 * i:3 * i + 3]) for i, a in enumerate(("mp", "dp", "dp", "dp", "mp", "dp"))]
    small_mp, small_dp, bias_dp, pair_dp, sq_mp, sq_dp = shares
    greet({"mp": n, "dp": ny * nz})
    at = lambda b: pl.ds(pl.multiple_of(b * rows, rows), rows)

    for s in range(3):
        acc = jnp.zeros((inner, width), F32)
        for b in range(n):
            acc = acc + mm(dqkv_ref[s, :, at(b)], h_ref[b])
        qg[s] = acc.reshape(qg.shape[1:]).astype(BF16)
        sums[s].push()
    load.wait()
    w[...] = w32[...].astype(BF16)

    def first_block(b):
        return sum(mm(dqkv_ref[s, :, at(b)], w[s], TN) for s in range(3))

    scat.push(first_block)
    squares = squares_ref[0:1]
    for s in olds:
        squares = squares + s.start()
    whole = scat.pass_on(first_block)
    bias_dp.start(jnp.broadcast_to(bg_ref[...], bias_dp.slots.shape[1:]))
    pair_dp.start(pair_ref[...])
    sums[0].near()
    for s in olds:
        s.second()
    sums[1].near()
    dh1 = scat.finish(whole)
    dv, gain, shift = norm_back(x_ref[...].astype(F32), np_ref[0:1], dh1)
    gi_ref[...] = dx_ref[...] + dv
    small_mp.start(jnp.concatenate([gain, shift, mid_small_ref[0:6]], 0))
    sums[0].far()
    sums[2].near()
    sums[1].far()
    small_dp.start(small_mp.total())
    for s in olds:
        s.third()
    sums[2].far()
    for s, t in zip(sums, spreads):
        s.collect()
        squares = squares + t.start()
    spreads[0].second()
    bias = bias_dp.total()
    bias_ref[...] = bias
    pairs = pair_dp.total()
    pairs_ref[...] = pairs
    row = lax.broadcasted_iota(jnp.int32, (8, LANE), 0)
    local = square(bias[0:1]) + square(pairs)
    sq_mp.start(jnp.where(row == 0, squares, jnp.where(row == 1, local, 0.0)))
    small = small_dp.total()
    small_ref[...] = small
    spreads[1].second()
    sq_dp.start(sq_mp.total())
    spreads[2].second()
    for s in spreads:
        s.third()
    norm_ref[...] = sq_dp.total()[0:1] + sq_dp.slots[0, 1:2] + square(small)
    for s in olds + spreads:
        s.close()
    for s in [scat] + sums + shares:
        s.drain()


def leave(n, ny, nz, x, dx, params, dqkv, h, bias_grad, pair_grad, squares, small, owns, qkv_weight):
    rows, width = x.shape
    inner = qkv_weight.shape[1]
    ndp = ny * nz
    hidden = bias_grad.shape[1]
    chunks = (3, ny, 2, nz // 2, inner // ndp, width)
    f = lambda *s: jax.ShapeDtypeStruct(s, F32)
    late = len(owns)
    return pl.pallas_call(
        functools.partial(leave_kernel, n, ny, nz, late),
        out_shape=(f(rows, width), *[jax.ShapeDtypeStruct((ny, 2, nz // 2, *o.shape), BF16) for o in owns],
                   jax.ShapeDtypeStruct(chunks, BF16), f(8, width), f(8, hidden), f(8, LANE), f(1, LANE)),
        in_specs=[VM] * (9 + late) + [HBM], out_specs=[VM] * (6 + late),
        scratch_shapes=[pltpu.VMEM(qkv_weight.shape, F32), pltpu.VMEM(qkv_weight.shape, BF16),
                        pltpu.VMEM(chunks, BF16), pltpu.VMEM((3, inner // ndp, width), F32), DMA,
                        *scatter_scratch(n, rows, width),
                        *[s for _ in range(3) for s in sum_scratch(chunks[1:])],
                        *[s for _ in range(3 + late) for s in spread_scratch(ny, nz)],
                        *share_scratch(n, 8, width), *share_scratch(ndp, 8, width), *share_scratch(ndp, 8, hidden),
                        *share_scratch(ndp, 8, LANE), *share_scratch(n, 8, LANE), *share_scratch(ndp, 8, LANE)],
        compiler_params=pltpu.CompilerParams(collective_id=2, has_side_effects=True, vmem_limit_bytes=LEAVE_MIB << 20),
        name="leave",
    )(x, dx, params, dqkv, h, bias_grad, pair_grad, squares, small, *owns, qkv_weight)


def leave_plain(n, x, dx, params, dqkv, h, grads, bias_grad, pair_grad, small, qkv_weight):
    part = sum(mm(dqkv[s], qkv_weight[s].astype(BF16), TN) for s in range(3))
    dh1 = lax.psum_scatter(part, "mp", scatter_dimension=0, tiled=True)
    dv, gain, shift = norm_back(x.astype(F32), params[0:1], dh1)
    hh = h.reshape(-1, h.shape[-1])
    qg = jnp.concatenate([mm(dqkv[s], hh) for s in range(3)], 0)
    og, ig, pg, qg, bias, pair = lax.psum((*[g.astype(F32) for g in grads], qg, bias_grad, pair_grad), "dp")
    small = lax.psum(jnp.concatenate([gain, shift, small[0:6]], 0), ("dp", "mp"))
    local = sum(square(v) for v in (og, ig, pg, qg, bias, pair))
    total = lax.psum(local, "mp") + square(small)
    return dx + dv, og, ig, pg, qg, small, bias, pair, total


NEAR_AT = (0, 0, 6, 14, 20)
FAR_AT = (4, 7, 16, 26, 32)
COLLECT_AT = (10, 15, 28, 38, 42)
SECOND_AT = (18, 24, 36, 48, 52)
THIRD_AT = (26, 33, 46, 60, 64)
FIRST = 1
EARLY = 5
BACK_MIB = 24
LEAVE_MIB = 16


def back_kernel(heads, ny, nz, parts, pushes, coords_ref, qkv_ref, do_ref, p_ref, og_ref, ig_ref, pg_ref, *rest):
    lands, (dqkv_ref, pair_ref, squares_ref), rest = rest[:pushes], rest[pushes:pushes + 3], rest[pushes + 3:]
    owns, rest = rest[:2 * parts + 1 - EARLY], rest[2 * parts + 1 - EARLY:]
    results, (dist, ds), rest = rest[:EARLY], rest[EARLY:EARLY + 2], rest[EARLY + 2:]
    early, rest = rest[:EARLY], rest[EARLY:]
    hd, span = do_ref.shape[1:]
    grid = Grid(ny, nz)
    pieces = [g.at[i] for g in (og_ref, ig_ref) for i in range(parts)] + [pg_ref]
    places = [*early, *owns]
    scratch, rest = take(rest, Sum, len(pieces))
    sums = [Sum(grid, *a) for a in zip(pieces, places, scratch)]
    scratch, rest = take(rest, Spread, EARLY)
    spreads = [Spread(grid, *a) for a in zip(places, results, scratch)]
    for s, land in zip(sums, lands):
        s.ia, s.pushed = land, False
    greet({"dp": ny * nz})
    for s in sums[pushes:]:
        s.push()
    for s in sums[:FIRST]:
        s.near()
    squares_ref[...] = jnp.zeros_like(squares_ref)

    def collect(i):
        sums[i].collect()
        if i < EARLY:
            squares_ref[...] += spreads[i].start()

    jobs = {}
    for i, s in enumerate(sums):
        if i >= FIRST:
            jobs.setdefault(NEAR_AT[i], []).append(s.near)
        jobs.setdefault(FAR_AT[i], []).append(s.far)
        jobs.setdefault(COLLECT_AT[i], []).append(functools.partial(collect, i))
    for i, s in enumerate(spreads):
        jobs.setdefault(SECOND_AT[i], []).append(s.second)
        jobs.setdefault(THIRD_AT[i], []).append(s.third)
    last = heads + span // SUB

    def beside(step, first, end):
        for when in sorted(jobs):
            if first <= when < end:
                @pl.when(step == when)
                def _():
                    for job in jobs[when]:
                        job()

    pair_ref[...] = back_pairs(heads, coords_ref, qkv_ref, do_ref, p_ref, dqkv_ref, dist, ds, beside)
    for when in sorted(jobs):
        if when >= last:
            for job in jobs[when]:
                job()
    for s in spreads:
        s.close()
    for s in sums:
        s.drain()


def attention_back_sums(qkv, do, probs, coords, ny, nz, og, ig, pg, lands):
    _, heads, hd, span = qkv.shape
    width = og.shape[1]
    ndp, parts, pushes = ny * nz, PARTS, len(lands)
    lands = [v.reshape(ny - 1, 2, nz // 2, -1, width) for v in lands]
    cut = lambda g, p: g.reshape(p, ny, 2, nz // 2, g.shape[0] // (p * ndp), width)
    og, ig, pg = cut(og, parts), cut(ig, parts), cut(pg, 1)[0]
    shapes = [og.shape[1:]] * parts + [ig.shape[1:]] * parts + [pg.shape]
    f = lambda *s: jax.ShapeDtypeStruct(s, F32)
    return pl.pallas_call(
        functools.partial(back_kernel, heads, ny, nz, parts, pushes),
        out_shape=(jax.ShapeDtypeStruct(qkv.shape, BF16), f(SUB, KERN), f(SUB, LANE),
                   *[f(*s[3:]) for s in shapes[EARLY:]], *[jax.ShapeDtypeStruct(s, BF16) for s in shapes[:EARLY]]),
        in_specs=[VM] * (7 + pushes), out_specs=[VM] * (3 + len(shapes)),
        scratch_shapes=[pltpu.VMEM((span, span), F32), pltpu.VMEM((span // LANE, SUB * span, LANE), F32),
                        *[pltpu.VMEM(shape[3:], F32) for shape in shapes[:EARLY]],
                        *[s for shape in shapes for s in sum_scratch(shape)],
                        *[s for _ in range(EARLY) for s in spread_scratch(ny, nz)]],
        compiler_params=pltpu.CompilerParams(collective_id=3, has_side_effects=True, vmem_limit_bytes=BACK_MIB << 20),
        name="attend_back_sums",
    )(coords, qkv, do, probs, og, ig, pg, *lands)


PUSHES = 2


def adam_step(weight, grad, first, second, clip, fix_one, fix_two, rate, decay):
    scaled = grad * clip
    first_new = beta_one * first + (1.0 - beta_one) * scaled
    second_new = beta_two * second + (1.0 - beta_two) * scaled * scaled
    ratio = first_new / fix_one / (jnp.sqrt(second_new / fix_two) + adam_eps)
    return (weight - rate * (ratio + decay * weight), first_new, second_new)


def per_device(n, ndp, block_in, coords, lengths, cotangent, step_count, *state):
    weights, firsts, seconds = state[:7], state[7:14], state[14:]
    qkv_weight, proj_weight, pair_weight, in_weight, in_bias, out_weight, params = weights
    heads = pair_weight.shape[0]
    pair_low = pair_weight.astype(BF16)
    h, qkv = enter(n, heads, block_in, params, qkv_weight)
    o, probs = attention(qkv, coords, lengths, pair_low)
    dy, _ = lax.optimization_barrier((cotangent, qkv))
    dys = [cotangent] + [lax.ppermute(dy, "mp", [((i + k) % n, i) for i in range(n)]) for k in range(1, n)]
    ny = n // 2 if ndp % (n // 2) == 0 else 1
    nz = ndp // ny
    inner, hidden = proj_weight.shape[0], in_weight.shape[0]
    beside = lengths.shape[0] == 1 and nz % 2 == 0 and inner % (8 * ndp) == 0 and hidden % (16 * PARTS * ndp) == 0
    block_out, dx, do, og, ig, pg, bg, small, *lands = middle(
        n, ny, nz, PUSHES if beside else 0, block_in, dys, o, params, in_bias.reshape(1, -1), proj_weight, in_weight, out_weight)
    if beside:
        dqkv, pair_grad, squares, *parts = attention_back_sums(qkv, do, probs, coords, ny, nz, og, ig, pg, lands)
        owns, done = parts[:-EARLY], parts[-EARLY:]
        grad_input, *sums, qg, small, bias, pair, total = leave(
            n, ny, nz, block_in, dx, params, dqkv.reshape(3, inner, -1), h, bg, pair_grad, squares, small, owns, qkv_weight)
        *pieces, pg = *done, *sums
        og, ig = pieces[:len(pieces) // 2], pieces[len(pieces) // 2:]
        og, ig = [jnp.concatenate([v.reshape(-1, v.shape[-1]) for v in g], 0) for g in (og, ig)]
    else:
        dqkv, pair_grad = attention_back(qkv, do, probs, coords)
        grad_input, og, ig, pg, qg, small, bias, pair, total = leave_plain(
            n, block_in, dx, params, dqkv.reshape(3, inner, -1), h, (og, ig, pg), bg, pair_grad, small, qkv_weight)
    grad_norm = jnp.sqrt(total[0, 0])
    clip = clip_level / jnp.maximum(grad_norm, clip_level)
    count = step_count[0].astype(F32)
    fix_one = 1.0 - jnp.power(beta_one, count)
    fix_two = 1.0 - jnp.power(beta_two, count)
    grads = (qg.reshape(qkv_weight.shape), pg.reshape(proj_weight.shape), pair[:heads], ig.reshape(in_weight.shape),
             bias[0], og.reshape(out_weight.shape), small[:5])
    rates = (0.9, 2.5, 7.5, 0.9, 7.5, 0.45, 3.0)
    decays = (0.01, 0.01, 0.01, 0.01, 0.0, 0.01, 0.0)
    outs = [block_out, grad_input, grad_norm.reshape(1)]
    for w, g, m, u, rate, decay in zip(weights, grads, firsts, seconds, rates, decays):
        outs.extend(adam_step(w, g.astype(F32), m, u, clip, fix_one, fix_two, rate, decay))
    return tuple(outs)


def solution(mesh):
    rows, mp = P(("dp", "mp"), None), P("mp", None)
    stacked = P(None, "mp", None)
    params = (stacked, mp, mp, mp, P("mp"), mp, P())
    in_specs = (rows, P(None, "dp"), P("dp", None), rows, P(), *params, *params, *params)
    out_specs = (rows, rows, P(), *[s for s in params for _ in range(3)])
    return jax.shard_map(
        functools.partial(per_device, mesh.shape["mp"], mesh.shape["dp"]),
        mesh=mesh, in_specs=in_specs, out_specs=out_specs, check_vma=False)
```

```python
import functools
import math

import jax
import jax.numpy as jnp
from jax import lax
from jax.experimental import pallas as pl
from jax.experimental.pallas import tpu as pltpu
from jax.sharding import PartitionSpec as P

ln_eps = 1e-05
beta_one = 0.9
beta_two = 0.999
adam_eps = 1e-08
clip_level = 1.0

F32, BF16 = jnp.float32, jnp.bfloat16
MESH = pl.DeviceIdType.MESH
NN = (((1,), (0,)), ((), ()))
NT = (((1,), (1,)), ((), ()))
TN = (((0,), (0,)), ((), ()))
VM = pl.BlockSpec(memory_space=pltpu.VMEM)
HBM = pl.BlockSpec(memory_space=pl.ANY)
DMA = pltpu.SemaphoreType.DMA
KERN = 128
LANE = 128
SUB = 8
TALL = 32
ATTEND_MIB = 20
KS = math.sqrt(0.5 * math.log2(math.e))
UNIT = KS / (12.8 / KERN)


def pair_distances(coords_ref, dist, span):
    pts = coords_ref[...]
    cols = jnp.transpose(jnp.concatenate([pts, jnp.zeros((5, span), F32)], 0))
    acc = None
    for a in range(3):
        d = cols[:, a:a + 1] - pts[a:a + 1, :]
        acc = d * d if acc is None else acc + d * d
    dist[...] = jnp.sqrt(acc) * UNIT


def pair_labels(len_ref, b, labs, labr, span, mols):
    lanes = lax.broadcasted_iota(jnp.int32, (SUB, span), 1)
    lc = jnp.zeros((SUB, span), F32)
    end = jnp.int32(0)
    for m in range(mols):
        end = end + len_ref[b, m]
        lc = lc + (lanes >= end).astype(F32)
    labr[...] = lc
    labs[...] = jnp.broadcast_to(jnp.transpose(lc)[:, 0:1], (span, LANE))


def tile_range(len_ref, b, first, last, span, mols):
    lo = jnp.int32(0)
    hi = jnp.int32(span)
    end = jnp.int32(0)
    for m in range(mols):
        end = end + len_ref[b, m]
        lo = jnp.where(end <= first, end, lo)
        hi = jnp.where((end > last) & (end < hi), end, hi)
    return lo // LANE, (hi + LANE - 1) // LANE


def row_of(block, r):
    return jnp.broadcast_to(block[r:r + 1], (SUB, LANE))


def gauss_tile(drow):
    sub = lax.broadcasted_iota(jnp.int32, (SUB, LANE), 0).astype(F32) * KS
    base = drow - sub
    parts = []
    for c in range(KERN // SUB):
        t = base - (KS * SUB * c)
        parts.append(jnp.exp2(-(t * t)))
    return jnp.concatenate(parts, 0).astype(BF16)


def wide(ref, rows):
    return jnp.concatenate([ref[t, rows, :] for t in range(ref.shape[0])], 1)


def fwd_kernel(heads, mols, len_ref, coords_ref, qkv_ref, w_ref, o_ref, p_ref, dist, labs, labr, sc):
    hd, span = qkv_ref.shape[2:]
    b = pl.program_id(0)
    scale = 1.0 / math.sqrt(hd)
    pair_distances(coords_ref, dist, span)
    pair_labels(len_ref, b, labs, labr, span, mols)
    wb = w_ref[...]
    step = LANE

    def fill(i, carry):
        r0 = pl.multiple_of(i * step, step)
        sc[:, pl.ds(r0, step), :] = jnp.full((span // LANE, step, LANE), -1e30, F32)
        return carry

    lax.fori_loop(0, SUB * span // step, fill, 0)

    def group(g, carry):
        i0 = pl.multiple_of(g * TALL, TALL)
        lo, hi = tile_range(len_ref, b, i0, i0 + TALL - 1, span, mols)

        def tile(jt, carry):
            j0 = pl.multiple_of(jt * LANE, LANE)
            lab = labr[:, pl.ds(j0, LANE)]
            dblk = dist[pl.ds(i0, TALL), pl.ds(j0, LANE)]
            lblk = labs[pl.ds(i0, TALL), :]
            for r in range(0, TALL, 2):
                bias = mm(wb, jnp.concatenate([gauss_tile(row_of(dblk, r)), gauss_tile(row_of(dblk, r + 1))], 1))
                for k in range(2):
                    sc[jt, pl.ds(i0 + r + k, SUB, span), :] = jnp.where(
                        row_of(lblk, r + k) == lab, bias[:, k * LANE:(k + 1) * LANE], -1e30)
            return carry

        return lax.fori_loop(lo, hi, tile, carry)

    lax.fori_loop(0, span // TALL, group, 0)

    def head(h, carry):
        for c in range(span // step):
            cols = pl.ds(c * step, step)
            rows = pl.ds(pl.multiple_of(h * span + c * step, step), step)
            s = mm(qkv_ref[0, h, :, cols], qkv_ref[1, h], TN) * scale + wide(sc, rows)
            e = jnp.exp(s - jnp.max(s, axis=-1, keepdims=True))
            p = (e * (1.0 / jnp.sum(e, axis=-1, keepdims=True))).astype(BF16)
            p_ref[rows, :] = p
            o_ref[h, :, cols] = mm(qkv_ref[2, h], p, NT).astype(BF16)
        return carry

    lax.fori_loop(0, heads, head, 0)


def attention(qkv, coords, lengths, pair_low):
    _, heads, hd, rows = qkv.shape
    blocks, mols = lengths.shape
    span = rows // blocks
    w = jnp.pad(pair_low, ((0, SUB - heads), (0, 0)))
    return pl.pallas_call(
        functools.partial(fwd_kernel, heads, mols),
        out_shape=(jax.ShapeDtypeStruct((heads, hd, rows), BF16),
                   jax.ShapeDtypeStruct((blocks * heads * span, span), BF16)),
        grid_spec=pltpu.PrefetchScalarGridSpec(
            num_scalar_prefetch=1, grid=(blocks,),
            in_specs=[pl.BlockSpec((3, span), lambda b, *_: (0, b)),
                      pl.BlockSpec((3, heads, hd, span), lambda b, *_: (0, 0, 0, b)),
                      pl.BlockSpec((SUB, KERN), lambda b, *_: (0, 0))],
            out_specs=[pl.BlockSpec((heads, hd, span), lambda b, *_: (0, 0, b)),
                       pl.BlockSpec((heads * span, span), lambda b, *_: (b, 0))],
            scratch_shapes=[pltpu.VMEM((span, span), F32), pltpu.VMEM((span, LANE), F32),
                            pltpu.VMEM((SUB, span), F32), pltpu.VMEM((span // LANE, SUB * span, LANE), F32)]),
        cost_estimate=pl.CostEstimate(flops=20 * heads * hd * rows * span, bytes_accessed=8 * rows * span,
                                      transcendentals=KERN * rows * span),
        compiler_params=pltpu.CompilerParams(vmem_limit_bytes=ATTEND_MIB << 20),
        name="attend",
    )(lengths, coords, qkv, w)


def back_pairs(heads, coords_ref, qkv_ref, do_ref, p_ref, dqkv_ref, dist, ds, beside, between):
    hd, span = do_ref.shape[1:]
    scale = 1.0 / math.sqrt(hd)
    step = LANE
    pair_distances(coords_ref, dist, span)
    if heads < SUB:
        ds[...] = jnp.zeros_like(ds)

    def head(h, carry):
        beside(h, 0, heads)
        dk = jnp.zeros((hd, span), F32)
        dv = jnp.zeros((hd, span), F32)
        for c in range(span // step):
            cols = pl.ds(c * step, step)
            rows = pl.ds(pl.multiple_of(h * span + c * step, step), step)
            pb = p_ref[rows, :]
            p = pb.astype(F32)
            dp = mm(do_ref[h, :, cols], qkv_ref[2, h], TN)
            d = p * (dp - jnp.sum(p * dp, axis=-1, keepdims=True))
            for t in range(span // LANE):
                ds[t, rows, :] = d[:, t * LANE:(t + 1) * LANE]
            low = d.astype(BF16)
            dqkv_ref[0, h, :, cols] = (mm(qkv_ref[1, h], low, NT) * scale).astype(BF16)
            dk = dk + mm(qkv_ref[0, h, :, cols], low)
            dv = dv + mm(do_ref[h, :, cols], pb)
        dqkv_ref[1, h] = (dk * scale).astype(BF16)
        dqkv_ref[2, h] = dv.astype(BF16)
        return carry

    lax.fori_loop(0, heads, head, 0)
    between()

    def group(g, acc):
        beside(100 + g, 100, 100 + span // SUB)
        i0 = pl.multiple_of(g * SUB, SUB)

        left, right = [], []
        for jt in range(span // LANE):
            dblk = dist[pl.ds(i0, SUB), jt * LANE:(jt + 1) * LANE]
            for r in range(SUB // 2):
                pair = (r, r + SUB // 2)
                left.append(jnp.concatenate([ds[jt, pl.ds(i0 + k, SUB, span), :] for k in pair], 0).astype(BF16))
                right.append(jnp.concatenate([gauss_tile(row_of(dblk, k)) for k in pair], 0))
        return acc + mm(jnp.concatenate(left, 1), jnp.concatenate(right, 1), NT)

    acc = lax.fori_loop(0, span // SUB, group, jnp.zeros((2 * SUB, 2 * KERN), F32))
    return acc[:SUB, :KERN] + acc[SUB:, KERN:]


def bwd_kernel(heads, coords_ref, qkv_ref, do_ref, p_ref, dqkv_ref, pair_ref, dist, ds):
    @pl.when(pl.program_id(0) == 0)
    def _():
        pair_ref[...] = jnp.zeros_like(pair_ref)

    pair_ref[...] += back_pairs(heads, coords_ref, qkv_ref, do_ref, p_ref, dqkv_ref, dist, ds,
                                lambda *_: None, lambda: None)


def attention_back(qkv, do, probs, coords):
    _, heads, hd, rows = qkv.shape
    span = probs.shape[1]
    wide = pl.BlockSpec((3, heads, hd, span), lambda b: (0, 0, 0, b))
    return pl.pallas_call(
        functools.partial(bwd_kernel, heads),
        out_shape=(jax.ShapeDtypeStruct(qkv.shape, BF16), jax.ShapeDtypeStruct((SUB, KERN), F32)),
        grid=(rows // span,),
        in_specs=[pl.BlockSpec((3, span), lambda b: (0, b)), wide,
                  pl.BlockSpec((heads, hd, span), lambda b: (0, 0, b)),
                  pl.BlockSpec((heads * span, span), lambda b: (b, 0))],
        out_specs=[wide, pl.BlockSpec((SUB, KERN), lambda b: (0, 0))],
        scratch_shapes=[pltpu.VMEM((span, span), F32), pltpu.VMEM((span // LANE, SUB * span, LANE), F32)],
        compiler_params=pltpu.CompilerParams(vmem_limit_bytes=60 << 20),
        name="attend_back",
    )(coords, qkv, do, probs)


def mm(a, b, dims=NN):
    return lax.dot_general(a, b, dims, preferred_element_type=F32)


def remote(src, dst, send, recv, axis, target):
    return pltpu.make_async_remote_copy(
        src_ref=src, dst_ref=dst, send_sem=send, recv_sem=recv,
        device_id={axis: target}, device_id_type=MESH)


def greet(sizes, others=()):
    barrier = pltpu.get_barrier_semaphore()
    total = len(others)
    for place in others:
        pl.semaphore_signal(barrier, inc=1, device_id={"dp": place}, device_id_type=MESH)
    for axis, size in sizes.items():
        me = lax.axis_index(axis)
        for k in range(1, size):
            pl.semaphore_signal(barrier, inc=1, device_id={axis: lax.rem(me + k, size)}, device_id_type=MESH)
        total += size - 1
    pl.semaphore_wait(barrier, total)


class Seat:
    def __init__(self, n):
        self.n, self.nx = n, n // 2
        self.me = lax.axis_index("mp")
        self.core = lax.rem(self.me, 2)
        self.x = self.me // 2
        self.sib = self.me + 1 - 2 * self.core

    def chip(self, k):
        return lax.rem(self.x + 1 + k, self.nx)

    def source(self, k):
        return lax.rem(self.x + self.nx - 1 - k, self.nx)


class Grid:
    def __init__(self, ny, nz):
        self.ny, self.nz = ny, nz
        self.me = lax.axis_index("dp")
        self.z, self.y = self.me // ny, lax.rem(self.me, ny)
        self.nh, self.a, self.p = nz // 2, self.z // 2, lax.rem(self.z, 2)
        self.near = self.z + 1 - 2 * self.p

    def at(self, z, y):
        return z * self.ny + y

    def other(self, k):
        return lax.rem(self.a + 1 + k, self.nh)

    def far(self, k):
        return 2 * self.other(k) + self.p

    def yto(self, k):
        return lax.rem(self.y + 1 + k, self.ny)


def scatter_scratch(n, rows, width):
    nx = n // 2
    buf = lambda m: pltpu.VMEM((m, rows, width), BF16)
    return [buf(nx), buf(nx), buf(max(nx - 1, 1)), buf(max(nx - 1, 1)), DMA((nx,)), DMA((nx,)),
            DMA((max(nx - 1, 1),)), DMA((max(nx - 1, 1),))]


class Scatter:
    def __init__(self, seat, scratch):
        self.seat = seat
        self.out1, self.in1, self.out2, self.in2, self.s1, self.r1, self.s2, self.r2 = scratch

    def first(self, k):
        return remote(self.out1.at[k], self.in1.at[k], self.s1.at[k], self.r1.at[k], "mp", self.seat.sib)

    def second(self, k):
        target = self.seat.chip(k) * 2 + self.seat.core
        return remote(self.out2.at[k], self.in2.at[k], self.s2.at[k], self.r2.at[k], "mp", target)

    def push(self, block):
        for k in range(self.seat.nx):
            self.out1[k] = block(self.seat.chip(k) * 2 + 1 - self.seat.core).astype(BF16)
            self.first(k).start()

    def pass_on(self, block):
        seat = self.seat
        parts = [block(seat.chip(k) * 2 + seat.core) for k in range(seat.nx)]
        for k in range(seat.nx):
            self.first(k).wait_recv()
            whole = parts[k] + self.in1[k].astype(F32)
            if k < seat.nx - 1:
                self.out2[k] = whole.astype(BF16)
                self.second(k).start()
        return whole

    def finish(self, whole):
        for k in range(self.seat.nx - 1):
            self.second(k).wait_recv()
            whole = whole + self.in2[k].astype(F32)
        return whole

    def drain(self):
        for k in range(self.seat.nx):
            self.first(k).wait_send()
        for k in range(self.seat.nx - 1):
            self.second(k).wait_send()


def gather_scratch(n):
    nx = n // 2
    return [DMA((max(nx - 1, 1),)), DMA((max(nx - 1, 1),)), DMA((nx,)), DMA((nx,))]


class Gather:
    def __init__(self, seat, rows, scratch):
        self.seat, self.rows = seat, rows
        self.sx, self.rx, self.sc, self.rc = scratch

    def across(self, k):
        r = self.rows.at[self.seat.me]
        return remote(r, r, self.sx.at[k], self.rx.at[k], "mp", self.seat.chip(k) * 2 + self.seat.core)

    def along(self, k):
        chip = self.seat.x if k == self.seat.nx - 1 else self.seat.source(k)
        r = self.rows.at[chip * 2 + self.seat.core]
        return remote(r, r, self.sc.at[k], self.rc.at[k], "mp", self.seat.sib)

    def start(self):
        for k in range(self.seat.nx - 1):
            self.across(k).start()
        self.along(self.seat.nx - 1).start()

    def forward(self):
        for k in range(self.seat.nx - 1):
            self.across(k).wait_recv()
            self.along(k).start()

    def finish(self):
        for k in range(self.seat.nx):
            self.along(k).wait_recv()

    def drain(self):
        for k in range(self.seat.nx - 1):
            self.across(k).wait_send()
        for k in range(self.seat.nx):
            self.along(k).wait_send()


def centre(rows):
    c = rows - jnp.mean(rows, axis=-1, keepdims=True)
    r = lax.rsqrt(jnp.mean(c * c, axis=-1, keepdims=True) + ln_eps)
    return c * r, r


def norm_back(rows, gain, e):
    vhat, r = centre(rows)
    ge = e * gain
    dv = r * (ge - jnp.mean(ge, axis=-1, keepdims=True) - vhat * jnp.mean(ge * vhat, axis=-1, keepdims=True))
    return dv, jnp.sum(e * vhat, axis=0, keepdims=True), jnp.sum(e, axis=0, keepdims=True)


def enter_kernel(n, x_ref, np_ref, w_hbm, h_ref, qkv_ref, w32, wsem, *sems):
    seat = Seat(n)
    load = pltpu.make_async_copy(w_hbm, w32, wsem)
    load.start()
    greet({"mp": n})
    vhat, _ = centre(x_ref[...].astype(F32))
    h_ref[seat.me] = (vhat * np_ref[0:1] + np_ref[1:2]).astype(BF16)
    gh = Gather(seat, h_ref, sems)
    gh.start()
    load.wait()
    gh.forward()
    gh.finish()
    rows = h_ref.shape[1]
    for s in range(3):
        w = w32[s].astype(BF16)

        def block(b, carry):
            out = mm(w, h_ref[b], NT)
            qkv_ref[s, :, :, pl.ds(pl.multiple_of(b * rows, rows), rows)] = out.reshape(
                *qkv_ref.shape[1:3], rows).astype(BF16)
            return carry

        lax.fori_loop(0, n, block, 0)
    gh.drain()


def enter(n, heads, x, params, qkv_weight):
    rows, width = x.shape
    _, inner, _ = qkv_weight.shape
    return pl.pallas_call(
        functools.partial(enter_kernel, n),
        out_shape=(jax.ShapeDtypeStruct((n, rows, width), BF16),
                   jax.ShapeDtypeStruct((3, heads, inner // heads, n * rows), BF16)),
        in_specs=[VM, VM, HBM], out_specs=[VM, VM],
        scratch_shapes=[pltpu.VMEM(qkv_weight.shape, F32), DMA, *gather_scratch(n)],
        compiler_params=pltpu.CompilerParams(collective_id=0, has_side_effects=True, vmem_limit_bytes=60 << 20),
        name="enter",
    )(x, params, qkv_weight)


def middle_kernel(n, ny, nz, pushes, x_ref, o_ref, np_ref, bias_ref, pw_hbm, iw_hbm, ow_hbm, *rest):
    dys, rest = rest[:n], rest[n:]
    (block_ref, mid_ref, do_ref, og_ref, ig_ref, pg_ref, bg_ref, small_ref), rest = rest[:8], rest[8:]
    lands, rest = rest[:pushes], rest[pushes:]
    (pw32, iw32, ow32, pw, iw, ow, h2, da, act, dpre, dact, dyall_ref, wsem), rest = rest[:13], rest[13:]
    seat, grid = Seat(n), Grid(ny, nz)
    dy_ref = dys[0]
    rows, width = x_ref.shape
    loads = [pltpu.make_async_copy(a, b, wsem.at[i])
             for i, (a, b) in enumerate([(pw_hbm, pw32), (ow_hbm, ow32), (iw_hbm, iw32)])]
    for c in loads:
        c.start()
    scat = [Scatter(seat, rest[8 * i:8 * i + 8]) for i in range(3)]
    gath = [Gather(seat, r, rest[24 + 4 * i:28 + 4 * i]) for i, r in enumerate((h2, da))]
    places = [grid.z * ny + grid.yto(k) for k in range(ny - 1)]
    greet({"mp": n}, places if pushes else ())

    def ahead(i, k):
        part = (og_ref, ig_ref)[i // PARTS]
        tall = part.shape[0] // (PARTS * ny)
        start = pl.multiple_of(((i % PARTS) * ny + grid.yto(k)) * tall, 16)
        return remote(part.at[pl.ds(start, tall), :], lands[i].at[k], rest[32].at[i, k], rest[33].at[i, k],
                      "dp", places[k])

    copies = [[ahead(i, k) for k in range(ny - 1)] for i in range(pushes)]
    for k in range(n):
        dyall_ref[lax.rem(seat.me + k, n)] = dys[k][...]
    at = lambda b: pl.ds(pl.multiple_of(b * rows, rows), rows)

    loads[0].wait()
    pw[...] = pw32[...].astype(BF16)
    attn_block = lambda b: mm(o_ref[:, at(b)], pw[...], TN)
    scat[0].push(attn_block)
    loads[1].wait()
    ow[...] = ow32[...].astype(BF16)
    whole = scat[0].pass_on(attn_block)
    loads[2].wait()
    iw[...] = iw32[...].astype(BF16)

    def back_act(b, carry):
        dact[b] = mm(dyall_ref[b], ow[...], NT)
        return carry

    lax.fori_loop(0, n, back_act, 0)
    mid = x_ref[...].astype(F32) + scat[0].finish(whole)
    vhat, _ = centre(mid)
    h2[seat.me] = (vhat * np_ref[2:3] + np_ref[3:4]).astype(BF16)
    mid_ref[...] = mid
    gath[0].start()
    gath[0].forward()
    gath[0].finish()

    bg_ref[...] = jnp.zeros_like(bg_ref)
    bias = bias_ref[...].astype(BF16).astype(F32)

    def feed_block(b):
        pre = mm(h2[b], iw[...], NT) + bias
        phi = 0.5 + 0.5 * lax.erf(pre * math.sqrt(0.5))
        act[b] = (pre * phi).astype(BF16)
        slope = phi + pre * (jnp.exp(-0.5 * pre * pre) * (1.0 / math.sqrt(2.0 * math.pi)))
        d = (dact[b] * slope).astype(BF16)
        dpre[b] = d
        bg_ref[...] += jnp.sum(d.astype(F32), axis=0, keepdims=True)
        return mm(d, iw[...])

    scat[1].push(feed_block)
    whole = scat[1].pass_on(feed_block)
    hidden = iw.shape[0]
    step = LANE if hidden % LANE == 0 else hidden

    def grads(left, right, out, first):
        def columns(i, carry):
            c0 = pl.multiple_of(i * step, step)
            acc = jnp.zeros((step, width), F32)
            for b in range(n):
                acc += mm(left[b, :, pl.ds(c0, step)], right[b], TN)
            out[pl.ds(c0, step), :] = acc.astype(BF16)
            return carry

        lax.fori_loop(0, hidden // step, columns, 0)
        for piece in copies[first:first + PARTS]:
            for copy in piece:
                copy.start()

    grads(act, dyall_ref, og_ref, 0)
    out_block = lambda b: mm(act[b], ow[...])
    scat[2].push(out_block)
    dh2 = scat[1].finish(whole)
    dv, gain, shift = norm_back(mid_ref[...], np_ref[2:3], dh2)
    dy = dy_ref[...].astype(F32)
    dx1 = dy + dv
    da[seat.me] = dx1.astype(BF16)
    gath[1].start()
    small_ref[...] = jnp.concatenate(
        [gain, shift, jnp.sum(dy, axis=0, keepdims=True), jnp.zeros((5, width), F32)], 0)
    whole = scat[2].pass_on(out_block)
    gath[1].forward()
    grads(dpre, h2, ig_ref, PARTS)
    block_ref[...] = mid_ref[...] + scat[2].finish(whole) + np_ref[4:5]
    mid_ref[...] = dx1
    gath[1].finish()

    def heads_block(b, acc):
        out = mm(pw[...], da[b], NT)
        do_ref[:, :, at(b)] = out.reshape(*do_ref.shape[:2], rows).astype(BF16)
        return acc + mm(o_ref[:, at(b)], da[b])

    pg_ref[...] = lax.fori_loop(0, n, heads_block, jnp.zeros(pg_ref.shape, F32)).astype(BF16)
    for c in scat + gath:
        c.drain()
    for piece in copies:
        for copy in piece:
            copy.wait()


PARTS = 2
MIDDLE_MIB = 24


def middle(n, ny, nz, pushes, x, dys, o, params, bias, proj_weight, in_weight, out_weight):
    rows, width = x.shape
    hidden = in_weight.shape[0]
    inner = proj_weight.shape[0]
    heads, hd, _ = o.shape
    f = lambda *s: jax.ShapeDtypeStruct(s, F32)
    return pl.pallas_call(
        functools.partial(middle_kernel, n, ny, nz, pushes),
        out_shape=(f(rows, width), f(rows, width), jax.ShapeDtypeStruct(o.shape, BF16),
                   *[jax.ShapeDtypeStruct((t, width), BF16) for t in (hidden, hidden, inner)], f(1, hidden), f(8, width),
                   *[jax.ShapeDtypeStruct((ny - 1, hidden // (PARTS * ny), width), BF16)] * pushes),
        in_specs=[VM] * 4 + [HBM] * 3 + [VM] * n, out_specs=[VM] * (8 + pushes),
        scratch_shapes=[pltpu.VMEM((inner, width), F32), pltpu.VMEM((hidden, width), F32),
                        pltpu.VMEM((hidden, width), F32), pltpu.VMEM((inner, width), BF16),
                        pltpu.VMEM((hidden, width), BF16), pltpu.VMEM((hidden, width), BF16),
                        pltpu.VMEM((n, rows, width), BF16), pltpu.VMEM((n, rows, width), BF16),
                        pltpu.VMEM((n, rows, hidden), BF16), pltpu.VMEM((n, rows, hidden), BF16),
                        pltpu.VMEM((n, rows, hidden), F32), pltpu.VMEM((n, rows, width), BF16), DMA((3,)),
                        *[s for _ in range(3) for s in scatter_scratch(n, rows, width)],
                        *gather_scratch(n), *gather_scratch(n),
                        *[DMA((max(pushes, 1), max(ny - 1, 1)))] * 2],
        compiler_params=pltpu.CompilerParams(collective_id=1, has_side_effects=True, vmem_limit_bytes=MIDDLE_MIB << 20),
        name="middle",
    )(x, o.reshape(inner, -1), params, bias, proj_weight, in_weight, out_weight, *dys)


def sum_scratch(shape):
    ny, _, nh, chunk, width = shape
    y, f = max(ny - 1, 1), max(nh - 1, 1)
    return [pltpu.VMEM((y, 2, nh, chunk, width), BF16), pltpu.VMEM((nh, chunk, width), F32),
            pltpu.VMEM((nh, chunk, width), BF16), pltpu.VMEM((nh, chunk, width), BF16),
            pltpu.VMEM((f, chunk, width), BF16), pltpu.VMEM((f, chunk, width), BF16),
            DMA((y,)), DMA((y,)), DMA((1,)), DMA((1,)), DMA((f,)), DMA((f,))]


class Sum:
    count = 12

    def __init__(self, grid, grad, own, scratch):
        self.grid, self.grad, self.own, self.pushed = grid, grad, own, True
        (self.ia, self.keep, self.ob, self.ib, self.oc, self.ic,
         self.sa, self.ra, self.sb, self.rb, self.sc, self.rc) = scratch

    def copy_y(self, k):
        g = self.grid
        return remote(self.grad.at[g.yto(k)], self.ia.at[k], self.sa.at[k], self.ra.at[k], "dp", g.at(g.z, g.yto(k)))

    def copy_near(self):
        g = self.grid
        return remote(self.ob, self.ib, self.sb.at[0], self.rb.at[0], "dp", g.at(g.near, g.y))

    def copy_far(self, k):
        g = self.grid
        return remote(self.oc.at[k], self.ic.at[k], self.sc.at[k], self.rc.at[k], "dp", g.at(g.far(k), g.y))

    def push(self):
        for k in range(self.grid.ny - 1):
            self.copy_y(k).start()

    def half(self, p):
        g = self.grid
        whole = self.grad[g.y, p].astype(F32)
        for k in range(g.ny - 1):
            whole = whole + self.ia[k, p].astype(F32)
        return whole

    def near(self):
        g = self.grid
        for k in range(g.ny - 1 if self.pushed else 0):
            self.copy_y(k).wait_recv()
        self.ob[...] = self.half(1 - g.p).astype(BF16)
        self.copy_near().start()
        self.keep[...] = self.half(g.p)

    def far(self):
        g = self.grid
        self.copy_near().wait_recv()
        for k in range(g.nh - 1):
            a = g.other(k)
            self.oc[k] = (self.keep[a] + self.ib[a].astype(F32)).astype(BF16)
            self.copy_far(k).start()
        self.own[...] = self.keep[g.a] + self.ib[g.a].astype(F32)

    def collect(self):
        whole = self.own[...]
        for k in range(self.grid.nh - 1):
            self.copy_far(k).wait_recv()
            whole = whole + self.ic[k].astype(F32)
        self.own[...] = whole

    def drain(self):
        g = self.grid
        for k in range(g.ny - 1 if self.pushed else 0):
            self.copy_y(k).wait_send()
        self.copy_near().wait_send()
        for k in range(g.nh - 1):
            self.copy_far(k).wait_send()


def spread_scratch(ny, nz):
    y, f = max(ny - 1, 1), max(nz // 2 - 1, 1)
    return [DMA((f,)), DMA((f,)), DMA((1,)), DMA((1,)), DMA((2, y)), DMA((2, y))]


class Spread:
    count = 6

    def __init__(self, grid, own, result, scratch):
        self.grid, self.own, self.result = grid, own, result
        self.sf, self.rf, self.sn, self.rn, self.sy, self.ry = scratch

    def to_far(self, k):
        g = self.grid
        r = self.result.at[g.y, g.p, g.a]
        return remote(r, r, self.sf.at[k], self.rf.at[k], "dp", g.at(g.far(k), g.y))

    def to_near(self):
        g = self.grid
        r = self.result.at[g.y, g.p]
        return remote(r, r, self.sn.at[0], self.rn.at[0], "dp", g.at(g.near, g.y))

    def to_y(self, i, k):
        g = self.grid
        r = self.result.at[g.y, g.p if i == 0 else 1 - g.p]
        return remote(r, r, self.sy.at[i, k], self.ry.at[i, k], "dp", g.at(g.z, g.yto(k)))

    def start(self):
        g = self.grid
        whole = self.own[...]
        self.result[g.y, g.p, g.a] = whole.astype(BF16)
        for k in range(g.nh - 1):
            self.to_far(k).start()
        return square(whole)

    def second(self):
        g = self.grid
        for k in range(g.nh - 1):
            self.to_far(k).wait_recv()
        self.to_near().start()
        for k in range(g.ny - 1):
            self.to_y(0, k).start()

    def third(self):
        self.to_near().wait_recv()
        for k in range(self.grid.ny - 1):
            self.to_y(1, k).start()

    def close(self):
        g = self.grid
        for i in range(2):
            for k in range(g.ny - 1):
                self.to_y(i, k).wait()
        for k in range(g.nh - 1):
            self.to_far(k).wait_send()
        self.to_near().wait_send()


def take(rest, cls, count):
    size = cls.count
    return [rest[size * i:size * (i + 1)] for i in range(count)], rest[size * count:]


class Share:
    def __init__(self, axis, slots, send, recv):
        self.axis, self.slots, self.send, self.recv = axis, slots, send, recv
        self.size = slots.shape[0]
        self.me = lax.axis_index(axis)

    def copy(self, k):
        r = self.slots.at[self.me]
        return remote(r, r, self.send.at[k], self.recv.at[k], self.axis, lax.rem(self.me + 1 + k, self.size))

    def start(self, value):
        self.slots[self.me] = value
        for k in range(self.size - 1):
            self.copy(k).start()

    def total(self):
        for k in range(self.size - 1):
            self.copy(k).wait_recv()
        out = self.slots[0]
        for i in range(1, self.size):
            out = out + self.slots[i]
        return out

    def drain(self):
        for k in range(self.size - 1):
            self.copy(k).wait_send()


def share_scratch(size, rows, width):
    return [pltpu.VMEM((size, rows, width), F32), DMA((max(size - 1, 1),)), DMA((max(size - 1, 1),))]


def square(v):
    return jnp.sum(jnp.sum(v * v, axis=1, keepdims=True), axis=0, keepdims=True)


NEAR_AT = (-1, -1, 5, 100, 105, 113, 120, 128)
FAR_AT = (2, 5, 99, 111, 113, 123, 131, 140)
COLLECT_AT = (7, 99, 106, 123, 124, 133, 144, 154)
SECOND_AT = (101, 110, 120, 139, 140, 149, 159, 167)
THIRD_AT = (114, 126, 139, 154, 157, 168, 168, 168)
NORM_AT = 118
SMALL_AT = 130
REAR_MIB = 36


def rear_kernel(n, ny, nz, pushes, coords_ref, qkv_ref, do_ref, p_ref, og_ref, ig_ref, pg_ref, x_ref, dx_ref, np_ref,
                h_ref, bg_ref, mid_small_ref, w_hbm, *rest):
    lands, rest = rest[:pushes], rest[pushes:]
    early = 2 * PARTS + 1
    results, (sq_ref, gi_ref, small_ref, bias_ref, pairs_ref, norm_ref), rest = rest[:early], rest[early:early + 6], rest[early + 6:]
    (dist, ds, dqkv, flat, w32, w, qg, qown, kept, squares, wsem), rest = rest[:11], rest[11:]
    owns, rest = rest[:early], rest[early:]
    _, heads, hd, span = qkv_ref.shape
    inner = heads * hd
    rows, width = x_ref.shape
    seat, grid = Seat(n), Grid(ny, nz)
    pieces = [g.at[i] for g in (og_ref, ig_ref) for i in range(PARTS)] + [pg_ref] + [qg.at[s] for s in range(3)]
    places = [*owns, *[qown.at[s] for s in range(3)]]
    targets = [*results, *[sq_ref.at[s] for s in range(3)]]
    scat, rest = Scatter(seat, rest[:8]), rest[8:]
    scratch, rest = take(rest, Sum, early + 3)
    sums = [Sum(grid, *a) for a in zip(pieces, places, scratch)]
    scratch, rest = take(rest, Spread, early + 3)
    spreads = [Spread(grid, *a) for a in zip(places, targets, scratch)]
    shares = [Share(a, *rest[3 * i:3 * i + 3]) for i, a in enumerate(("mp", "dp", "dp", "dp", "mp", "dp"))]
    small_mp, small_dp, bias_dp, pair_dp, sq_mp, sq_dp = shares
    for s, land in zip(sums, lands):
        s.ia, s.pushed = land, False
    at = lambda b: pl.ds(pl.multiple_of(b * rows, rows), rows)
    load = pltpu.make_async_copy(w_hbm, w32, wsem)
    load.start()
    greet({"mp": n, "dp": ny * nz})
    for s in sums[pushes:early]:
        s.push()
    squares[...] = jnp.zeros_like(squares)

    def collect(i):
        sums[i].collect()
        squares[...] += spreads[i].start()

    def project():
        for s in range(3):
            flat[s] = dqkv[s].astype(F32).reshape(inner, span).astype(BF16)
            acc = jnp.zeros((inner, width), F32)
            for b in range(n):
                acc = acc + mm(flat[s, :, at(b)], h_ref[b])
            qg[s] = acc.reshape(qg.shape[1:]).astype(BF16)
            sums[early + s].push()
        load.wait()
        w[...] = w32[...].astype(BF16)
        block = lambda b: sum(mm(flat[s, :, at(b)], w[s], TN) for s in range(3))
        scat.push(block)
        kept[...] = scat.pass_on(block)
        bias_dp.start(jnp.broadcast_to(bg_ref[...], bias_dp.slots.shape[1:]))

    def norm():
        dh1 = scat.finish(kept[...])
        dv, gain, shift = norm_back(x_ref[...].astype(F32), np_ref[0:1], dh1)
        gi_ref[...] = dx_ref[...] + dv
        small_mp.start(jnp.concatenate([gain, shift, mid_small_ref[0:6]], 0))

    jobs = {99: [project], NORM_AT: [norm], SMALL_AT: [lambda: small_dp.start(small_mp.total())]}
    for i, s in enumerate(sums):
        for when, job in ((NEAR_AT[i], s.near), (FAR_AT[i], s.far), (COLLECT_AT[i], functools.partial(collect, i)),
                          (SECOND_AT[i], spreads[i].second), (THIRD_AT[i], spreads[i].third)):
            jobs.setdefault(when, []).append(job)

    def now(first, end):
        for when in sorted(jobs):
            if first <= when < end:
                for job in jobs[when]:
                    job()

    def beside(step, first, end):
        for when in sorted(jobs):
            if first <= when < end:
                @pl.when(step == when)
                def _():
                    for job in jobs[when]:
                        job()

    now(-1, 0)
    pair = back_pairs(heads, coords_ref, qkv_ref, do_ref, p_ref, dqkv, dist, ds, beside, lambda: now(99, 100))
    pair_dp.start(pair)
    last = 100 + span // SUB
    now(last, last + 4)
    bias = bias_dp.total()
    bias_ref[...] = bias
    small = small_dp.total()
    small_ref[...] = small
    pairs = pair_dp.total()
    pairs_ref[...] = pairs
    row = lax.broadcasted_iota(jnp.int32, (8, LANE), 0)
    local = square(bias[0:1]) + square(pairs)
    sq_mp.start(jnp.where(row == 0, squares[...], jnp.where(row == 1, local, 0.0)))
    now(last + 4, 1000)
    sq_dp.start(sq_mp.total())
    norm_ref[...] = sq_dp.total()[0:1] + sq_dp.slots[0, 1:2] + square(small)
    for s in spreads:
        s.close()
    for s in [scat] + sums + shares:
        s.drain()


def rear(n, ny, nz, qkv, do, probs, coords, og, ig, pg, lands, x, dx, params, h, bias_grad, small, qkv_weight):
    _, heads, hd, span = qkv.shape
    rows, width = x.shape
    inner, hidden = heads * hd, bias_grad.shape[1]
    ndp, pushes = ny * nz, len(lands)
    cut = lambda g, p: g.reshape(p, ny, 2, nz // 2, g.shape[0] // (p * ndp), width)
    lands = [v.reshape(ny - 1, 2, nz // 2, -1, width) for v in lands]
    og, ig, pg = cut(og, PARTS), cut(ig, PARTS), cut(pg, 1)[0]
    chunks = (3, ny, 2, nz // 2, inner // ndp, width)
    shapes = [og.shape[1:]] * PARTS + [ig.shape[1:]] * PARTS + [pg.shape]
    every = shapes + [chunks[1:]] * 3
    f = lambda *s: jax.ShapeDtypeStruct(s, F32)
    return pl.pallas_call(
        functools.partial(rear_kernel, n, ny, nz, pushes),
        out_shape=(*[jax.ShapeDtypeStruct(s, BF16) for s in (*shapes, chunks)],
                   f(rows, width), f(8, width), f(8, hidden), f(8, LANE), f(1, LANE)),
        in_specs=[VM] * 13 + [HBM] + [VM] * pushes, out_specs=[VM] * (len(shapes) + 6),
        scratch_shapes=[pltpu.VMEM((span, span), F32), pltpu.VMEM((span // LANE, SUB * span, LANE), F32),
                        pltpu.VMEM(qkv.shape, BF16), pltpu.VMEM((3, inner, span), BF16),
                        pltpu.VMEM(qkv_weight.shape, F32), pltpu.VMEM(qkv_weight.shape, BF16), pltpu.VMEM(chunks, BF16),
                        pltpu.VMEM((3, inner // ndp, width), F32), pltpu.VMEM((rows, width), F32),
                        pltpu.VMEM((1, LANE), F32), DMA, *[pltpu.VMEM(s[3:], F32) for s in shapes],
                        *scatter_scratch(n, rows, width),
                        *[v for s in every for v in sum_scratch(s)], *[v for _ in every for v in spread_scratch(ny, nz)],
                        *share_scratch(n, 8, width), *share_scratch(ndp, 8, width), *share_scratch(ndp, 8, hidden),
                        *share_scratch(ndp, 8, LANE), *share_scratch(n, 8, LANE), *share_scratch(ndp, 8, LANE)],
        compiler_params=pltpu.CompilerParams(collective_id=2, has_side_effects=True, vmem_limit_bytes=REAR_MIB << 20),
        name="rear",
    )(coords, qkv, do, probs, og, ig, pg, x, dx, params, h, bias_grad, small, qkv_weight, *lands)


def leave_plain(n, x, dx, params, dqkv, h, grads, bias_grad, pair_grad, small, qkv_weight):
    part = sum(mm(dqkv[s], qkv_weight[s].astype(BF16), TN) for s in range(3))
    dh1 = lax.psum_scatter(part, "mp", scatter_dimension=0, tiled=True)
    dv, gain, shift = norm_back(x.astype(F32), params[0:1], dh1)
    hh = h.reshape(-1, h.shape[-1])
    qg = jnp.concatenate([mm(dqkv[s], hh) for s in range(3)], 0)
    og, ig, pg, qg, bias, pair = lax.psum((*[g.astype(F32) for g in grads], qg, bias_grad, pair_grad), "dp")
    small = lax.psum(jnp.concatenate([gain, shift, small[0:6]], 0), ("dp", "mp"))
    local = sum(square(v) for v in (og, ig, pg, qg, bias, pair))
    total = lax.psum(local, "mp") + square(small)
    return dx + dv, og, ig, pg, qg, small, bias, pair, total


PUSHES = 2


def adam_step(weight, grad, first, second, clip, fix_one, fix_two, rate, decay):
    scaled = grad * clip
    first_new = beta_one * first + (1.0 - beta_one) * scaled
    second_new = beta_two * second + (1.0 - beta_two) * scaled * scaled
    ratio = first_new / fix_one / (jnp.sqrt(second_new / fix_two) + adam_eps)
    return (weight - rate * (ratio + decay * weight), first_new, second_new)


def per_device(n, ndp, block_in, coords, lengths, cotangent, step_count, *state):
    weights, firsts, seconds = state[:7], state[7:14], state[14:]
    qkv_weight, proj_weight, pair_weight, in_weight, in_bias, out_weight, params = weights
    heads = pair_weight.shape[0]
    pair_low = pair_weight.astype(BF16)
    h, qkv = enter(n, heads, block_in, params, qkv_weight)
    o, probs = attention(qkv, coords, lengths, pair_low)
    dy, _ = lax.optimization_barrier((cotangent, qkv))
    dys = [cotangent] + [lax.ppermute(dy, "mp", [((i + k) % n, i) for i in range(n)]) for k in range(1, n)]
    ny = n // 2 if ndp % (n // 2) == 0 else 1
    nz = ndp // ny
    inner, hidden = proj_weight.shape[0], in_weight.shape[0]
    beside = lengths.shape[0] == 1 and nz % 2 == 0 and inner % (8 * ndp) == 0 and hidden % (16 * PARTS * ndp) == 0
    block_out, dx, do, og, ig, pg, bg, small, *lands = middle(
        n, ny, nz, PUSHES if beside else 0, block_in, dys, o, params, in_bias.reshape(1, -1), proj_weight, in_weight, out_weight)
    if beside:
        *pieces, pg, qg, grad_input, small, bias, pair, total = rear(
            n, ny, nz, qkv, do, probs, coords, og, ig, pg, lands, block_in, dx, params, h, bg, small, qkv_weight)
        og, ig = pieces[:PARTS], pieces[PARTS:]
        og, ig = [jnp.concatenate([v.reshape(-1, v.shape[-1]) for v in g], 0) for g in (og, ig)]
    else:
        dqkv, pair_grad = attention_back(qkv, do, probs, coords)
        grad_input, og, ig, pg, qg, small, bias, pair, total = leave_plain(
            n, block_in, dx, params, dqkv.reshape(3, inner, -1), h, (og, ig, pg), bg, pair_grad, small, qkv_weight)
    grad_norm = jnp.sqrt(total[0, 0])
    clip = clip_level / jnp.maximum(grad_norm, clip_level)
    count = step_count[0].astype(F32)
    fix_one = 1.0 - jnp.power(beta_one, count)
    fix_two = 1.0 - jnp.power(beta_two, count)
    grads = (qg.reshape(qkv_weight.shape), pg.reshape(proj_weight.shape), pair[:heads], ig.reshape(in_weight.shape),
             bias[0], og.reshape(out_weight.shape), small[:5])
    rates = (0.9, 2.5, 7.5, 0.9, 7.5, 0.45, 3.0)
    decays = (0.01, 0.01, 0.01, 0.01, 0.0, 0.01, 0.0)
    outs = [block_out, grad_input, grad_norm.reshape(1)]
    for w, g, m, u, rate, decay in zip(weights, grads, firsts, seconds, rates, decays):
        outs.extend(adam_step(w, g.astype(F32), m, u, clip, fix_one, fix_two, rate, decay))
    return tuple(outs)


def solution(mesh):
    rows, mp = P(("dp", "mp"), None), P("mp", None)
    stacked = P(None, "mp", None)
    params = (stacked, mp, mp, mp, P("mp"), mp, P())
    in_specs = (rows, P(None, "dp"), P("dp", None), rows, P(), *params, *params, *params)
    out_specs = (rows, rows, P(), *[s for s in params for _ in range(3)])
    return jax.shard_map(
        functools.partial(per_device, mesh.shape["mp"], mesh.shape["dp"]),
        mesh=mesh, in_specs=in_specs, out_specs=out_specs, check_vma=False)
```

```python
import functools
import math

import jax
import jax.numpy as jnp
from jax import lax
from jax.experimental import pallas as pl
from jax.experimental.pallas import tpu as pltpu
from jax.sharding import PartitionSpec as P

ln_eps = 1e-05
beta_one = 0.9
beta_two = 0.999
adam_eps = 1e-08
clip_level = 1.0

F32, BF16 = jnp.float32, jnp.bfloat16
MESH = pl.DeviceIdType.MESH
NN = (((1,), (0,)), ((), ()))
NT = (((1,), (1,)), ((), ()))
TN = (((0,), (0,)), ((), ()))
VM = pl.BlockSpec(memory_space=pltpu.VMEM)
HBM = pl.BlockSpec(memory_space=pl.ANY)
DMA = pltpu.SemaphoreType.DMA
KERN = 128
LANE = 128
SUB = 8
TALL = 32
ATTEND_MIB = 20
KS = math.sqrt(0.5 * math.log2(math.e))
UNIT = KS / (12.8 / KERN)


def pair_distances(coords_ref, dist, span):
    pts = coords_ref[...]
    cols = jnp.transpose(jnp.concatenate([pts, jnp.zeros((5, span), F32)], 0))
    acc = None
    for a in range(3):
        d = cols[:, a:a + 1] - pts[a:a + 1, :]
        acc = d * d if acc is None else acc + d * d
    dist[...] = jnp.sqrt(acc) * UNIT


def pair_labels(len_ref, b, labs, labr, span, mols):
    lanes = lax.broadcasted_iota(jnp.int32, (SUB, span), 1)
    lc = jnp.zeros((SUB, span), F32)
    end = jnp.int32(0)
    for m in range(mols):
        end = end + len_ref[b, m]
        lc = lc + (lanes >= end).astype(F32)
    labr[...] = lc
    labs[...] = jnp.broadcast_to(jnp.transpose(lc)[:, 0:1], (span, LANE))


def tile_range(len_ref, b, first, last, span, mols):
    lo = jnp.int32(0)
    hi = jnp.int32(span)
    end = jnp.int32(0)
    for m in range(mols):
        end = end + len_ref[b, m]
        lo = jnp.where(end <= first, end, lo)
        hi = jnp.where((end > last) & (end < hi), end, hi)
    return lo // LANE, (hi + LANE - 1) // LANE


def row_of(block, r):
    return jnp.broadcast_to(block[r:r + 1], (SUB, LANE))


def gauss_tile(drow):
    sub = lax.broadcasted_iota(jnp.int32, (SUB, LANE), 0).astype(F32) * KS
    base = drow - sub
    parts = []
    for c in range(KERN // SUB):
        t = base - (KS * SUB * c)
        parts.append(jnp.exp2(-(t * t)))
    return jnp.concatenate(parts, 0).astype(BF16)


def wide(ref, rows):
    return jnp.concatenate([ref[t, rows, :] for t in range(ref.shape[0])], 1)


def fwd_kernel(heads, mols, len_ref, coords_ref, qkv_ref, w_ref, o_ref, p_ref, dist, labs, labr, sc):
    hd, span = qkv_ref.shape[2:]
    b = pl.program_id(0)
    scale = 1.0 / math.sqrt(hd)
    pair_distances(coords_ref, dist, span)
    pair_labels(len_ref, b, labs, labr, span, mols)
    wb = w_ref[...].astype(BF16)
    step = LANE

    def fill(i, carry):
        r0 = pl.multiple_of(i * step, step)
        sc[:, pl.ds(r0, step), :] = jnp.full((span // LANE, step, LANE), -1e30, F32)
        return carry

    lax.fori_loop(0, SUB * span // step, fill, 0)

    def group(g, carry):
        i0 = pl.multiple_of(g * TALL, TALL)
        lo, hi = tile_range(len_ref, b, i0, i0 + TALL - 1, span, mols)

        def tile(jt, carry):
            j0 = pl.multiple_of(jt * LANE, LANE)
            lab = labr[:, pl.ds(j0, LANE)]
            dblk = dist[pl.ds(i0, TALL), pl.ds(j0, LANE)]
            lblk = labs[pl.ds(i0, TALL), :]
            for r in range(0, TALL, 2):
                bias = mm(wb, jnp.concatenate([gauss_tile(row_of(dblk, r)), gauss_tile(row_of(dblk, r + 1))], 1))
                for k in range(2):
                    sc[jt, pl.ds(i0 + r + k, SUB, span), :] = jnp.where(
                        row_of(lblk, r + k) == lab, bias[:, k * LANE:(k + 1) * LANE], -1e30)
            return carry

        return lax.fori_loop(lo, hi, tile, carry)

    lax.fori_loop(0, span // TALL, group, 0)

    def head(h, carry):
        for c in range(span // step):
            cols = pl.ds(c * step, step)
            rows = pl.ds(pl.multiple_of(h * span + c * step, step), step)
            s = mm(qkv_ref[0, h, :, cols], qkv_ref[1, h], TN) * scale + wide(sc, rows)
            e = jnp.exp(s - jnp.max(s, axis=-1, keepdims=True))
            p = (e * (1.0 / jnp.sum(e, axis=-1, keepdims=True))).astype(BF16)
            p_ref[rows, :] = p
            o_ref[h, :, cols] = mm(qkv_ref[2, h], p, NT).astype(BF16)
        return carry

    lax.fori_loop(0, heads, head, 0)


def attention(qkv, coords, lengths, pair_weight):
    _, heads, hd, rows = qkv.shape
    blocks, mols = lengths.shape
    span = rows // blocks
    w = jnp.pad(pair_weight, ((0, SUB - heads), (0, 0))) if heads < SUB else pair_weight
    return pl.pallas_call(
        functools.partial(fwd_kernel, heads, mols),
        out_shape=(jax.ShapeDtypeStruct((heads, hd, rows), BF16),
                   jax.ShapeDtypeStruct((blocks * heads * span, span), BF16)),
        grid_spec=pltpu.PrefetchScalarGridSpec(
            num_scalar_prefetch=1, grid=(blocks,),
            in_specs=[pl.BlockSpec((3, span), lambda b, *_: (0, b)),
                      pl.BlockSpec((3, heads, hd, span), lambda b, *_: (0, 0, 0, b)),
                      pl.BlockSpec((SUB, KERN), lambda b, *_: (0, 0))],
            out_specs=[pl.BlockSpec((heads, hd, span), lambda b, *_: (0, 0, b)),
                       pl.BlockSpec((heads * span, span), lambda b, *_: (b, 0))],
            scratch_shapes=[pltpu.VMEM((span, span), F32), pltpu.VMEM((span, LANE), F32),
                            pltpu.VMEM((SUB, span), F32), pltpu.VMEM((span // LANE, SUB * span, LANE), F32)]),
        cost_estimate=pl.CostEstimate(flops=20 * heads * hd * rows * span, bytes_accessed=8 * rows * span,
                                      transcendentals=KERN * rows * span),
        compiler_params=pltpu.CompilerParams(vmem_limit_bytes=ATTEND_MIB << 20),
        name="attend",
    )(lengths, coords, qkv, w)


def back_pairs(heads, coords_ref, qkv_ref, do_ref, p_ref, dqkv_ref, dist, ds, beside, between):
    hd, span = do_ref.shape[1:]
    scale = 1.0 / math.sqrt(hd)
    step = LANE
    pair_distances(coords_ref, dist, span)
    if heads < SUB:
        ds[...] = jnp.zeros_like(ds)

    def head(h, carry):
        beside(h, 0, heads)
        dk = jnp.zeros((hd, span), F32)
        dv = jnp.zeros((hd, span), F32)
        for c in range(span // step):
            cols = pl.ds(c * step, step)
            rows = pl.ds(pl.multiple_of(h * span + c * step, step), step)
            pb = p_ref[rows, :]
            p = pb.astype(F32)
            dp = mm(do_ref[h, :, cols], qkv_ref[2, h], TN)
            d = p * (dp - jnp.sum(p * dp, axis=-1, keepdims=True))
            for t in range(span // LANE):
                ds[t, rows, :] = d[:, t * LANE:(t + 1) * LANE]
            low = d.astype(BF16)
            dqkv_ref[0, h, :, cols] = (mm(qkv_ref[1, h], low, NT) * scale).astype(BF16)
            dk = dk + mm(qkv_ref[0, h, :, cols], low)
            dv = dv + mm(do_ref[h, :, cols], pb)
        dqkv_ref[1, h] = (dk * scale).astype(BF16)
        dqkv_ref[2, h] = dv.astype(BF16)
        return carry

    lax.fori_loop(0, heads, head, 0)
    between()

    def group(g, acc):
        beside(100 + g, 100, 100 + span // SUB)
        i0 = pl.multiple_of(g * SUB, SUB)

        left, right = [], []
        for jt in range(span // LANE):
            dblk = dist[pl.ds(i0, SUB), jt * LANE:(jt + 1) * LANE]
            for r in range(SUB // 2):
                pair = (r, r + SUB // 2)
                left.append(jnp.concatenate([ds[jt, pl.ds(i0 + k, SUB, span), :] for k in pair], 0).astype(BF16))
                right.append(jnp.concatenate([gauss_tile(row_of(dblk, k)) for k in pair], 0))
        return acc + mm(jnp.concatenate(left, 1), jnp.concatenate(right, 1), NT)

    acc = lax.fori_loop(0, span // SUB, group, jnp.zeros((2 * SUB, 2 * KERN), F32))
    return acc[:SUB, :KERN] + acc[SUB:, KERN:]


def bwd_kernel(heads, coords_ref, qkv_ref, do_ref, p_ref, dqkv_ref, pair_ref, dist, ds):
    @pl.when(pl.program_id(0) == 0)
    def _():
        pair_ref[...] = jnp.zeros_like(pair_ref)

    pair_ref[...] += back_pairs(heads, coords_ref, qkv_ref, do_ref, p_ref, dqkv_ref, dist, ds,
                                lambda *_: None, lambda: None)


def attention_back(qkv, do, probs, coords):
    _, heads, hd, rows = qkv.shape
    span = probs.shape[1]
    wide = pl.BlockSpec((3, heads, hd, span), lambda b: (0, 0, 0, b))
    return pl.pallas_call(
        functools.partial(bwd_kernel, heads),
        out_shape=(jax.ShapeDtypeStruct(qkv.shape, BF16), jax.ShapeDtypeStruct((SUB, KERN), F32)),
        grid=(rows // span,),
        in_specs=[pl.BlockSpec((3, span), lambda b: (0, b)), wide,
                  pl.BlockSpec((heads, hd, span), lambda b: (0, 0, b)),
                  pl.BlockSpec((heads * span, span), lambda b: (b, 0))],
        out_specs=[wide, pl.BlockSpec((SUB, KERN), lambda b: (0, 0))],
        scratch_shapes=[pltpu.VMEM((span, span), F32), pltpu.VMEM((span // LANE, SUB * span, LANE), F32)],
        compiler_params=pltpu.CompilerParams(vmem_limit_bytes=60 << 20),
        name="attend_back",
    )(coords, qkv, do, probs)


def mm(a, b, dims=NN):
    return lax.dot_general(a, b, dims, preferred_element_type=F32)


def remote(src, dst, send, recv, axis, target):
    return pltpu.make_async_remote_copy(
        src_ref=src, dst_ref=dst, send_sem=send, recv_sem=recv,
        device_id={axis: target}, device_id_type=MESH)


def greet(sizes, others=()):
    barrier = pltpu.get_barrier_semaphore()
    total = len(others)
    for place in others:
        pl.semaphore_signal(barrier, inc=1, device_id={"dp": place}, device_id_type=MESH)
    for axis, size in sizes.items():
        me = lax.axis_index(axis)
        for k in range(1, size):
            pl.semaphore_signal(barrier, inc=1, device_id={axis: lax.rem(me + k, size)}, device_id_type=MESH)
        total += size - 1
    pl.semaphore_wait(barrier, total)


class Seat:
    def __init__(self, n):
        self.n, self.nx = n, n // 2
        self.me = lax.axis_index("mp")
        self.core = lax.rem(self.me, 2)
        self.x = self.me // 2
        self.sib = self.me + 1 - 2 * self.core

    def chip(self, k):
        return lax.rem(self.x + 1 + k, self.nx)

    def source(self, k):
        return lax.rem(self.x + self.nx - 1 - k, self.nx)


class Grid:
    def __init__(self, ny, nz):
        self.ny, self.nz = ny, nz
        self.me = lax.axis_index("dp")
        self.z, self.y = self.me // ny, lax.rem(self.me, ny)
        self.nh, self.a, self.p = nz // 2, self.z // 2, lax.rem(self.z, 2)
        self.near = self.z + 1 - 2 * self.p

    def at(self, z, y):
        return z * self.ny + y

    def other(self, k):
        return lax.rem(self.a + 1 + k, self.nh)

    def far(self, k):
        return 2 * self.other(k) + self.p

    def yto(self, k):
        return lax.rem(self.y + 1 + k, self.ny)


def scatter_scratch(n, rows, width):
    nx = n // 2
    buf = lambda m: pltpu.VMEM((m, rows, width), BF16)
    return [buf(nx), buf(nx), buf(max(nx - 1, 1)), buf(max(nx - 1, 1)), DMA((nx,)), DMA((nx,)),
            DMA((max(nx - 1, 1),)), DMA((max(nx - 1, 1),))]


class Scatter:
    def __init__(self, seat, scratch):
        self.seat = seat
        self.out1, self.in1, self.out2, self.in2, self.s1, self.r1, self.s2, self.r2 = scratch

    def first(self, k):
        return remote(self.out1.at[k], self.in1.at[k], self.s1.at[k], self.r1.at[k], "mp", self.seat.sib)

    def second(self, k):
        target = self.seat.chip(k) * 2 + self.seat.core
        return remote(self.out2.at[k], self.in2.at[k], self.s2.at[k], self.r2.at[k], "mp", target)

    def push_one(self, k, block):
        self.out1[k] = block(self.seat.chip(k) * 2 + 1 - self.seat.core).astype(BF16)
        self.first(k).start()

    def push(self, block):
        for k in range(self.seat.nx):
            self.push_one(k, block)

    def pass_on(self, block, own=None):
        seat = self.seat
        parts = [block(seat.chip(k) * 2 + seat.core) for k in range(seat.nx - (own is not None))]
        if own is not None:
            parts.append(own[...])
        for k in range(seat.nx):
            self.first(k).wait_recv()
            whole = parts[k] + self.in1[k].astype(F32)
            if k < seat.nx - 1:
                self.out2[k] = whole.astype(BF16)
                self.second(k).start()
        return whole

    def finish(self, whole):
        for k in range(self.seat.nx - 1):
            self.second(k).wait_recv()
            whole = whole + self.in2[k].astype(F32)
        return whole

    def drain(self):
        for k in range(self.seat.nx):
            self.first(k).wait_send()
        for k in range(self.seat.nx - 1):
            self.second(k).wait_send()


def gather_scratch(n):
    nx = n // 2
    return [DMA((max(nx - 1, 1),)), DMA((max(nx - 1, 1),)), DMA((nx,)), DMA((nx,))]


class Gather:
    def __init__(self, seat, rows, scratch):
        self.seat, self.rows = seat, rows
        self.sx, self.rx, self.sc, self.rc = scratch

    def across(self, k):
        r = self.rows.at[self.seat.me]
        return remote(r, r, self.sx.at[k], self.rx.at[k], "mp", self.seat.chip(k) * 2 + self.seat.core)

    def along(self, k):
        chip = self.seat.x if k == self.seat.nx - 1 else self.seat.source(k)
        r = self.rows.at[chip * 2 + self.seat.core]
        return remote(r, r, self.sc.at[k], self.rc.at[k], "mp", self.seat.sib)

    def start(self):
        for k in range(self.seat.nx - 1):
            self.across(k).start()
        self.along(self.seat.nx - 1).start()

    def forward(self):
        for k in range(self.seat.nx - 1):
            self.across(k).wait_recv()
            self.along(k).start()

    def sibling(self):
        self.along(self.seat.nx - 1).wait_recv()

    def finish(self, sibling=True):
        for k in range(self.seat.nx - (not sibling)):
            self.along(k).wait_recv()

    def drain(self):
        for k in range(self.seat.nx - 1):
            self.across(k).wait_send()
        for k in range(self.seat.nx):
            self.along(k).wait_send()


def centre(rows):
    c = rows - jnp.mean(rows, axis=-1, keepdims=True)
    r = lax.rsqrt(jnp.mean(c * c, axis=-1, keepdims=True) + ln_eps)
    return c * r, r


def norm_back(rows, gain, e):
    vhat, r = centre(rows)
    ge = e * gain
    dv = r * (ge - jnp.mean(ge, axis=-1, keepdims=True) - vhat * jnp.mean(ge * vhat, axis=-1, keepdims=True))
    return dv, jnp.sum(e * vhat, axis=0, keepdims=True), jnp.sum(e, axis=0, keepdims=True)


def enter_kernel(n, x_ref, np_ref, w_hbm, h_ref, qkv_ref, w32, wsem, *sems):
    seat = Seat(n)
    load = pltpu.make_async_copy(w_hbm, w32, wsem)
    load.start()
    greet({"mp": n})
    vhat, _ = centre(x_ref[...].astype(F32))
    h_ref[seat.me] = (vhat * np_ref[0:1] + np_ref[1:2]).astype(BF16)
    gh = Gather(seat, h_ref, sems)
    gh.start()
    load.wait()
    gh.forward()
    gh.finish()
    rows = h_ref.shape[1]
    for s in range(3):
        w = w32[s].astype(BF16)

        def block(b, carry):
            out = mm(w, h_ref[b], NT)
            qkv_ref[s, :, :, pl.ds(pl.multiple_of(b * rows, rows), rows)] = out.reshape(
                *qkv_ref.shape[1:3], rows).astype(BF16)
            return carry

        lax.fori_loop(0, n, block, 0)
    gh.drain()


def enter(n, heads, x, params, qkv_weight):
    rows, width = x.shape
    _, inner, _ = qkv_weight.shape
    return pl.pallas_call(
        functools.partial(enter_kernel, n),
        out_shape=(jax.ShapeDtypeStruct((n, rows, width), BF16),
                   jax.ShapeDtypeStruct((3, heads, inner // heads, n * rows), BF16)),
        in_specs=[VM, VM, HBM], out_specs=[VM, VM],
        scratch_shapes=[pltpu.VMEM(qkv_weight.shape, F32), DMA, *gather_scratch(n)],
        compiler_params=pltpu.CompilerParams(collective_id=0, has_side_effects=True, vmem_limit_bytes=60 << 20),
        name="enter",
    )(x, params, qkv_weight)


def middle_kernel(n, ny, nz, pushes, x_ref, o_ref, np_ref, bias_ref, pw_hbm, iw_hbm, ow_hbm, *rest):
    dys, rest = rest[:n], rest[n:]
    (block_ref, mid_ref, do_ref, og_ref, ig_ref, pg_ref, bg_ref, small_ref), rest = rest[:8], rest[8:]
    lands, rest = rest[:pushes], rest[pushes:]
    (pw32, iw32, ow32, pw, iw, ow, h2, da, act, dpre, dact, dyall_ref, kept, wsem), rest = rest[:14], rest[14:]
    seat, grid = Seat(n), Grid(ny, nz)
    dy_ref = dys[0]
    rows, width = x_ref.shape
    loads = [pltpu.make_async_copy(a, b, wsem.at[i])
             for i, (a, b) in enumerate([(pw_hbm, pw32), (ow_hbm, ow32), (iw_hbm, iw32)])]
    for c in loads:
        c.start()
    scat = [Scatter(seat, rest[8 * i:8 * i + 8]) for i in range(3)]
    gath = [Gather(seat, r, rest[24 + 4 * i:28 + 4 * i]) for i, r in enumerate((h2, da))]
    places = [grid.z * ny + grid.yto(k) for k in range(ny - 1)]
    greet({"mp": n}, places if pushes else ())

    def ahead(i, k):
        part = (og_ref, ig_ref)[i // PARTS]
        tall = part.shape[0] // (PARTS * ny)
        start = pl.multiple_of(((i % PARTS) * ny + grid.yto(k)) * tall, 16)
        return remote(part.at[pl.ds(start, tall), :], lands[i].at[k], rest[32].at[i, k], rest[33].at[i, k],
                      "dp", places[k])

    copies = [[ahead(i, k) for k in range(ny - 1)] for i in range(pushes)]
    for k in range(n):
        dyall_ref[lax.rem(seat.me + k, n)] = dys[k][...]
    at = lambda b: pl.ds(pl.multiple_of(b * rows, rows), rows)

    loads[0].wait()
    pw[...] = pw32[...].astype(BF16)
    attn_block = lambda b: mm(o_ref[:, at(b)], pw[...], TN)
    scat[0].push(attn_block)
    loads[1].wait()
    ow[...] = ow32[...].astype(BF16)
    whole = scat[0].pass_on(attn_block)
    loads[2].wait()
    iw[...] = iw32[...].astype(BF16)

    def back_act(b, carry):
        dact[b] = mm(dyall_ref[b], ow[...], NT)
        return carry

    lax.fori_loop(0, n, back_act, 0)
    mid = x_ref[...].astype(F32) + scat[0].finish(whole)
    vhat, _ = centre(mid)
    h2[seat.me] = (vhat * np_ref[2:3] + np_ref[3:4]).astype(BF16)
    mid_ref[...] = mid
    gath[0].start()
    bg_ref[...] = jnp.zeros_like(bg_ref)
    bias = bias_ref[...].astype(BF16).astype(F32)

    def feed_block(b):
        pre = mm(h2[b], iw[...], NT) + bias
        phi = 0.5 + 0.5 * lax.erf(pre * math.sqrt(0.5))
        act[b] = (pre * phi).astype(BF16)
        slope = phi + pre * (jnp.exp(-0.5 * pre * pre) * (1.0 / math.sqrt(2.0 * math.pi)))
        d = (dact[b] * slope).astype(BF16)
        dpre[b] = d
        bg_ref[...] += jnp.sum(d.astype(F32), axis=0, keepdims=True)
        return mm(d, iw[...])

    last = seat.nx - 1
    kept[...] = feed_block(seat.me)
    gath[0].sibling()
    scat[1].push_one(last, feed_block)
    gath[0].forward()
    gath[0].finish(sibling=False)
    for k in range(last):
        scat[1].push_one(k, feed_block)
    whole = scat[1].pass_on(feed_block, kept)
    hidden = iw.shape[0]
    step = LANE if hidden % LANE == 0 else hidden

    def grads(left, right, out, first):
        def columns(i, carry):
            c0 = pl.multiple_of(i * step, step)
            acc = jnp.zeros((step, width), F32)
            for b in range(n):
                acc += mm(left[b, :, pl.ds(c0, step)], right[b], TN)
            out[pl.ds(c0, step), :] = acc.astype(BF16)
            return carry

        lax.fori_loop(0, hidden // step, columns, 0)
        for piece in copies[first:first + PARTS]:
            for copy in piece:
                copy.start()

    grads(act, dyall_ref, og_ref, 0)
    out_block = lambda b: mm(act[b], ow[...])
    scat[2].push(out_block)
    dh2 = scat[1].finish(whole)
    dv, gain, shift = norm_back(mid_ref[...], np_ref[2:3], dh2)
    dy = dy_ref[...].astype(F32)
    dx1 = dy + dv
    da[seat.me] = dx1.astype(BF16)
    gath[1].start()
    small_ref[...] = jnp.concatenate(
        [gain, shift, jnp.sum(dy, axis=0, keepdims=True), jnp.zeros((5, width), F32)], 0)
    whole = scat[2].pass_on(out_block)
    gath[1].forward()
    grads(dpre, h2, ig_ref, PARTS)
    block_ref[...] = mid_ref[...] + scat[2].finish(whole) + np_ref[4:5]
    mid_ref[...] = dx1
    gath[1].finish()

    def heads_block(b, acc):
        out = mm(pw[...], da[b], NT)
        do_ref[:, :, at(b)] = out.reshape(*do_ref.shape[:2], rows).astype(BF16)
        return acc + mm(o_ref[:, at(b)], da[b])

    pg_ref[...] = lax.fori_loop(0, n, heads_block, jnp.zeros(pg_ref.shape, F32)).astype(BF16)
    for c in scat + gath:
        c.drain()
    for piece in copies:
        for copy in piece:
            copy.wait()


PARTS = 2
MIDDLE_MIB = 24


def middle(n, ny, nz, pushes, x, dys, o, params, bias, proj_weight, in_weight, out_weight):
    rows, width = x.shape
    hidden = in_weight.shape[0]
    inner = proj_weight.shape[0]
    heads, hd, _ = o.shape
    f = lambda *s: jax.ShapeDtypeStruct(s, F32)
    return pl.pallas_call(
        functools.partial(middle_kernel, n, ny, nz, pushes),
        out_shape=(f(rows, width), f(rows, width), jax.ShapeDtypeStruct(o.shape, BF16),
                   *[jax.ShapeDtypeStruct((t, width), BF16) for t in (hidden, hidden, inner)], f(1, hidden), f(8, width),
                   *[jax.ShapeDtypeStruct((ny - 1, hidden // (PARTS * ny), width), BF16)] * pushes),
        in_specs=[VM] * 4 + [HBM] * 3 + [VM] * n, out_specs=[VM] * (8 + pushes),
        scratch_shapes=[pltpu.VMEM((inner, width), F32), pltpu.VMEM((hidden, width), F32),
                        pltpu.VMEM((hidden, width), F32), pltpu.VMEM((inner, width), BF16),
                        pltpu.VMEM((hidden, width), BF16), pltpu.VMEM((hidden, width), BF16),
                        pltpu.VMEM((n, rows, width), BF16), pltpu.VMEM((n, rows, width), BF16),
                        pltpu.VMEM((n, rows, hidden), BF16), pltpu.VMEM((n, rows, hidden), BF16),
                        pltpu.VMEM((n, rows, hidden), F32), pltpu.VMEM((n, rows, width), BF16), pltpu.VMEM((rows, width), F32), DMA((3,)),
                        *[s for _ in range(3) for s in scatter_scratch(n, rows, width)],
                        *gather_scratch(n), *gather_scratch(n),
                        *[DMA((max(pushes, 1), max(ny - 1, 1)))] * 2],
        compiler_params=pltpu.CompilerParams(collective_id=1, has_side_effects=True, vmem_limit_bytes=MIDDLE_MIB << 20),
        name="middle",
    )(x, o.reshape(inner, -1), params, bias, proj_weight, in_weight, out_weight, *dys)


def sum_scratch(shape):
    ny, _, nh, chunk, width = shape
    y, f = max(ny - 1, 1), max(nh - 1, 1)
    return [pltpu.VMEM((y, 2, nh, chunk, width), BF16), pltpu.VMEM((nh, chunk, width), F32),
            pltpu.VMEM((nh, chunk, width), BF16), pltpu.VMEM((nh, chunk, width), BF16),
            pltpu.VMEM((f, chunk, width), BF16), pltpu.VMEM((f, chunk, width), BF16),
            DMA((y,)), DMA((y,)), DMA((1,)), DMA((1,)), DMA((f,)), DMA((f,))]


class Sum:
    count = 12

    def __init__(self, grid, grad, own, scratch):
        self.grid, self.grad, self.own, self.pushed = grid, grad, own, True
        (self.ia, self.keep, self.ob, self.ib, self.oc, self.ic,
         self.sa, self.ra, self.sb, self.rb, self.sc, self.rc) = scratch

    def copy_y(self, k):
        g = self.grid
        return remote(self.grad.at[g.yto(k)], self.ia.at[k], self.sa.at[k], self.ra.at[k], "dp", g.at(g.z, g.yto(k)))

    def copy_near(self):
        g = self.grid
        return remote(self.ob, self.ib, self.sb.at[0], self.rb.at[0], "dp", g.at(g.near, g.y))

    def copy_far(self, k):
        g = self.grid
        return remote(self.oc.at[k], self.ic.at[k], self.sc.at[k], self.rc.at[k], "dp", g.at(g.far(k), g.y))

    def push(self):
        for k in range(self.grid.ny - 1):
            self.copy_y(k).start()

    def half(self, p):
        g = self.grid
        whole = self.grad[g.y, p].astype(F32)
        for k in range(g.ny - 1):
            whole = whole + self.ia[k, p].astype(F32)
        return whole

    def near(self):
        g = self.grid
        for k in range(g.ny - 1 if self.pushed else 0):
            self.copy_y(k).wait_recv()
        self.ob[...] = self.half(1 - g.p).astype(BF16)
        self.copy_near().start()
        self.keep[...] = self.half(g.p)

    def far(self):
        g = self.grid
        self.copy_near().wait_recv()
        for k in range(g.nh - 1):
            a = g.other(k)
            self.oc[k] = (self.keep[a] + self.ib[a].astype(F32)).astype(BF16)
            self.copy_far(k).start()
        self.own[...] = self.keep[g.a] + self.ib[g.a].astype(F32)

    def collect(self):
        whole = self.own[...]
        for k in range(self.grid.nh - 1):
            self.copy_far(k).wait_recv()
            whole = whole + self.ic[k].astype(F32)
        self.own[...] = whole

    def drain(self):
        g = self.grid
        for k in range(g.ny - 1 if self.pushed else 0):
            self.copy_y(k).wait_send()
        self.copy_near().wait_send()
        for k in range(g.nh - 1):
            self.copy_far(k).wait_send()


def spread_scratch(ny, nz):
    y, f = max(ny - 1, 1), max(nz // 2 - 1, 1)
    return [DMA((f,)), DMA((f,)), DMA((1,)), DMA((1,)), DMA((2, y)), DMA((2, y))]


class Spread:
    count = 6

    def __init__(self, grid, own, result, scratch):
        self.grid, self.own, self.result = grid, own, result
        self.sf, self.rf, self.sn, self.rn, self.sy, self.ry = scratch

    def to_far(self, k):
        g = self.grid
        r = self.result.at[g.y, g.p, g.a]
        return remote(r, r, self.sf.at[k], self.rf.at[k], "dp", g.at(g.far(k), g.y))

    def to_near(self):
        g = self.grid
        r = self.result.at[g.y, g.p]
        return remote(r, r, self.sn.at[0], self.rn.at[0], "dp", g.at(g.near, g.y))

    def to_y(self, i, k):
        g = self.grid
        r = self.result.at[g.y, g.p if i == 0 else 1 - g.p]
        return remote(r, r, self.sy.at[i, k], self.ry.at[i, k], "dp", g.at(g.z, g.yto(k)))

    def start(self):
        g = self.grid
        whole = self.own[...]
        self.result[g.y, g.p, g.a] = whole.astype(BF16)
        for k in range(g.nh - 1):
            self.to_far(k).start()
        return square(whole)

    def second(self):
        g = self.grid
        for k in range(g.nh - 1):
            self.to_far(k).wait_recv()
        self.to_near().start()
        for k in range(g.ny - 1):
            self.to_y(0, k).start()

    def third(self):
        self.to_near().wait_recv()
        for k in range(self.grid.ny - 1):
            self.to_y(1, k).start()

    def close(self):
        g = self.grid
        for i in range(2):
            for k in range(g.ny - 1):
                self.to_y(i, k).wait()
        for k in range(g.nh - 1):
            self.to_far(k).wait_send()
        self.to_near().wait_send()


def take(rest, cls, count):
    size = cls.count
    return [rest[size * i:size * (i + 1)] for i in range(count)], rest[size * count:]


class Share:
    def __init__(self, axis, slots, send, recv):
        self.axis, self.slots, self.send, self.recv = axis, slots, send, recv
        self.size = slots.shape[0]
        self.me = lax.axis_index(axis)

    def copy(self, k):
        r = self.slots.at[self.me]
        return remote(r, r, self.send.at[k], self.recv.at[k], self.axis, lax.rem(self.me + 1 + k, self.size))

    def start(self, value):
        self.slots[self.me] = value
        for k in range(self.size - 1):
            self.copy(k).start()

    def total(self):
        for k in range(self.size - 1):
            self.copy(k).wait_recv()
        out = self.slots[0]
        for i in range(1, self.size):
            out = out + self.slots[i]
        return out

    def drain(self):
        for k in range(self.size - 1):
            self.copy(k).wait_send()


def share_scratch(size, rows, width):
    return [pltpu.VMEM((size, rows, width), F32), DMA((max(size - 1, 1),)), DMA((max(size - 1, 1),))]


def square(v):
    return jnp.sum(jnp.sum(v * v, axis=1, keepdims=True), axis=0, keepdims=True)


NEAR_AT = (-1, -1, 5, 100, 105, 113, 120, 128)
FAR_AT = (2, 5, 99, 111, 113, 123, 131, 140)
COLLECT_AT = (7, 99, 106, 123, 124, 133, 144, 154)
SECOND_AT = (101, 110, 120, 139, 140, 149, 159, 167)
THIRD_AT = (114, 126, 139, 154, 157, 168, 168, 168)
NORM_AT = 118
SMALL_AT = 130
REAR_MIB = 36


def rear_kernel(n, ny, nz, pushes, coords_ref, qkv_ref, do_ref, p_ref, og_ref, ig_ref, pg_ref, x_ref, dx_ref, np_ref,
                h_ref, bg_ref, mid_small_ref, w_hbm, *rest):
    lands, rest = rest[:pushes], rest[pushes:]
    early = 2 * PARTS + 1
    results, (sq_ref, gi_ref, small_ref, bias_ref, pairs_ref, norm_ref), rest = rest[:early], rest[early:early + 6], rest[early + 6:]
    (dist, ds, dqkv, flat, w32, w, qg, qown, kept, squares, wsem), rest = rest[:11], rest[11:]
    owns, rest = rest[:early], rest[early:]
    _, heads, hd, span = qkv_ref.shape
    inner = heads * hd
    rows, width = x_ref.shape
    seat, grid = Seat(n), Grid(ny, nz)
    pieces = [g.at[i] for g in (og_ref, ig_ref) for i in range(PARTS)] + [pg_ref] + [qg.at[s] for s in range(3)]
    places = [*owns, *[qown.at[s] for s in range(3)]]
    targets = [*results, *[sq_ref.at[s] for s in range(3)]]
    scat, rest = Scatter(seat, rest[:8]), rest[8:]
    scratch, rest = take(rest, Sum, early + 3)
    sums = [Sum(grid, *a) for a in zip(pieces, places, scratch)]
    scratch, rest = take(rest, Spread, early + 3)
    spreads = [Spread(grid, *a) for a in zip(places, targets, scratch)]
    shares = [Share(a, *rest[3 * i:3 * i + 3]) for i, a in enumerate(("mp", "dp", "dp", "dp", "mp", "dp", "mp"))]
    small_mp, small_dp, bias_dp, pair_dp, sq_mp, sq_dp, local_mp = shares
    for s, land in zip(sums, lands):
        s.ia, s.pushed = land, False
    at = lambda b: pl.ds(pl.multiple_of(b * rows, rows), rows)
    load = pltpu.make_async_copy(w_hbm, w32, wsem)
    load.start()
    greet({"mp": n, "dp": ny * nz})
    for s in sums[pushes:early]:
        s.push()
    squares[...] = jnp.zeros_like(squares)

    def collect(i):
        sums[i].collect()
        squares[...] += spreads[i].start()

    def project():
        for s in range(3):
            flat[s] = dqkv[s].astype(F32).reshape(inner, span).astype(BF16)
            acc = jnp.zeros((inner, width), F32)
            for b in range(n):
                acc = acc + mm(flat[s, :, at(b)], h_ref[b])
            qg[s] = acc.reshape(qg.shape[1:]).astype(BF16)
            sums[early + s].push()
        load.wait()
        w[...] = w32[...].astype(BF16)
        block = lambda b: sum(mm(flat[s, :, at(b)], w[s], TN) for s in range(3))
        scat.push(block)
        kept[...] = scat.pass_on(block)
        bias_dp.start(jnp.broadcast_to(bg_ref[...], bias_dp.slots.shape[1:]))

    def norm():
        dh1 = scat.finish(kept[...])
        dv, gain, shift = norm_back(x_ref[...].astype(F32), np_ref[0:1], dh1)
        gi_ref[...] = dx_ref[...] + dv
        small_mp.start(jnp.concatenate([gain, shift, mid_small_ref[0:6]], 0))

    jobs = {99: [project], NORM_AT: [norm], SMALL_AT: [lambda: small_dp.start(small_mp.total())]}
    for i, s in enumerate(sums):
        for when, job in ((NEAR_AT[i], s.near), (FAR_AT[i], s.far), (COLLECT_AT[i], functools.partial(collect, i)),
                          (SECOND_AT[i], spreads[i].second), (THIRD_AT[i], spreads[i].third)):
            jobs.setdefault(when, []).append(job)

    def now(first, end):
        for when in sorted(jobs):
            if first <= when < end:
                for job in jobs[when]:
                    job()

    def beside(step, first, end):
        for when in sorted(jobs):
            if first <= when < end:
                @pl.when(step == when)
                def _():
                    for job in jobs[when]:
                        job()

    now(-1, 0)
    pair = back_pairs(heads, coords_ref, qkv_ref, do_ref, p_ref, dqkv, dist, ds, beside, lambda: now(99, 100))
    pair_dp.start(pair)
    last = 100 + span // SUB
    now(last, last + 4)
    sq_mp.start(jnp.broadcast_to(squares[...], (8, LANE)))
    now(last + 4, 1000)
    bias = bias_dp.total()
    bias_ref[...] = bias
    pairs = pair_dp.total()
    pairs_ref[...] = pairs
    local_mp.start(jnp.broadcast_to(square(bias[0:1]) + square(pairs), (8, LANE)))
    sq_dp.start(sq_mp.total())
    small = small_dp.total()
    small_ref[...] = small
    norm_ref[...] = sq_dp.total()[0:1] + local_mp.total()[0:1] + square(small)
    for s in spreads:
        s.close()
    for s in [scat] + sums + shares:
        s.drain()


def rear(n, ny, nz, qkv, do, probs, coords, og, ig, pg, lands, x, dx, params, h, bias_grad, small, qkv_weight):
    _, heads, hd, span = qkv.shape
    rows, width = x.shape
    inner, hidden = heads * hd, bias_grad.shape[1]
    ndp, pushes = ny * nz, len(lands)
    cut = lambda g, p: g.reshape(p, ny, 2, nz // 2, g.shape[0] // (p * ndp), width)
    lands = [v.reshape(ny - 1, 2, nz // 2, -1, width) for v in lands]
    og, ig, pg = cut(og, PARTS), cut(ig, PARTS), cut(pg, 1)[0]
    chunks = (3, ny, 2, nz // 2, inner // ndp, width)
    shapes = [og.shape[1:]] * PARTS + [ig.shape[1:]] * PARTS + [pg.shape]
    every = shapes + [chunks[1:]] * 3
    f = lambda *s: jax.ShapeDtypeStruct(s, F32)
    return pl.pallas_call(
        functools.partial(rear_kernel, n, ny, nz, pushes),
        out_shape=(*[jax.ShapeDtypeStruct(s, BF16) for s in (*shapes, chunks)],
                   f(rows, width), f(8, width), f(8, hidden), f(8, LANE), f(1, LANE)),
        in_specs=[VM] * 13 + [HBM] + [VM] * pushes, out_specs=[VM] * (len(shapes) + 6),
        scratch_shapes=[pltpu.VMEM((span, span), F32), pltpu.VMEM((span // LANE, SUB * span, LANE), F32),
                        pltpu.VMEM(qkv.shape, BF16), pltpu.VMEM((3, inner, span), BF16),
                        pltpu.VMEM(qkv_weight.shape, F32), pltpu.VMEM(qkv_weight.shape, BF16), pltpu.VMEM(chunks, BF16),
                        pltpu.VMEM((3, inner // ndp, width), F32), pltpu.VMEM((rows, width), F32),
                        pltpu.VMEM((1, LANE), F32), DMA, *[pltpu.VMEM(s[3:], F32) for s in shapes],
                        *scatter_scratch(n, rows, width),
                        *[v for s in every for v in sum_scratch(s)], *[v for _ in every for v in spread_scratch(ny, nz)],
                        *share_scratch(n, 8, width), *share_scratch(ndp, 8, width), *share_scratch(ndp, 8, hidden),
                        *share_scratch(ndp, 8, LANE), *share_scratch(n, 8, LANE), *share_scratch(ndp, 8, LANE),
                        *share_scratch(n, 8, LANE)],
        compiler_params=pltpu.CompilerParams(collective_id=2, has_side_effects=True, vmem_limit_bytes=REAR_MIB << 20),
        name="rear",
    )(coords, qkv, do, probs, og, ig, pg, x, dx, params, h, bias_grad, small, qkv_weight, *lands)


def leave_plain(n, x, dx, params, dqkv, h, grads, bias_grad, pair_grad, small, qkv_weight):
    part = sum(mm(dqkv[s], qkv_weight[s].astype(BF16), TN) for s in range(3))
    dh1 = lax.psum_scatter(part, "mp", scatter_dimension=0, tiled=True)
    dv, gain, shift = norm_back(x.astype(F32), params[0:1], dh1)
    hh = h.reshape(-1, h.shape[-1])
    qg = jnp.concatenate([mm(dqkv[s], hh) for s in range(3)], 0)
    og, ig, pg, qg, bias, pair = lax.psum((*[g.astype(F32) for g in grads], qg, bias_grad, pair_grad), "dp")
    small = lax.psum(jnp.concatenate([gain, shift, small[0:6]], 0), ("dp", "mp"))
    local = sum(square(v) for v in (og, ig, pg, qg, bias, pair))
    total = lax.psum(local, "mp") + square(small)
    return dx + dv, og, ig, pg, qg, small, bias, pair, total


PUSHES = 2


def adam_step(weight, grad, first, second, clip, fix_one, fix_two, rate, decay):
    scaled = grad * clip
    first_new = beta_one * first + (1.0 - beta_one) * scaled
    second_new = beta_two * second + (1.0 - beta_two) * scaled * scaled
    ratio = first_new / fix_one / (jnp.sqrt(second_new / fix_two) + adam_eps)
    return (weight - rate * (ratio + decay * weight), first_new, second_new)


def per_device(n, ndp, block_in, coords, lengths, cotangent, step_count, *state):
    weights, firsts, seconds = state[:7], state[7:14], state[14:]
    qkv_weight, proj_weight, pair_weight, in_weight, in_bias, out_weight, params = weights
    heads = pair_weight.shape[0]
    h, qkv = enter(n, heads, block_in, params, qkv_weight)
    o, probs = attention(qkv, coords, lengths, pair_weight)
    dy, _ = lax.optimization_barrier((cotangent, qkv))
    dys = [cotangent] + [lax.ppermute(dy, "mp", [((i + k) % n, i) for i in range(n)]) for k in range(1, n)]
    ny = n // 2 if ndp % (n // 2) == 0 else 1
    nz = ndp // ny
    inner, hidden = proj_weight.shape[0], in_weight.shape[0]
    beside = lengths.shape[0] == 1 and nz % 2 == 0 and inner % (8 * ndp) == 0 and hidden % (16 * PARTS * ndp) == 0
    block_out, dx, do, og, ig, pg, bg, small, *lands = middle(
        n, ny, nz, PUSHES if beside else 0, block_in, dys, o, params, in_bias.reshape(1, -1), proj_weight, in_weight, out_weight)
    if beside:
        *pieces, pg, qg, grad_input, small, bias, pair, total = rear(
            n, ny, nz, qkv, do, probs, coords, og, ig, pg, lands, block_in, dx, params, h, bg, small, qkv_weight)
        og, ig = pieces[:PARTS], pieces[PARTS:]
        og, ig = [jnp.concatenate([v.reshape(-1, v.shape[-1]) for v in g], 0) for g in (og, ig)]
    else:
        dqkv, pair_grad = attention_back(qkv, do, probs, coords)
        grad_input, og, ig, pg, qg, small, bias, pair, total = leave_plain(
            n, block_in, dx, params, dqkv.reshape(3, inner, -1), h, (og, ig, pg), bg, pair_grad, small, qkv_weight)
    grad_norm = jnp.sqrt(total[0, 0])
    clip = clip_level / jnp.maximum(grad_norm, clip_level)
    count = step_count[0].astype(F32)
    fix_one = 1.0 - jnp.power(beta_one, count)
    fix_two = 1.0 - jnp.power(beta_two, count)
    grads = (qg.reshape(qkv_weight.shape), pg.reshape(proj_weight.shape), pair[:heads], ig.reshape(in_weight.shape),
             bias[0], og.reshape(out_weight.shape), small[:5])
    rates = (0.9, 2.5, 7.5, 0.9, 7.5, 0.45, 3.0)
    decays = (0.01, 0.01, 0.01, 0.01, 0.0, 0.01, 0.0)
    outs = [block_out, grad_input, grad_norm.reshape(1)]
    for w, g, m, u, rate, decay in zip(weights, grads, firsts, seconds, rates, decays):
        outs.extend(adam_step(w, g.astype(F32), m, u, clip, fix_one, fix_two, rate, decay))
    return tuple(outs)


def solution(mesh):
    rows, mp = P(("dp", "mp"), None), P("mp", None)
    stacked = P(None, "mp", None)
    params = (stacked, mp, mp, mp, P("mp"), mp, P())
    in_specs = (rows, P(None, "dp"), P("dp", None), rows, P(), *params, *params, *params)
    out_specs = (rows, rows, P(), *[s for s in params for _ in range(3)])
    return jax.shard_map(
        functools.partial(per_device, mesh.shape["mp"], mesh.shape["dp"]),
        mesh=mesh, in_specs=in_specs, out_specs=out_specs, check_vma=False)
```

```python
import functools
import math

import jax
import jax.numpy as jnp
from jax import lax
from jax.experimental import pallas as pl
from jax.experimental.pallas import tpu as pltpu
from jax.sharding import PartitionSpec as P

ln_eps = 1e-05
beta_one = 0.9
beta_two = 0.999
adam_eps = 1e-08
clip_level = 1.0

F32, BF16 = jnp.float32, jnp.bfloat16
MESH = pl.DeviceIdType.MESH
NN = (((1,), (0,)), ((), ()))
NT = (((1,), (1,)), ((), ()))
TN = (((0,), (0,)), ((), ()))
VM = pl.BlockSpec(memory_space=pltpu.VMEM)
HBM = pl.BlockSpec(memory_space=pl.ANY)
DMA = pltpu.SemaphoreType.DMA
KERN = 128
LANE = 128
SUB = 8
TALL = 32
ATTEND_MIB = 20
KS = math.sqrt(0.5 * math.log2(math.e))
UNIT = KS / (12.8 / KERN)


def pair_distances(coords_ref, dist, span):
    pts = coords_ref[...]
    cols = jnp.transpose(jnp.concatenate([pts, jnp.zeros((5, span), F32)], 0))
    acc = None
    for a in range(3):
        d = cols[:, a:a + 1] - pts[a:a + 1, :]
        acc = d * d if acc is None else acc + d * d
    dist[...] = jnp.sqrt(acc) * UNIT


def pair_labels(len_ref, b, labs, labr, span, mols):
    lanes = lax.broadcasted_iota(jnp.int32, (SUB, span), 1)
    lc = jnp.zeros((SUB, span), F32)
    end = jnp.int32(0)
    for m in range(mols):
        end = end + len_ref[b, m]
        lc = lc + (lanes >= end).astype(F32)
    labr[...] = lc
    labs[...] = jnp.broadcast_to(jnp.transpose(lc)[:, 0:1], (span, LANE))


def tile_range(len_ref, b, first, last, span, mols):
    lo = jnp.int32(0)
    hi = jnp.int32(span)
    end = jnp.int32(0)
    for m in range(mols):
        end = end + len_ref[b, m]
        lo = jnp.where(end <= first, end, lo)
        hi = jnp.where((end > last) & (end < hi), end, hi)
    return lo // LANE, (hi + LANE - 1) // LANE


def row_of(block, r):
    return jnp.broadcast_to(block[r:r + 1], (SUB, LANE))


def gauss_tile(drow):
    sub = lax.broadcasted_iota(jnp.int32, (SUB, LANE), 0).astype(F32) * KS
    base = drow - sub
    parts = []
    for c in range(KERN // SUB):
        t = base - (KS * SUB * c)
        parts.append(jnp.exp2(-(t * t)))
    return jnp.concatenate(parts, 0).astype(BF16)


def wide(ref, rows):
    return jnp.concatenate([ref[t, rows, :] for t in range(ref.shape[0])], 1)


def fwd_kernel(heads, mols, len_ref, coords_ref, qkv_ref, w_ref, o_ref, p_ref, dist, labs, labr, sc):
    hd, span = qkv_ref.shape[2:]
    b = pl.program_id(0)
    scale = 1.0 / math.sqrt(hd)
    pair_distances(coords_ref, dist, span)
    pair_labels(len_ref, b, labs, labr, span, mols)
    wb = w_ref[...].astype(BF16)
    step = LANE

    def fill(i, carry):
        r0 = pl.multiple_of(i * step, step)
        sc[:, pl.ds(r0, step), :] = jnp.full((span // LANE, step, LANE), -1e30, F32)
        return carry

    lax.fori_loop(0, SUB * span // step, fill, 0)

    def group(g, carry):
        i0 = pl.multiple_of(g * TALL, TALL)
        lo, hi = tile_range(len_ref, b, i0, i0 + TALL - 1, span, mols)

        def tile(jt, carry):
            j0 = pl.multiple_of(jt * LANE, LANE)
            lab = labr[:, pl.ds(j0, LANE)]
            dblk = dist[pl.ds(i0, TALL), pl.ds(j0, LANE)]
            lblk = labs[pl.ds(i0, TALL), :]
            for r in range(0, TALL, 2):
                bias = mm(wb, jnp.concatenate([gauss_tile(row_of(dblk, r)), gauss_tile(row_of(dblk, r + 1))], 1))
                for k in range(2):
                    sc[jt, pl.ds(i0 + r + k, SUB, span), :] = jnp.where(
                        row_of(lblk, r + k) == lab, bias[:, k * LANE:(k + 1) * LANE], -1e30)
            return carry

        return lax.fori_loop(lo, hi, tile, carry)

    lax.fori_loop(0, span // TALL, group, 0)

    def head(h, carry):
        for c in range(span // step):
            cols = pl.ds(c * step, step)
            rows = pl.ds(pl.multiple_of(h * span + c * step, step), step)
            s = mm(qkv_ref[0, h, :, cols], qkv_ref[1, h], TN) * scale + wide(sc, rows)
            e = jnp.exp(s - jnp.max(s, axis=-1, keepdims=True))
            p = (e * (1.0 / jnp.sum(e, axis=-1, keepdims=True))).astype(BF16)
            p_ref[rows, :] = p
            o_ref[h, :, cols] = mm(qkv_ref[2, h], p, NT).astype(BF16)
        return carry

    lax.fori_loop(0, heads, head, 0, unroll=4)


def attention(qkv, coords, lengths, pair_weight):
    _, heads, hd, rows = qkv.shape
    blocks, mols = lengths.shape
    span = rows // blocks
    w = jnp.pad(pair_weight, ((0, SUB - heads), (0, 0))) if heads < SUB else pair_weight
    return pl.pallas_call(
        functools.partial(fwd_kernel, heads, mols),
        out_shape=(jax.ShapeDtypeStruct((heads, hd, rows), BF16),
                   jax.ShapeDtypeStruct((blocks * heads * span, span), BF16)),
        grid_spec=pltpu.PrefetchScalarGridSpec(
            num_scalar_prefetch=1, grid=(blocks,),
            in_specs=[pl.BlockSpec((3, span), lambda b, *_: (0, b)),
                      pl.BlockSpec((3, heads, hd, span), lambda b, *_: (0, 0, 0, b)),
                      pl.BlockSpec((SUB, KERN), lambda b, *_: (0, 0))],
            out_specs=[pl.BlockSpec((heads, hd, span), lambda b, *_: (0, 0, b)),
                       pl.BlockSpec((heads * span, span), lambda b, *_: (b, 0))],
            scratch_shapes=[pltpu.VMEM((span, span), F32), pltpu.VMEM((span, LANE), F32),
                            pltpu.VMEM((SUB, span), F32), pltpu.VMEM((span // LANE, SUB * span, LANE), F32)]),
        cost_estimate=pl.CostEstimate(flops=20 * heads * hd * rows * span, bytes_accessed=8 * rows * span,
                                      transcendentals=KERN * rows * span),
        compiler_params=pltpu.CompilerParams(vmem_limit_bytes=ATTEND_MIB << 20),
        name="attend",
    )(lengths, coords, qkv, w)


def back_pairs(heads, coords_ref, qkv_ref, do_ref, p_ref, dqkv_ref, dist, ds, beside, between):
    hd, span = do_ref.shape[1:]
    scale = 1.0 / math.sqrt(hd)
    step = LANE
    pair_distances(coords_ref, dist, span)
    if heads < SUB:
        ds[...] = jnp.zeros_like(ds)

    def head(h, carry):
        beside(h, 0, heads)
        dk = jnp.zeros((hd, span), F32)
        dv = jnp.zeros((hd, span), F32)
        for c in range(span // step):
            cols = pl.ds(c * step, step)
            rows = pl.ds(pl.multiple_of(h * span + c * step, step), step)
            pb = p_ref[rows, :]
            p = pb.astype(F32)
            dp = mm(do_ref[h, :, cols], qkv_ref[2, h], TN)
            d = p * (dp - jnp.sum(p * dp, axis=-1, keepdims=True))
            for t in range(span // LANE):
                ds[t, rows, :] = d[:, t * LANE:(t + 1) * LANE]
            low = d.astype(BF16)
            dqkv_ref[0, h, :, cols] = (mm(qkv_ref[1, h], low, NT) * scale).astype(BF16)
            dk = dk + mm(qkv_ref[0, h, :, cols], low)
            dv = dv + mm(do_ref[h, :, cols], pb)
        dqkv_ref[1, h] = (dk * scale).astype(BF16)
        dqkv_ref[2, h] = dv.astype(BF16)
        return carry

    lax.fori_loop(0, heads, head, 0)
    between()

    def group(g, acc):
        beside(100 + g, 100, 100 + span // SUB)
        i0 = pl.multiple_of(g * SUB, SUB)

        left, right = [], []
        for jt in range(span // LANE):
            dblk = dist[pl.ds(i0, SUB), jt * LANE:(jt + 1) * LANE]
            for r in range(SUB // 2):
                pair = (r, r + SUB // 2)
                left.append(jnp.concatenate([ds[jt, pl.ds(i0 + k, SUB, span), :] for k in pair], 0).astype(BF16))
                right.append(jnp.concatenate([gauss_tile(row_of(dblk, k)) for k in pair], 0))
        return acc + mm(jnp.concatenate(left, 1), jnp.concatenate(right, 1), NT)

    acc = lax.fori_loop(0, span // SUB, group, jnp.zeros((2 * SUB, 2 * KERN), F32))
    return acc[:SUB, :KERN] + acc[SUB:, KERN:]


def bwd_kernel(heads, coords_ref, qkv_ref, do_ref, p_ref, dqkv_ref, pair_ref, dist, ds):
    @pl.when(pl.program_id(0) == 0)
    def _():
        pair_ref[...] = jnp.zeros_like(pair_ref)

    pair_ref[...] += back_pairs(heads, coords_ref, qkv_ref, do_ref, p_ref, dqkv_ref, dist, ds,
                                lambda *_: None, lambda: None)


def attention_back(qkv, do, probs, coords):
    _, heads, hd, rows = qkv.shape
    span = probs.shape[1]
    wide = pl.BlockSpec((3, heads, hd, span), lambda b: (0, 0, 0, b))
    return pl.pallas_call(
        functools.partial(bwd_kernel, heads),
        out_shape=(jax.ShapeDtypeStruct(qkv.shape, BF16), jax.ShapeDtypeStruct((SUB, KERN), F32)),
        grid=(rows // span,),
        in_specs=[pl.BlockSpec((3, span), lambda b: (0, b)), wide,
                  pl.BlockSpec((heads, hd, span), lambda b: (0, 0, b)),
                  pl.BlockSpec((heads * span, span), lambda b: (b, 0))],
        out_specs=[wide, pl.BlockSpec((SUB, KERN), lambda b: (0, 0))],
        scratch_shapes=[pltpu.VMEM((span, span), F32), pltpu.VMEM((span // LANE, SUB * span, LANE), F32)],
        compiler_params=pltpu.CompilerParams(vmem_limit_bytes=60 << 20),
        name="attend_back",
    )(coords, qkv, do, probs)


def mm(a, b, dims=NN):
    return lax.dot_general(a, b, dims, preferred_element_type=F32)


def remote(src, dst, send, recv, axis, target):
    return pltpu.make_async_remote_copy(
        src_ref=src, dst_ref=dst, send_sem=send, recv_sem=recv,
        device_id={axis: target}, device_id_type=MESH)


def greet(sizes, others=()):
    barrier = pltpu.get_barrier_semaphore()
    total = len(others)
    for place in others:
        pl.semaphore_signal(barrier, inc=1, device_id={"dp": place}, device_id_type=MESH)
    for axis, size in sizes.items():
        me = lax.axis_index(axis)
        for k in range(1, size):
            pl.semaphore_signal(barrier, inc=1, device_id={axis: lax.rem(me + k, size)}, device_id_type=MESH)
        total += size - 1
    pl.semaphore_wait(barrier, total)


class Seat:
    def __init__(self, n):
        self.n, self.nx = n, n // 2
        self.me = lax.axis_index("mp")
        self.core = lax.rem(self.me, 2)
        self.x = self.me // 2
        self.sib = self.me + 1 - 2 * self.core

    def chip(self, k):
        return lax.rem(self.x + 1 + k, self.nx)

    def source(self, k):
        return lax.rem(self.x + self.nx - 1 - k, self.nx)


class Grid:
    def __init__(self, ny, nz):
        self.ny, self.nz = ny, nz
        self.me = lax.axis_index("dp")
        self.z, self.y = self.me // ny, lax.rem(self.me, ny)
        self.nh, self.a, self.p = nz // 2, self.z // 2, lax.rem(self.z, 2)
        self.near = self.z + 1 - 2 * self.p

    def at(self, z, y):
        return z * self.ny + y

    def other(self, k):
        return lax.rem(self.a + 1 + k, self.nh)

    def far(self, k):
        return 2 * self.other(k) + self.p

    def yto(self, k):
        return lax.rem(self.y + 1 + k, self.ny)


def scatter_scratch(n, rows, width):
    nx = n // 2
    buf = lambda m: pltpu.VMEM((m, rows, width), BF16)
    return [buf(nx), buf(nx), buf(max(nx - 1, 1)), buf(max(nx - 1, 1)), DMA((nx,)), DMA((nx,)),
            DMA((max(nx - 1, 1),)), DMA((max(nx - 1, 1),))]


class Scatter:
    def __init__(self, seat, scratch):
        self.seat = seat
        self.out1, self.in1, self.out2, self.in2, self.s1, self.r1, self.s2, self.r2 = scratch

    def first(self, k):
        return remote(self.out1.at[k], self.in1.at[k], self.s1.at[k], self.r1.at[k], "mp", self.seat.sib)

    def second(self, k):
        target = self.seat.chip(k) * 2 + self.seat.core
        return remote(self.out2.at[k], self.in2.at[k], self.s2.at[k], self.r2.at[k], "mp", target)

    def push_one(self, k, block):
        self.out1[k] = block(self.seat.chip(k) * 2 + 1 - self.seat.core).astype(BF16)
        self.first(k).start()

    def push(self, block):
        for k in range(self.seat.nx):
            self.push_one(k, block)

    def pass_on(self, block, own=None):
        seat = self.seat
        parts = [block(seat.chip(k) * 2 + seat.core) for k in range(seat.nx - (own is not None))]
        if own is not None:
            parts.append(own[...])
        for k in range(seat.nx):
            self.first(k).wait_recv()
            whole = parts[k] + self.in1[k].astype(F32)
            if k < seat.nx - 1:
                self.out2[k] = whole.astype(BF16)
                self.second(k).start()
        return whole

    def finish(self, whole):
        for k in range(self.seat.nx - 1):
            self.second(k).wait_recv()
            whole = whole + self.in2[k].astype(F32)
        return whole

    def drain(self):
        for k in range(self.seat.nx):
            self.first(k).wait_send()
        for k in range(self.seat.nx - 1):
            self.second(k).wait_send()


def gather_scratch(n):
    nx = n // 2
    return [DMA((max(nx - 1, 1),)), DMA((max(nx - 1, 1),)), DMA((nx,)), DMA((nx,))]


class Gather:
    def __init__(self, seat, rows, scratch):
        self.seat, self.rows = seat, rows
        self.sx, self.rx, self.sc, self.rc = scratch

    def across(self, k):
        r = self.rows.at[self.seat.me]
        return remote(r, r, self.sx.at[k], self.rx.at[k], "mp", self.seat.chip(k) * 2 + self.seat.core)

    def along(self, k):
        chip = self.seat.x if k == self.seat.nx - 1 else self.seat.source(k)
        r = self.rows.at[chip * 2 + self.seat.core]
        return remote(r, r, self.sc.at[k], self.rc.at[k], "mp", self.seat.sib)

    def start(self):
        for k in range(self.seat.nx - 1):
            self.across(k).start()
        self.along(self.seat.nx - 1).start()

    def forward(self):
        for k in range(self.seat.nx - 1):
            self.across(k).wait_recv()
            self.along(k).start()

    def sibling(self):
        self.along(self.seat.nx - 1).wait_recv()

    def finish(self, sibling=True):
        for k in range(self.seat.nx - (not sibling)):
            self.along(k).wait_recv()

    def drain(self):
        for k in range(self.seat.nx - 1):
            self.across(k).wait_send()
        for k in range(self.seat.nx):
            self.along(k).wait_send()


def centre(rows):
    c = rows - jnp.mean(rows, axis=-1, keepdims=True)
    r = lax.rsqrt(jnp.mean(c * c, axis=-1, keepdims=True) + ln_eps)
    return c * r, r


def norm_back(rows, gain, e):
    vhat, r = centre(rows)
    ge = e * gain
    dv = r * (ge - jnp.mean(ge, axis=-1, keepdims=True) - vhat * jnp.mean(ge * vhat, axis=-1, keepdims=True))
    return dv, jnp.sum(e * vhat, axis=0, keepdims=True), jnp.sum(e, axis=0, keepdims=True)


def enter_kernel(n, x_ref, np_ref, w_hbm, h_ref, qkv_ref, w32, wsem, *sems):
    seat = Seat(n)
    load = pltpu.make_async_copy(w_hbm, w32, wsem)
    load.start()
    greet({"mp": n})
    vhat, _ = centre(x_ref[...].astype(F32))
    h_ref[seat.me] = (vhat * np_ref[0:1] + np_ref[1:2]).astype(BF16)
    gh = Gather(seat, h_ref, sems)
    gh.start()
    load.wait()
    gh.forward()
    gh.finish()
    rows = h_ref.shape[1]
    for s in range(3):
        w = w32[s].astype(BF16)

        def block(b, carry):
            out = mm(w, h_ref[b], NT)
            qkv_ref[s, :, :, pl.ds(pl.multiple_of(b * rows, rows), rows)] = out.reshape(
                *qkv_ref.shape[1:3], rows).astype(BF16)
            return carry

        lax.fori_loop(0, n, block, 0)
    gh.drain()


def enter(n, heads, x, params, qkv_weight):
    rows, width = x.shape
    _, inner, _ = qkv_weight.shape
    return pl.pallas_call(
        functools.partial(enter_kernel, n),
        out_shape=(jax.ShapeDtypeStruct((n, rows, width), BF16),
                   jax.ShapeDtypeStruct((3, heads, inner // heads, n * rows), BF16)),
        in_specs=[VM, VM, HBM], out_specs=[VM, VM],
        scratch_shapes=[pltpu.VMEM(qkv_weight.shape, F32), DMA, *gather_scratch(n)],
        compiler_params=pltpu.CompilerParams(collective_id=0, has_side_effects=True, vmem_limit_bytes=60 << 20),
        name="enter",
    )(x, params, qkv_weight)


def middle_kernel(n, ny, nz, pushes, x_ref, o_ref, np_ref, bias_ref, pw_hbm, iw_hbm, ow_hbm, *rest):
    dys, rest = rest[:n], rest[n:]
    (block_ref, mid_ref, do_ref, og_ref, ig_ref, pg_ref, bg_ref, small_ref), rest = rest[:8], rest[8:]
    lands, rest = rest[:pushes], rest[pushes:]
    (pw32, iw32, ow32, pw, iw, ow, h2, da, act, dpre, dact, dyall_ref, kept, wsem), rest = rest[:14], rest[14:]
    seat, grid = Seat(n), Grid(ny, nz)
    dy_ref = dys[0]
    rows, width = x_ref.shape
    loads = [pltpu.make_async_copy(a, b, wsem.at[i])
             for i, (a, b) in enumerate([(pw_hbm, pw32), (ow_hbm, ow32), (iw_hbm, iw32)])]
    for c in loads:
        c.start()
    scat = [Scatter(seat, rest[8 * i:8 * i + 8]) for i in range(3)]
    gath = [Gather(seat, r, rest[24 + 4 * i:28 + 4 * i]) for i, r in enumerate((h2, da))]
    places = [grid.z * ny + grid.yto(k) for k in range(ny - 1)]
    greet({"mp": n}, places if pushes else ())

    def ahead(i, k):
        part = (og_ref, ig_ref)[i // PARTS]
        tall = part.shape[0] // (PARTS * ny)
        start = pl.multiple_of(((i % PARTS) * ny + grid.yto(k)) * tall, 16)
        return remote(part.at[pl.ds(start, tall), :], lands[i].at[k], rest[32].at[i, k], rest[33].at[i, k],
                      "dp", places[k])

    copies = [[ahead(i, k) for k in range(ny - 1)] for i in range(pushes)]
    for k in range(n):
        dyall_ref[lax.rem(seat.me + k, n)] = dys[k][...]
    at = lambda b: pl.ds(pl.multiple_of(b * rows, rows), rows)

    loads[0].wait()
    pw[...] = pw32[...].astype(BF16)
    attn_block = lambda b: mm(o_ref[:, at(b)], pw[...], TN)
    scat[0].push(attn_block)
    loads[1].wait()
    ow[...] = ow32[...].astype(BF16)
    whole = scat[0].pass_on(attn_block)
    loads[2].wait()
    iw[...] = iw32[...].astype(BF16)

    def back_act(b, carry):
        dact[b] = mm(dyall_ref[b], ow[...], NT)
        return carry

    lax.fori_loop(0, n, back_act, 0)
    mid = x_ref[...].astype(F32) + scat[0].finish(whole)
    vhat, _ = centre(mid)
    h2[seat.me] = (vhat * np_ref[2:3] + np_ref[3:4]).astype(BF16)
    mid_ref[...] = mid
    gath[0].start()
    bg_ref[...] = jnp.zeros_like(bg_ref)
    bias = bias_ref[...].astype(BF16).astype(F32)

    def feed_block(b):
        pre = mm(h2[b], iw[...], NT) + bias
        phi = 0.5 + 0.5 * lax.erf(pre * math.sqrt(0.5))
        act[b] = (pre * phi).astype(BF16)
        slope = phi + pre * (jnp.exp(-0.5 * pre * pre) * (1.0 / math.sqrt(2.0 * math.pi)))
        d = (dact[b] * slope).astype(BF16)
        dpre[b] = d
        bg_ref[...] += jnp.sum(d.astype(F32), axis=0, keepdims=True)
        return mm(d, iw[...])

    last = seat.nx - 1
    kept[...] = feed_block(seat.me)
    gath[0].sibling()
    scat[1].push_one(last, feed_block)
    gath[0].forward()
    gath[0].finish(sibling=False)
    for k in range(last):
        scat[1].push_one(k, feed_block)
    whole = scat[1].pass_on(feed_block, kept)
    hidden = iw.shape[0]
    step = LANE if hidden % LANE == 0 else hidden

    def grads(left, right, out, first):
        def columns(i, carry):
            c0 = pl.multiple_of(i * step, step)
            acc = jnp.zeros((step, width), F32)
            for b in range(n):
                acc += mm(left[b, :, pl.ds(c0, step)], right[b], TN)
            out[pl.ds(c0, step), :] = acc.astype(BF16)
            return carry

        lax.fori_loop(0, hidden // step, columns, 0)
        for piece in copies[first:first + PARTS]:
            for copy in piece:
                copy.start()

    grads(act, dyall_ref, og_ref, 0)
    out_block = lambda b: mm(act[b], ow[...])
    scat[2].push(out_block)
    dh2 = scat[1].finish(whole)
    dv, gain, shift = norm_back(mid_ref[...], np_ref[2:3], dh2)
    dy = dy_ref[...].astype(F32)
    dx1 = dy + dv
    da[seat.me] = dx1.astype(BF16)
    gath[1].start()
    small_ref[...] = jnp.concatenate(
        [gain, shift, jnp.sum(dy, axis=0, keepdims=True), jnp.zeros((5, width), F32)], 0)
    whole = scat[2].pass_on(out_block)
    gath[1].forward()
    grads(dpre, h2, ig_ref, PARTS)
    block_ref[...] = mid_ref[...] + scat[2].finish(whole) + np_ref[4:5]
    mid_ref[...] = dx1
    gath[1].finish()

    def heads_block(b, acc):
        out = mm(pw[...], da[b], NT)
        do_ref[:, :, at(b)] = out.reshape(*do_ref.shape[:2], rows).astype(BF16)
        return acc + mm(o_ref[:, at(b)], da[b])

    pg_ref[...] = lax.fori_loop(0, n, heads_block, jnp.zeros(pg_ref.shape, F32)).astype(BF16)
    for c in scat + gath:
        c.drain()
    for piece in copies:
        for copy in piece:
            copy.wait()


PARTS = 2
MIDDLE_MIB = 24


def middle(n, ny, nz, pushes, x, dys, o, params, bias, proj_weight, in_weight, out_weight):
    rows, width = x.shape
    hidden = in_weight.shape[0]
    inner = proj_weight.shape[0]
    heads, hd, _ = o.shape
    f = lambda *s: jax.ShapeDtypeStruct(s, F32)
    return pl.pallas_call(
        functools.partial(middle_kernel, n, ny, nz, pushes),
        out_shape=(f(rows, width), f(rows, width), jax.ShapeDtypeStruct(o.shape, BF16),
                   *[jax.ShapeDtypeStruct((t, width), BF16) for t in (hidden, hidden, inner)], f(1, hidden), f(8, width),
                   *[jax.ShapeDtypeStruct((ny - 1, hidden // (PARTS * ny), width), BF16)] * pushes),
        in_specs=[VM] * 4 + [HBM] * 3 + [VM] * n, out_specs=[VM] * (8 + pushes),
        scratch_shapes=[pltpu.VMEM((inner, width), F32), pltpu.VMEM((hidden, width), F32),
                        pltpu.VMEM((hidden, width), F32), pltpu.VMEM((inner, width), BF16),
                        pltpu.VMEM((hidden, width), BF16), pltpu.VMEM((hidden, width), BF16),
                        pltpu.VMEM((n, rows, width), BF16), pltpu.VMEM((n, rows, width), BF16),
                        pltpu.VMEM((n, rows, hidden), BF16), pltpu.VMEM((n, rows, hidden), BF16),
                        pltpu.VMEM((n, rows, hidden), F32), pltpu.VMEM((n, rows, width), BF16), pltpu.VMEM((rows, width), F32), DMA((3,)),
                        *[s for _ in range(3) for s in scatter_scratch(n, rows, width)],
                        *gather_scratch(n), *gather_scratch(n),
                        *[DMA((max(pushes, 1), max(ny - 1, 1)))] * 2],
        compiler_params=pltpu.CompilerParams(collective_id=1, has_side_effects=True, vmem_limit_bytes=MIDDLE_MIB << 20),
        name="middle",
    )(x, o.reshape(inner, -1), params, bias, proj_weight, in_weight, out_weight, *dys)


def sum_scratch(shape):
    ny, _, nh, chunk, width = shape
    y, f = max(ny - 1, 1), max(nh - 1, 1)
    return [pltpu.VMEM((y, 2, nh, chunk, width), BF16), pltpu.VMEM((nh, chunk, width), F32),
            pltpu.VMEM((nh, chunk, width), BF16), pltpu.VMEM((nh, chunk, width), BF16),
            pltpu.VMEM((f, chunk, width), BF16), pltpu.VMEM((f, chunk, width), BF16),
            DMA((y,)), DMA((y,)), DMA((1,)), DMA((1,)), DMA((f,)), DMA((f,))]


class Sum:
    count = 12

    def __init__(self, grid, grad, own, scratch):
        self.grid, self.grad, self.own, self.pushed = grid, grad, own, True
        (self.ia, self.keep, self.ob, self.ib, self.oc, self.ic,
         self.sa, self.ra, self.sb, self.rb, self.sc, self.rc) = scratch

    def copy_y(self, k):
        g = self.grid
        return remote(self.grad.at[g.yto(k)], self.ia.at[k], self.sa.at[k], self.ra.at[k], "dp", g.at(g.z, g.yto(k)))

    def copy_near(self):
        g = self.grid
        return remote(self.ob, self.ib, self.sb.at[0], self.rb.at[0], "dp", g.at(g.near, g.y))

    def copy_far(self, k):
        g = self.grid
        return remote(self.oc.at[k], self.ic.at[k], self.sc.at[k], self.rc.at[k], "dp", g.at(g.far(k), g.y))

    def push(self):
        for k in range(self.grid.ny - 1):
            self.copy_y(k).start()

    def half(self, p):
        g = self.grid
        whole = self.grad[g.y, p].astype(F32)
        for k in range(g.ny - 1):
            whole = whole + self.ia[k, p].astype(F32)
        return whole

    def near(self):
        g = self.grid
        for k in range(g.ny - 1 if self.pushed else 0):
            self.copy_y(k).wait_recv()
        self.ob[...] = self.half(1 - g.p).astype(BF16)
        self.copy_near().start()
        self.keep[...] = self.half(g.p)

    def far(self):
        g = self.grid
        self.copy_near().wait_recv()
        for k in range(g.nh - 1):
            a = g.other(k)
            self.oc[k] = (self.keep[a] + self.ib[a].astype(F32)).astype(BF16)
            self.copy_far(k).start()
        self.own[...] = self.keep[g.a] + self.ib[g.a].astype(F32)

    def collect(self):
        whole = self.own[...]
        for k in range(self.grid.nh - 1):
            self.copy_far(k).wait_recv()
            whole = whole + self.ic[k].astype(F32)
        self.own[...] = whole

    def drain(self):
        g = self.grid
        for k in range(g.ny - 1 if self.pushed else 0):
            self.copy_y(k).wait_send()
        self.copy_near().wait_send()
        for k in range(g.nh - 1):
            self.copy_far(k).wait_send()


def spread_scratch(ny, nz):
    y, f = max(ny - 1, 1), max(nz // 2 - 1, 1)
    return [DMA((f,)), DMA((f,)), DMA((1,)), DMA((1,)), DMA((2, y)), DMA((2, y))]


class Spread:
    count = 6

    def __init__(self, grid, own, result, scratch):
        self.grid, self.own, self.result = grid, own, result
        self.sf, self.rf, self.sn, self.rn, self.sy, self.ry = scratch

    def to_far(self, k):
        g = self.grid
        r = self.result.at[g.y, g.p, g.a]
        return remote(r, r, self.sf.at[k], self.rf.at[k], "dp", g.at(g.far(k), g.y))

    def to_near(self):
        g = self.grid
        r = self.result.at[g.y, g.p]
        return remote(r, r, self.sn.at[0], self.rn.at[0], "dp", g.at(g.near, g.y))

    def to_y(self, i, k):
        g = self.grid
        r = self.result.at[g.y, g.p if i == 0 else 1 - g.p]
        return remote(r, r, self.sy.at[i, k], self.ry.at[i, k], "dp", g.at(g.z, g.yto(k)))

    def start(self):
        g = self.grid
        whole = self.own[...]
        self.result[g.y, g.p, g.a] = whole.astype(BF16)
        for k in range(g.nh - 1):
            self.to_far(k).start()
        return square(whole)

    def second(self):
        g = self.grid
        for k in range(g.nh - 1):
            self.to_far(k).wait_recv()
        self.to_near().start()
        for k in range(g.ny - 1):
            self.to_y(0, k).start()

    def third(self):
        self.to_near().wait_recv()
        for k in range(self.grid.ny - 1):
            self.to_y(1, k).start()

    def close(self):
        g = self.grid
        for i in range(2):
            for k in range(g.ny - 1):
                self.to_y(i, k).wait()
        for k in range(g.nh - 1):
            self.to_far(k).wait_send()
        self.to_near().wait_send()


def take(rest, cls, count):
    size = cls.count
    return [rest[size * i:size * (i + 1)] for i in range(count)], rest[size * count:]


class Share:
    def __init__(self, axis, slots, send, recv):
        self.axis, self.slots, self.send, self.recv = axis, slots, send, recv
        self.size = slots.shape[0]
        self.me = lax.axis_index(axis)

    def copy(self, k):
        r = self.slots.at[self.me]
        return remote(r, r, self.send.at[k], self.recv.at[k], self.axis, lax.rem(self.me + 1 + k, self.size))

    def start(self, value):
        self.slots[self.me] = value
        for k in range(self.size - 1):
            self.copy(k).start()

    def total(self):
        for k in range(self.size - 1):
            self.copy(k).wait_recv()
        out = self.slots[0]
        for i in range(1, self.size):
            out = out + self.slots[i]
        return out

    def drain(self):
        for k in range(self.size - 1):
            self.copy(k).wait_send()


def share_scratch(size, rows, width):
    return [pltpu.VMEM((size, rows, width), F32), DMA((max(size - 1, 1),)), DMA((max(size - 1, 1),))]


def square(v):
    return jnp.sum(jnp.sum(v * v, axis=1, keepdims=True), axis=0, keepdims=True)


NEAR_AT = (-1, -1, 5, 100, 105, 113, 120, 128)
FAR_AT = (2, 5, 99, 111, 113, 123, 131, 140)
COLLECT_AT = (7, 99, 106, 123, 124, 133, 144, 154)
SECOND_AT = (101, 110, 120, 139, 140, 149, 159, 167)
THIRD_AT = (114, 126, 139, 154, 157, 168, 168, 168)
NORM_AT = 118
SMALL_AT = 130
REAR_MIB = 36


def rear_kernel(n, ny, nz, pushes, coords_ref, qkv_ref, do_ref, p_ref, og_ref, ig_ref, pg_ref, x_ref, dx_ref, np_ref,
                h_ref, bg_ref, mid_small_ref, w_hbm, *rest):
    lands, rest = rest[:pushes], rest[pushes:]
    early = 2 * PARTS + 1
    results, (sq_ref, gi_ref, small_ref, bias_ref, pairs_ref, norm_ref), rest = rest[:early], rest[early:early + 6], rest[early + 6:]
    (dist, ds, dqkv, flat, w32, w, qg, qown, kept, squares, wsem), rest = rest[:11], rest[11:]
    owns, rest = rest[:early], rest[early:]
    _, heads, hd, span = qkv_ref.shape
    inner = heads * hd
    rows, width = x_ref.shape
    seat, grid = Seat(n), Grid(ny, nz)
    pieces = [g.at[i] for g in (og_ref, ig_ref) for i in range(PARTS)] + [pg_ref] + [qg.at[s] for s in range(3)]
    places = [*owns, *[qown.at[s] for s in range(3)]]
    targets = [*results, *[sq_ref.at[s] for s in range(3)]]
    scat, rest = Scatter(seat, rest[:8]), rest[8:]
    scratch, rest = take(rest, Sum, early + 3)
    sums = [Sum(grid, *a) for a in zip(pieces, places, scratch)]
    scratch, rest = take(rest, Spread, early + 3)
    spreads = [Spread(grid, *a) for a in zip(places, targets, scratch)]
    shares = [Share(a, *rest[3 * i:3 * i + 3]) for i, a in enumerate(("mp", "dp", "dp", "dp", "mp", "dp", "mp"))]
    small_mp, small_dp, bias_dp, pair_dp, sq_mp, sq_dp, local_mp = shares
    for s, land in zip(sums, lands):
        s.ia, s.pushed = land, False
    at = lambda b: pl.ds(pl.multiple_of(b * rows, rows), rows)
    load = pltpu.make_async_copy(w_hbm, w32, wsem)
    load.start()
    greet({"mp": n, "dp": ny * nz})
    for s in sums[pushes:early]:
        s.push()
    squares[...] = jnp.zeros_like(squares)

    def collect(i):
        sums[i].collect()
        squares[...] += spreads[i].start()

    def project():
        for s in range(3):
            flat[s] = dqkv[s].astype(F32).reshape(inner, span).astype(BF16)
            acc = jnp.zeros((inner, width), F32)
            for b in range(n):
                acc = acc + mm(flat[s, :, at(b)], h_ref[b])
            qg[s] = acc.reshape(qg.shape[1:]).astype(BF16)
            sums[early + s].push()
        load.wait()
        w[...] = w32[...].astype(BF16)
        block = lambda b: sum(mm(flat[s, :, at(b)], w[s], TN) for s in range(3))
        scat.push(block)
        kept[...] = scat.pass_on(block)
        bias_dp.start(jnp.broadcast_to(bg_ref[...], bias_dp.slots.shape[1:]))

    def norm():
        dh1 = scat.finish(kept[...])
        dv, gain, shift = norm_back(x_ref[...].astype(F32), np_ref[0:1], dh1)
        gi_ref[...] = dx_ref[...] + dv
        small_mp.start(jnp.concatenate([gain, shift, mid_small_ref[0:6]], 0))

    jobs = {99: [project], NORM_AT: [norm], SMALL_AT: [lambda: small_dp.start(small_mp.total())]}
    for i, s in enumerate(sums):
        for when, job in ((NEAR_AT[i], s.near), (FAR_AT[i], s.far), (COLLECT_AT[i], functools.partial(collect, i)),
                          (SECOND_AT[i], spreads[i].second), (THIRD_AT[i], spreads[i].third)):
            jobs.setdefault(when, []).append(job)

    def now(first, end):
        for when in sorted(jobs):
            if first <= when < end:
                for job in jobs[when]:
                    job()

    def beside(step, first, end):
        for when in sorted(jobs):
            if first <= when < end:
                @pl.when(step == when)
                def _():
                    for job in jobs[when]:
                        job()

    now(-1, 0)
    pair = back_pairs(heads, coords_ref, qkv_ref, do_ref, p_ref, dqkv, dist, ds, beside, lambda: now(99, 100))
    pair_dp.start(pair)
    last = 100 + span // SUB
    now(last, last + 4)
    sq_mp.start(jnp.broadcast_to(squares[...], (8, LANE)))
    now(last + 4, 1000)
    bias = bias_dp.total()
    bias_ref[...] = bias
    pairs = pair_dp.total()
    pairs_ref[...] = pairs
    local_mp.start(jnp.broadcast_to(square(bias[0:1]) + square(pairs), (8, LANE)))
    sq_dp.start(sq_mp.total())
    small = small_dp.total()
    small_ref[...] = small
    norm_ref[...] = sq_dp.total()[0:1] + local_mp.total()[0:1] + square(small)
    for s in spreads:
        s.close()
    for s in [scat] + sums + shares:
        s.drain()


def rear(n, ny, nz, qkv, do, probs, coords, og, ig, pg, lands, x, dx, params, h, bias_grad, small, qkv_weight):
    _, heads, hd, span = qkv.shape
    rows, width = x.shape
    inner, hidden = heads * hd, bias_grad.shape[1]
    ndp, pushes = ny * nz, len(lands)
    cut = lambda g, p: g.reshape(p, ny, 2, nz // 2, g.shape[0] // (p * ndp), width)
    lands = [v.reshape(ny - 1, 2, nz // 2, -1, width) for v in lands]
    og, ig, pg = cut(og, PARTS), cut(ig, PARTS), cut(pg, 1)[0]
    chunks = (3, ny, 2, nz // 2, inner // ndp, width)
    shapes = [og.shape[1:]] * PARTS + [ig.shape[1:]] * PARTS + [pg.shape]
    every = shapes + [chunks[1:]] * 3
    f = lambda *s: jax.ShapeDtypeStruct(s, F32)
    return pl.pallas_call(
        functools.partial(rear_kernel, n, ny, nz, pushes),
        out_shape=(*[jax.ShapeDtypeStruct(s, BF16) for s in (*shapes, chunks)],
                   f(rows, width), f(8, width), f(8, hidden), f(8, LANE), f(1, LANE)),
        in_specs=[VM] * 13 + [HBM] + [VM] * pushes, out_specs=[VM] * (len(shapes) + 6),
        scratch_shapes=[pltpu.VMEM((span, span), F32), pltpu.VMEM((span // LANE, SUB * span, LANE), F32),
                        pltpu.VMEM(qkv.shape, BF16), pltpu.VMEM((3, inner, span), BF16),
                        pltpu.VMEM(qkv_weight.shape, F32), pltpu.VMEM(qkv_weight.shape, BF16), pltpu.VMEM(chunks, BF16),
                        pltpu.VMEM((3, inner // ndp, width), F32), pltpu.VMEM((rows, width), F32),
                        pltpu.VMEM((1, LANE), F32), DMA, *[pltpu.VMEM(s[3:], F32) for s in shapes],
                        *scatter_scratch(n, rows, width),
                        *[v for s in every for v in sum_scratch(s)], *[v for _ in every for v in spread_scratch(ny, nz)],
                        *share_scratch(n, 8, width), *share_scratch(ndp, 8, width), *share_scratch(ndp, 8, hidden),
                        *share_scratch(ndp, 8, LANE), *share_scratch(n, 8, LANE), *share_scratch(ndp, 8, LANE),
                        *share_scratch(n, 8, LANE)],
        compiler_params=pltpu.CompilerParams(collective_id=2, has_side_effects=True, vmem_limit_bytes=REAR_MIB << 20),
        name="rear",
    )(coords, qkv, do, probs, og, ig, pg, x, dx, params, h, bias_grad, small, qkv_weight, *lands)


def leave_plain(n, x, dx, params, dqkv, h, grads, bias_grad, pair_grad, small, qkv_weight):
    part = sum(mm(dqkv[s], qkv_weight[s].astype(BF16), TN) for s in range(3))
    dh1 = lax.psum_scatter(part, "mp", scatter_dimension=0, tiled=True)
    dv, gain, shift = norm_back(x.astype(F32), params[0:1], dh1)
    hh = h.reshape(-1, h.shape[-1])
    qg = jnp.concatenate([mm(dqkv[s], hh) for s in range(3)], 0)
    og, ig, pg, qg, bias, pair = lax.psum((*[g.astype(F32) for g in grads], qg, bias_grad, pair_grad), "dp")
    small = lax.psum(jnp.concatenate([gain, shift, small[0:6]], 0), ("dp", "mp"))
    local = sum(square(v) for v in (og, ig, pg, qg, bias, pair))
    total = lax.psum(local, "mp") + square(small)
    return dx + dv, og, ig, pg, qg, small, bias, pair, total


PUSHES = 2


def adam_step(weight, grad, first, second, clip, fix_one, fix_two, rate, decay):
    scaled = grad * clip
    first_new = beta_one * first + (1.0 - beta_one) * scaled
    second_new = beta_two * second + (1.0 - beta_two) * scaled * scaled
    ratio = first_new / fix_one / (jnp.sqrt(second_new / fix_two) + adam_eps)
    return (weight - rate * (ratio + decay * weight), first_new, second_new)


def per_device(n, ndp, block_in, coords, lengths, cotangent, step_count, *state):
    weights, firsts, seconds = state[:7], state[7:14], state[14:]
    qkv_weight, proj_weight, pair_weight, in_weight, in_bias, out_weight, params = weights
    heads = pair_weight.shape[0]
    h, qkv = enter(n, heads, block_in, params, qkv_weight)
    o, probs = attention(qkv, coords, lengths, pair_weight)
    dy, _ = lax.optimization_barrier((cotangent, qkv))
    dys = [cotangent] + [lax.ppermute(dy, "mp", [((i + k) % n, i) for i in range(n)]) for k in range(1, n)]
    ny = n // 2 if ndp % (n // 2) == 0 else 1
    nz = ndp // ny
    inner, hidden = proj_weight.shape[0], in_weight.shape[0]
    beside = lengths.shape[0] == 1 and nz % 2 == 0 and inner % (8 * ndp) == 0 and hidden % (16 * PARTS * ndp) == 0
    block_out, dx, do, og, ig, pg, bg, small, *lands = middle(
        n, ny, nz, PUSHES if beside else 0, block_in, dys, o, params, in_bias.reshape(1, -1), proj_weight, in_weight, out_weight)
    if beside:
        *pieces, pg, qg, grad_input, small, bias, pair, total = rear(
            n, ny, nz, qkv, do, probs, coords, og, ig, pg, lands, block_in, dx, params, h, bg, small, qkv_weight)
        og, ig = pieces[:PARTS], pieces[PARTS:]
        og, ig = [jnp.concatenate([v.reshape(-1, v.shape[-1]) for v in g], 0) for g in (og, ig)]
    else:
        dqkv, pair_grad = attention_back(qkv, do, probs, coords)
        grad_input, og, ig, pg, qg, small, bias, pair, total = leave_plain(
            n, block_in, dx, params, dqkv.reshape(3, inner, -1), h, (og, ig, pg), bg, pair_grad, small, qkv_weight)
    grad_norm = jnp.sqrt(total[0, 0])
    clip = clip_level / jnp.maximum(grad_norm, clip_level)
    count = step_count[0].astype(F32)
    fix_one = 1.0 - jnp.power(beta_one, count)
    fix_two = 1.0 - jnp.power(beta_two, count)
    grads = (qg.reshape(qkv_weight.shape), pg.reshape(proj_weight.shape), pair[:heads], ig.reshape(in_weight.shape),
             bias[0], og.reshape(out_weight.shape), small[:5])
    rates = (0.9, 2.5, 7.5, 0.9, 7.5, 0.45, 3.0)
    decays = (0.01, 0.01, 0.01, 0.01, 0.0, 0.01, 0.0)
    outs = [block_out, grad_input, grad_norm.reshape(1)]
    for w, g, m, u, rate, decay in zip(weights, grads, firsts, seconds, rates, decays):
        outs.extend(adam_step(w, g.astype(F32), m, u, clip, fix_one, fix_two, rate, decay))
    return tuple(outs)


def solution(mesh):
    rows, mp = P(("dp", "mp"), None), P("mp", None)
    stacked = P(None, "mp", None)
    params = (stacked, mp, mp, mp, P("mp"), mp, P())
    in_specs = (rows, P(None, "dp"), P("dp", None), rows, P(), *params, *params, *params)
    out_specs = (rows, rows, P(), *[s for s in params for _ in range(3)])
    return jax.shard_map(
        functools.partial(per_device, mesh.shape["mp"], mesh.shape["dp"]),
        mesh=mesh, in_specs=in_specs, out_specs=out_specs, check_vma=False)
```
